32 devices in a mesh: dp: 16 (over z, y, x), seq: 2 (over core).
Axes of the slice: x: 2, y: 2, z: 4, core: 2. Of those that a mesh axis runs over, the one named last changes fastest.
Arguments:
- layer_input: bfloat16 [64, 512, 768], P('dp', 'seq'), may hold values from -24 to 24, as said below
- segment_ids: int32 [64, 512], P('dp'), may hold values from 0 to 3, never falling along the last dimension, each value on 1 to 256 neighbouring positions
- cotangent: bfloat16 [64, 512, 768], P('dp', 'seq'), may hold values from -6 to 6
- heads_weight: float32 [768, 2304], P(('dp', 'seq')), may hold values from -0.21875 to 0.21875
- heads_first: float32 [768, 2304], P(('dp', 'seq')), may hold values from -0.00024414062 to 0.00024414062
- heads_second: float32 [768, 2304], P(('dp', 'seq')), may hold values from 1.4128508e-10 to 5.651403e-10
- merge_weight: float32 [768, 768], P(('dp', 'seq')), may hold values from -0.625 to 0.625
- merge_first: float32 [768, 768], P(('dp', 'seq')), may hold values from -0.00024414062 to 0.00024414062
- merge_second: float32 [768, 768], P(('dp', 'seq')), may hold values from 1.4128508e-10 to 5.651403e-10
- expand_weight: float32 [768, 3072], P(('dp', 'seq')), may hold values from -0.21875 to 0.21875
- expand_first: float32 [768, 3072], P(('dp', 'seq')), may hold values from -0.00024414062 to 0.00024414062
- expand_second: float32 [768, 3072], P(('dp', 'seq')), may hold values from 1.4128508e-10 to 5.651403e-10
- shrink_weight: float32 [3072, 768], P(('dp', 'seq')), may hold values from -0.109375 to 0.109375
- shrink_first: float32 [3072, 768], P(('dp', 'seq')), may hold values from -0.00024414062 to 0.00024414062
- shrink_second: float32 [3072, 768], P(('dp', 'seq')), may hold values from 1.4128508e-10 to 5.651403e-10
- norm_gains: float32 [768, 2], P(('dp', 'seq')), may hold values from 0.25 to 2.7, as said below
- gains_first: float32 [768, 2], P(('dp', 'seq')), may hold values from -0.0007324219 to 0.0007324219
- gains_second: float32 [768, 2], P(('dp', 'seq')), may hold values from 1.2715657e-09 to 5.086263e-09
- branch_bias: float32 [768, 6], P(('dp', 'seq')), may hold values from -0.6 to 0.6
- branch_first: float32 [768, 6], P(('dp', 'seq')), may hold values from -0.0007324219 to 0.0007324219
- branch_second: float32 [768, 6], P(('dp', 'seq')), may hold values from 1.2715657e-09 to 5.086263e-09
- hidden_bias: float32 [3072], P(('dp', 'seq')), may hold values from -0.6 to 0.6
- hidden_first: float32 [3072], P(('dp', 'seq')), may hold values from -0.00024414062 to 0.00024414062
- hidden_second: float32 [3072], P(('dp', 'seq')), may hold values from 1.4128508e-10 to 5.651403e-10
Outputs:
- layer_output: bfloat16 [64, 512, 768], P('dp', 'seq')
- input_gradient: float32 [64, 512, 768], P('dp', 'seq')
- gradient_norm: float32 [], replicated
- heads_updated: float32 [768, 2304], P(('dp', 'seq'))
- heads_moment: float32 [768, 2304], P(('dp', 'seq'))
- heads_square: float32 [768, 2304], P(('dp', 'seq'))
- merge_updated: float32 [768, 768], P(('dp', 'seq'))
- merge_moment: float32 [768, 768], P(('dp', 'seq'))
- merge_square: float32 [768, 768], P(('dp', 'seq'))
- expand_updated: float32 [768, 3072], P(('dp', 'seq'))
- expand_moment: float32 [768, 3072], P(('dp', 'seq'))
- expand_square: float32 [768, 3072], P(('dp', 'seq'))
- shrink_updated: float32 [3072, 768], P(('dp', 'seq'))
- shrink_moment: float32 [3072, 768], P(('dp', 'seq'))
- shrink_square: float32 [3072, 768], P(('dp', 'seq'))
- gains_updated: float32 [768, 2], P(('dp', 'seq'))
- gains_moment: float32 [768, 2], P(('dp', 'seq'))
- gains_square: float32 [768, 2], P(('dp', 'seq'))
- branch_updated: float32 [768, 6], P(('dp', 'seq'))
- branch_moment: float32 [768, 6], P(('dp', 'seq'))
- branch_square: float32 [768, 6], P(('dp', 'seq'))
- hidden_updated: float32 [3072], P(('dp', 'seq'))
- hidden_moment: float32 [3072], P(('dp', 'seq'))
- hidden_square: float32 [3072], P(('dp', 'seq'))
- heads_copy: bfloat16 [768, 2304], P(('dp', 'seq'))
- merge_copy: bfloat16 [768, 768], P(('dp', 'seq'))
- expand_copy: bfloat16 [768, 3072], P(('dp', 'seq'))
- shrink_copy: bfloat16 [3072, 768], P(('dp', 'seq'))
The draws below stay inside these ranges and needn't reach their ends.
Inputs may be any that keep to these rules, and one draw needn't show every extreme that they name: `segment_ids`: along each row the segment numbers never fall and every one of them appears; each segment holds 1 to 256 tokens, and one segment holds exactly 256. `layer_input`: activations of order one. `norm_gains`: positive gains.
All inputs are finite; a program needn't handle non-finite values.
Results may differ from the reference program's by a relative error of at most 0.014.
The reference program's roundings to bfloat16 on the way count: a program that leaves them out, or rounds other values in their place, can miss the bound.
Values may be sent and summed in bfloat16 or wider, within the bound.
A program may use at most 192 MiB of HBM per device.

```python
import math
import jax
import jax.numpy as jnp
import numpy as np
from jax import lax

D = 768
HEADS = 12
HEAD_DIM = 64
FF = 3072
LENGTH = 512
SEGS = 4
STEP = 5
ROWS_DEV = 4
ROWS = 64


def draw_layer_input(key, part):
    feature = jnp.arange(D, dtype=jnp.float32) / (D - 1)
    group_count = ROWS // ROWS_DEV
    block_width = D // group_count
    pairing = jax.random.permutation(jax.random.fold_in(key, 7), group_count)
    row_group = jnp.arange(ROWS) // ROWS_DEV
    paired = pairing[row_group]
    feature_group = jnp.arange(D) // block_width
    spike = jnp.where(paired[:, None] == feature_group[None, :], 3.0, 1.0)
    rising = 0.6 + 1.2 * feature
    noise = jnp.clip(jax.random.normal(jax.random.fold_in(key, 11), (ROWS, LENGTH, D), jnp.float32), -4.0, 4.0)
    return (noise * rising[None, None, :] * spike[:, None, :]).astype(jnp.bfloat16)


def draw_norm_gains(key, part):
    feature = jnp.arange(D, dtype=jnp.float32) / (D - 1)
    rising = 0.5 + feature
    jitter = jnp.clip(0.1 * jax.random.normal(jax.random.fold_in(key, 13), (D, 2), jnp.float32), -0.3, 0.3)
    first_column = rising * (1.0 + jitter[:, 0])
    second_column = 1.0 + jitter[:, 1]
    return jnp.stack((first_column, second_column), axis=1).astype(jnp.float32)


def levels(rng, extent, cuts, low, high):
    def one(dim, parts):
        draws = jax.random.uniform(jax.random.fold_in(jax.random.fold_in(rng, 6), dim), (parts,), jnp.float32, low / len(cuts), high / len(cuts))
        return jnp.repeat(jnp.exp(draws), extent[dim] // parts).reshape((-1,) + (1,) * (len(extent) - dim - 1))

    level = one(*cuts[0])
    for cut in cuts[1:]:
        level = level * one(*cut)
    return level


def split_up(number_of, total, limit, lean):
    loads = [(1 << 20) // math.isqrt(grade ** lean) + 1 for grade in range(2, number_of + 1)]
    surplus, holding = total - limit - (number_of - 1), [1] * (number_of - 1)
    while surplus > 0:
        candidates = [i for i in range(number_of - 1) if holding[i] < limit]
        whole, left = sum([loads[i] for i in candidates]), surplus
        for i in candidates:
            addition = min(limit - holding[i], max(1, left * loads[i] // whole), surplus)
            holding[i] = holding[i] + addition
            surplus = surplus - addition
    return np.array([limit] + holding)


def ragged(rng, count, total, limit, skew):
    if count == 2:
        one = jax.random.randint(rng, (), max(1, total - limit), min(limit, total - 1) + 1)
        return jnp.stack([one, total - one])
    lengths = jnp.asarray(split_up(count, total, limit, skew), jnp.int32)
    couples = (count - 1) // 2
    giver, receiver = lengths[1:1 + 2 * couples:2], lengths[2:2 + 2 * couples:2]
    margin = jnp.minimum(giver - 1, limit - receiver)
    shifted = jax.random.randint(jax.random.fold_in(rng, 1), (couples,), 0, 1 << 20) % (margin + 1)
    lengths = lengths.at[1:1 + 2 * couples:2].set(giver - shifted).at[2:2 + 2 * couples:2].set(receiver + shifted)
    return lengths[jax.random.permutation(jax.random.fold_in(rng, 2), count)]


def gaussian(rng, shape, width, limit, cuts=(), held_as=jnp.bfloat16):
    values = width * jax.random.normal(rng, shape, jnp.float32)
    if cuts:
        values = values * levels(rng, shape, cuts, -0.22, 0.18)
    return jnp.clip(values, -limit, limit).astype(held_as)


def setup_inputs(seed: int = 0) -> dict:
    key_of = jax.random.split(jax.random.key(seed), 25)
    layer_input = draw_layer_input(jax.random.fold_in(key_of[24], 71), 0)
    segment_ids = jax.vmap(lambda own: jnp.searchsorted(jnp.cumsum(ragged(own, SEGS, LENGTH, LENGTH // 2, 0)), jnp.arange(LENGTH), side="right"))(jax.random.split(key_of[1], ROWS)).reshape((ROWS, LENGTH)).astype(jnp.int32)
    cotangent = gaussian(key_of[2], (ROWS, LENGTH, D), 1.0, 6.0, ((0, 16), (1, 2)))
    heads_weight = gaussian(key_of[3], (D, 3 * D), D ** -0.5, 0.21875, ((0, 32),), jnp.float32)
    heads_first = gaussian(key_of[4], (D, 3 * D), (0.111 / (4 * D * D + 2 * D * FF) ** 0.5), 0.00024414062, ((0, 32),), jnp.float32)
    heads_second = jnp.clip(jnp.exp(math.log(5.65140323427471e-10) - 1.3862944 * jax.random.uniform(key_of[5], (D, 3 * D), jnp.float32) ** levels(key_of[5], (D, 3 * D), ((0, 32),), -0.2, 0.2)), 1.4128508085686775e-10, 5.65140323427471e-10)
    merge_weight = gaussian(key_of[6], (D, D), (D // 8) ** -0.5, 0.625, ((0, 32),), jnp.float32)
    merge_first = gaussian(key_of[7], (D, D), (0.111 / (4 * D * D + 2 * D * FF) ** 0.5), 0.00024414062, ((0, 32),), jnp.float32)
    merge_second = jnp.clip(jnp.exp(math.log(5.65140323427471e-10) - 1.3862944 * jax.random.uniform(key_of[8], (D, D), jnp.float32) ** levels(key_of[8], (D, D), ((0, 32),), -0.2, 0.2)), 1.4128508085686775e-10, 5.65140323427471e-10)
    expand_weight = gaussian(key_of[9], (D, FF), D ** -0.5, 0.21875, ((0, 32),), jnp.float32)
    expand_first = gaussian(key_of[10], (D, FF), (0.111 / (4 * D * D + 2 * D * FF) ** 0.5), 0.00024414062, ((0, 32),), jnp.float32)
    expand_second = jnp.clip(jnp.exp(math.log(5.65140323427471e-10) - 1.3862944 * jax.random.uniform(key_of[11], (D, FF), jnp.float32) ** levels(key_of[11], (D, FF), ((0, 32),), -0.2, 0.2)), 1.4128508085686775e-10, 5.65140323427471e-10)
    shrink_weight = gaussian(key_of[12], (FF, D), FF ** -0.5, 0.109375, ((0, 32),), jnp.float32)
    shrink_first = gaussian(key_of[13], (FF, D), (0.111 / (4 * D * D + 2 * D * FF) ** 0.5), 0.00024414062, ((0, 32),), jnp.float32)
    shrink_second = jnp.clip(jnp.exp(math.log(5.65140323427471e-10) - 1.3862944 * jax.random.uniform(key_of[14], (FF, D), jnp.float32) ** levels(key_of[14], (FF, D), ((0, 32),), -0.2, 0.2)), 1.4128508085686775e-10, 5.65140323427471e-10)
    norm_gains = draw_norm_gains(jax.random.fold_in(key_of[24], 71), 0)
    gains_first = gaussian(key_of[16], (D, 2), (0.333 / (4 * D * D + 2 * D * FF) ** 0.5), 0.0007324219, ((0, 32),), jnp.float32)
    gains_second = jnp.clip(jnp.exp(math.log(5.08626296635839e-09) - 1.3862944 * jax.random.uniform(key_of[17], (D, 2), jnp.float32) ** levels(key_of[17], (D, 2), ((0, 32),), -0.2, 0.2)), 1.2715657415895976e-09, 5.08626296635839e-09)
    branch_bias = gaussian(key_of[18], (D, 6), 0.1, 0.6, ((0, 32),), jnp.float32)
    branch_first = gaussian(key_of[19], (D, 6), (0.333 / (4 * D * D + 2 * D * FF) ** 0.5), 0.0007324219, ((0, 32),), jnp.float32)
    branch_second = jnp.clip(jnp.exp(math.log(5.08626296635839e-09) - 1.3862944 * jax.random.uniform(key_of[20], (D, 6), jnp.float32) ** levels(key_of[20], (D, 6), ((0, 32),), -0.2, 0.2)), 1.2715657415895976e-09, 5.08626296635839e-09)
    hidden_bias = gaussian(key_of[21], (FF,), 0.1, 0.6, ((0, 32),), jnp.float32)
    hidden_first = gaussian(key_of[22], (FF,), (0.111 / (4 * D * D + 2 * D * FF) ** 0.5), 0.00024414062, ((0, 32),), jnp.float32)
    hidden_second = jnp.clip(jnp.exp(math.log(5.65140323427471e-10) - 1.3862944 * jax.random.uniform(key_of[23], (FF,), jnp.float32) ** levels(key_of[23], (FF,), ((0, 32),), -0.2, 0.2)), 1.4128508085686775e-10, 5.65140323427471e-10)
    return {"layer_input": layer_input, "segment_ids": segment_ids, "cotangent": cotangent, "heads_weight": heads_weight, "heads_first": heads_first, "heads_second": heads_second, "merge_weight": merge_weight, "merge_first": merge_first, "merge_second": merge_second, "expand_weight": expand_weight, "expand_first": expand_first, "expand_second": expand_second, "shrink_weight": shrink_weight, "shrink_first": shrink_first, "shrink_second": shrink_second, "norm_gains": norm_gains, "gains_first": gains_first, "gains_second": gains_second, "branch_bias": branch_bias, "branch_first": branch_first, "branch_second": branch_second, "hidden_bias": hidden_bias, "hidden_first": hidden_first, "hidden_second": hidden_second}


@jax.custom_vjp
def low(v):
    return lax.optimization_barrier(v.astype(jnp.bfloat16)).astype(jnp.float32)

@jax.custom_vjp
def low_back(v):
    return v

def low_keep(v):
    return (low(v), None)

def low_pass(kept, grad):
    return (grad,)

def back_keep(v):
    return (v, None)

def back_low(kept, grad):
    return (low(grad),)
low.defvjp(low_keep, low_pass)
low_back.defvjp(back_keep, back_low)
norm_epsilon = 1e-12
masked_score = -1e+30
root_half = 0.7071067811865476
clip_limit = 1.0
decay_first = 0.9
decay_second = 0.999
adam_epsilon = 1e-08
weight_decay = 0.01
rate_matrix = 0.05
rate_vector = 0.5

def normalize(hidden, gain, shift):
    center = hidden - lax.optimization_barrier(jnp.mean(hidden, axis=-1, keepdims=True))
    inverse_scale = lax.rsqrt(lax.optimization_barrier(jnp.mean(center * center, axis=-1, keepdims=True)) + norm_epsilon)
    return center * inverse_scale * gain + shift

def gelu_exact(inputs):
    return 0.5 * inputs * (1.0 + lax.erf(inputs * root_half))

def layer(params, inputs, segments):
    heads_low, merge_low, expand_low, shrink_low, gains, biases, hidden_low = [low(param) for param in params]
    row_count = inputs.shape[0]
    flat_input = inputs.reshape(-1, D)
    projected = jnp.dot(flat_input, heads_low, preferred_element_type=jnp.float32, precision=lax.Precision.HIGHEST)
    queries = low_back(low(projected[:, :D] + biases[:, 0]))
    key_rows = low_back(low(projected[:, D:2 * D]))
    values = low_back(low(projected[:, 2 * D:] + biases[:, 1]))
    query_heads = queries.reshape(row_count, LENGTH, HEADS, HEAD_DIM)
    key_heads = key_rows.reshape(row_count, LENGTH, HEADS, HEAD_DIM)
    value_heads = values.reshape(row_count, LENGTH, HEADS, HEAD_DIM)
    scores = jnp.einsum('bqhd,bkhd->bhqk', query_heads, key_heads, precision=lax.Precision.HIGHEST) * HEAD_DIM ** (-0.5)
    scores = low_back(scores)
    allowed = (segments[:, :, None] == segments[:, None, :])[:, None]
    softmax_full = jax.nn.softmax(jnp.where(allowed, scores, masked_score), axis=-1)
    context = jnp.einsum('bhqk,bkhd->bqhd', low(softmax_full), value_heads, precision=lax.Precision.HIGHEST)
    context = low_back(low(context.reshape(-1, D)))
    attended = low_back(jnp.dot(context, merge_low, preferred_element_type=jnp.float32, precision=lax.Precision.HIGHEST) + biases[:, 2])
    first_out = low(normalize(flat_input + attended, gains[:, 0], biases[:, 3]))
    pre_active = low_back(jnp.dot(first_out, expand_low, preferred_element_type=jnp.float32, precision=lax.Precision.HIGHEST) + hidden_low)
    active = low(gelu_exact(pre_active))
    branch_out = low_back(jnp.dot(active, shrink_low, preferred_element_type=jnp.float32, precision=lax.Precision.HIGHEST) + biases[:, 4])
    return normalize(first_out + branch_out, gains[:, 1], biases[:, 5]).reshape(inputs.shape)

def adamw(weight, moment, square, gradient, factor, step_rate):
    clipped = gradient * factor
    moment_new = decay_first * moment + (1.0 - decay_first) * clipped
    square_new = decay_second * square + (1.0 - decay_second) * clipped * clipped
    corrected = moment_new / (1.0 - decay_first ** STEP) / (jnp.sqrt(square_new / (1.0 - decay_second ** STEP)) + adam_epsilon)
    return (weight - step_rate * (corrected + weight_decay * weight), moment_new, square_new)

def reference(layer_input, segment_ids, cotangent, heads_weight, heads_first, heads_second, merge_weight, merge_first, merge_second, expand_weight, expand_first, expand_second, shrink_weight, shrink_first, shrink_second, norm_gains, gains_first, gains_second, branch_bias, branch_first, branch_second, hidden_bias, hidden_first, hidden_second):
    masters = (heads_weight, merge_weight, expand_weight, shrink_weight, norm_gains, branch_bias, hidden_bias)
    group_rows = math.gcd(ROWS, max(1, 4096 // LENGTH))
    group_count = ROWS // group_rows
    inputs = layer_input.astype(jnp.float32).reshape(group_count, group_rows, LENGTH, D)
    segments = segment_ids.reshape(group_count, group_rows, LENGTH)
    upstream = cotangent.astype(jnp.float32).reshape(group_count, group_rows, LENGTH, D)

    def one_group(carry, pieces):
        group_input, group_segments, group_upstream = pieces
        output, pullback = jax.vjp(lambda params, values: layer(params, values, group_segments), masters, group_input)
        param_grads, input_grad = pullback(group_upstream)
        carry = jax.tree.map(jnp.add, carry, param_grads)
        return (carry, (output.astype(jnp.bfloat16), input_grad))
    zeros = tuple((jnp.zeros_like(master) for master in masters))
    gradients, (outputs, input_grads) = lax.scan(one_group, zeros, (inputs, segments, upstream))
    squares = sum((jnp.sum(piece * piece) for piece in gradients))
    gradient_norm = jnp.sqrt(squares)
    factor = jnp.minimum(1.0, clip_limit / gradient_norm)
    states = ((heads_weight, heads_first, heads_second, rate_matrix), (merge_weight, merge_first, merge_second, rate_matrix), (expand_weight, expand_first, expand_second, rate_matrix), (shrink_weight, shrink_first, shrink_second, rate_matrix), (norm_gains, gains_first, gains_second, rate_vector), (branch_bias, branch_first, branch_second, rate_vector), (hidden_bias, hidden_first, hidden_second, rate_vector))
    results = [adamw(state[0], state[1], state[2], gradient, factor, state[3]) for state, gradient in zip(states, gradients)]
    return (outputs.reshape(ROWS, LENGTH, D), input_grads.reshape(ROWS, LENGTH, D), gradient_norm, results[0][0], results[0][1], results[0][2], results[1][0], results[1][1], results[1][2], results[2][0], results[2][1], results[2][2], results[3][0], results[3][1], results[3][2], results[4][0], results[4][1], results[4][2], results[5][0], results[5][1], results[5][2], results[6][0], results[6][1], results[6][2], results[0][0].astype(jnp.bfloat16), results[1][0].astype(jnp.bfloat16), results[2][0].astype(jnp.bfloat16), results[3][0].astype(jnp.bfloat16))
```

```python
import functools

import jax
import jax.numpy as jnp
from jax import lax
from jax.experimental import pallas as pl
from jax.experimental.pallas import tpu as pltpu
from jax.sharding import PartitionSpec as P

D = 768
HEAD_DIM = 64
STEP = 5
MESH = pl.DeviceIdType.MESH

norm_epsilon = 1e-12
masked_score = -1e30
root_half = 0.7071067811865476
inv_root_tau = 0.3989422804014327
clip_limit = 1.0
decay_first = 0.9
decay_second = 0.999
adam_epsilon = 1e-08
weight_decay = 0.01
rate_matrix = 0.05
rate_vector = 0.5


def place():
    chip, core = lax.axis_index("dp"), lax.axis_index("seq")
    return chip // 4, (chip // 2) % 2, chip % 2, core


def device(z, y, x, core):
    return ((z * 2 + y) * 2 + x, core)


def signal(semaphore, target):
    pl.semaphore_signal(semaphore, inc=1, device_id=target, device_id_type=MESH)


def greet(layers, others=()):
    z, y, x, core = place()
    barrier = pltpu.get_barrier_semaphore()
    across = (device(z, y, x, 1 - core), device(z, y, 1 - x, core), device(z, 1 - y, x, core))
    for target in across + tuple(others):
        signal(barrier, target)

    @pl.when(z > 0)
    def _():
        signal(barrier, device(z - 1, y, x, core))

    @pl.when(z < layers - 1)
    def _():
        signal(barrier, device(z + 1, y, x, core))

    beside = jnp.where(z > 0, 1, 0) + jnp.where(z < layers - 1, 1, 0)
    pl.semaphore_wait(barrier, 3 + len(others) + beside)


def remote(source, target, sent, received, to):
    return pltpu.make_async_remote_copy(
        src_ref=source,
        dst_ref=target,
        send_sem=sent,
        recv_sem=received,
        device_id=to,
        device_id_type=MESH,
    )


GATHERED = (
    ("heads", 0, 768, False),
    ("merge", 0, 768, True),
    ("small", 0, 128, True),
    ("heads", 768, 384, True),
    ("shrink", 0, 768, False),
    ("expand", 0, 3072, True),
)


def gather_kernel(
    layers,
    heads_in,
    merge_in,
    expand_in,
    shrink_in,
    small_in,
    tokens_in,
    heads_all,
    merge_all,
    expand_all,
    shrink_all,
    small_all,
    tokens_all,
    heads_block,
    token_room,
    pair_send,
    pair_recv,
    own_sem,
    line_send,
    line_recv,
    first_send,
    first_recv,
    second_send,
    second_recv,
    core_send,
    core_recv,
):
    z, y, x, core = place()
    partner = device(z, y, x, 1 - core)
    own = {"merge": merge_in, "expand": expand_in, "shrink": shrink_in, "small": small_in}
    full = {
        "merge": merge_all,
        "expand": expand_all,
        "shrink": shrink_all,
        "small": small_all,
        "heads": heads_all,
    }
    greet(layers)

    heads_out = remote(
        heads_in.at[1 - core], heads_block.at[core], pair_send.at[0], pair_recv.at[0], partner
    )
    heads_out.start()
    heads_keep = pltpu.make_async_copy(heads_in.at[core], heads_block.at[core], own_sem.at[0])
    heads_keep.start()
    tokens_load = pltpu.make_async_copy(tokens_in, token_room, own_sem.at[1])
    tokens_load.start()

    def own_block(piece):
        name, start, width, _ = GATHERED[piece]
        if name == "heads":
            return heads_block.at[:, :, pl.ds(start, width)]
        return own[name]

    def block(piece, zz, yy, xx, plane):
        name, start, width, _ = GATHERED[piece]
        if name == "heads":
            return full[name].at[zz, yy, xx, :, :, pl.ds(start, width)]
        return full[name].at[zz, yy, xx, plane]

    def couple(piece, zz, plane, moved):
        name, start, width, y_first = GATHERED[piece]
        yy = y if y_first or not moved else 1 - y
        xx = x if not y_first or not moved else 1 - x
        if name == "heads":
            if y_first:
                return full[name].at[zz, :, xx, :, :, pl.ds(start, width)]
            return full[name].at[zz, yy, :, :, :, pl.ds(start, width)]
        if y_first:
            return full[name].at[zz, :, xx, plane]
        return full[name].at[zz, yy, :, plane]

    def across(piece, second):
        y_turn = GATHERED[piece][3] != second
        return device(z, 1 - y, x, core) if y_turn else device(z, y, 1 - x, core)

    def first_block(piece, zz):
        if GATHERED[piece][3]:
            return (zz, 1 - y, x)
        return (zz, y, 1 - x)

    def line_copy(piece, zz, source, target_z):
        return remote(
            source,
            block(piece, zz, y, x, core),
            line_send.at[piece, zz, jnp.where(target_z > z, 0, 1)],
            line_recv.at[piece, zz],
            device(target_z, y, x, core),
        )

    def first_copy(piece, zz, source):
        return remote(
            source,
            block(piece, zz, y, x, core),
            first_send.at[piece, zz],
            first_recv.at[piece, zz],
            across(piece, False),
        )

    def second_copy(piece, zz):
        both = couple(piece, zz, core, False)
        return remote(
            both, both, second_send.at[piece, zz], second_recv.at[piece, zz], across(piece, True)
        )

    def core_copy(piece, zz, stage, source, target):
        return remote(
            source,
            target,
            core_send.at[piece, zz, stage],
            core_recv.at[piece, zz, stage],
            partner,
        )

    def shared(piece):
        return GATHERED[piece][0] != "heads"

    pieces = range(len(GATHERED))
    order = sorted(pieces, key=lambda piece: (GATHERED[piece][0] == "heads", piece))

    def begin(piece):
        mine = own_block(piece)

        @pl.when(z < layers - 1)
        def _():
            line_copy(piece, z, mine, z + 1).start()

        @pl.when(z > 0)
        def _():
            line_copy(piece, z, mine, z - 1).start()

        first_copy(piece, z, mine).start()
        if shared(piece):
            core_copy(piece, z, 0, mine, block(piece, z, y, x, core)).start()
        pltpu.make_async_copy(
            mine, block(piece, z, y, x, core), own_sem.at[2 + piece]
        ).start()

    for piece in order:
        if piece == order[-2]:
            heads_out.wait_recv()
            heads_keep.wait()
        begin(piece)
    tokens_load.wait()
    tokens_out = remote(
        token_room, tokens_all.at[1], pair_send.at[1], pair_recv.at[1], partner
    )
    tokens_out.start()
    tokens_keep = pltpu.make_async_copy(token_room, tokens_all.at[0], own_sem.at[1])
    tokens_keep.start()
    for piece in order:
        pltpu.make_async_copy(
            own_block(piece), block(piece, z, y, x, core), own_sem.at[2 + piece]
        ).wait()

    def arrive_line(piece, zz, below):
        here = block(piece, zz, y, x, core)
        line_copy(piece, zz, here, z).wait_recv()
        if below:

            @pl.when(z < layers - 1)
            def _():
                line_copy(piece, zz, here, z + 1).start()

        else:

            @pl.when(z > 0)
            def _():
                line_copy(piece, zz, here, z - 1).start()

        first_copy(piece, zz, here).start()
        if shared(piece):
            core_copy(piece, zz, 0, here, here).start()

    def arrive_first(piece, zz):
        here = block(piece, *first_block(piece, zz), core)
        remote(
            here, here, first_send.at[piece, zz], first_recv.at[piece, zz], across(piece, False)
        ).wait_recv()
        second_copy(piece, zz).start()
        if shared(piece):
            core_copy(piece, zz, 1, here, here).start()

    def arrive_second(piece, zz):
        here = couple(piece, zz, core, True)
        remote(
            here, here, second_send.at[piece, zz], second_recv.at[piece, zz], across(piece, True)
        ).wait_recv()
        if shared(piece):
            core_copy(piece, zz, 2, here, here).start()

    def each(distance, action):
        if distance == 0:
            action(z, None)
            return

        @pl.when(z - distance >= 0)
        def _():
            action(z - distance, True)

        @pl.when(z + distance < layers)
        def _():
            action(z + distance, False)

    for step in range(layers + 2):
        for piece in pieces:
            if 0 < step < layers:
                each(step, lambda zz, below, piece=piece: arrive_line(piece, zz, below))
            if 0 <= step - 1 < layers:
                each(step - 1, lambda zz, below, piece=piece: arrive_first(piece, zz))
            if 0 <= step - 2 < layers:
                each(step - 2, lambda zz, below, piece=piece: arrive_second(piece, zz))

    heads_out.wait_send()
    tokens_out.wait_send()
    remote(
        token_room, tokens_all.at[1], pair_send.at[1], pair_recv.at[1], partner
    ).wait_recv()
    tokens_keep.wait()
    other = 1 - core
    for piece in pieces:
        for zz in range(layers):
            mine = block(piece, zz, y, x, core)
            theirs = block(piece, zz, y, x, other)
            crossed = block(piece, *first_block(piece, zz), other)
            first_copy(piece, zz, mine).wait_send()
            second_copy(piece, zz).wait_send()
            if shared(piece):
                core_copy(piece, zz, 0, mine, theirs).wait()
                core_copy(piece, zz, 1, mine, crossed).wait()
                both = couple(piece, zz, other, True)
                core_copy(piece, zz, 2, both, both).wait()

            @pl.when(jnp.logical_and(z < layers - 1, zz <= z))
            def _(piece=piece, zz=zz, mine=mine):
                line_copy(piece, zz, mine, z + 1).wait_send()

            @pl.when(jnp.logical_and(z > 0, zz >= z))
            def _(piece=piece, zz=zz, mine=mine):
                line_copy(piece, zz, mine, z - 1).wait_send()


def gather_all(layers, heads, merge, expand, shrink, small, tokens):
    chips = (layers, 2, 2, 2)
    low = jnp.bfloat16
    count = len(GATHERED)
    sems = pltpu.SemaphoreType.DMA
    inputs = (heads, merge, expand, shrink, small)
    return pl.pallas_call(
        functools.partial(gather_kernel, layers),
        out_shape=[
            jax.ShapeDtypeStruct(chips + heads.shape[1:], low),
            *[jax.ShapeDtypeStruct(chips + part.shape, low) for part in inputs[1:]],
            jax.ShapeDtypeStruct((2,) + tokens.shape, low),
        ],
        in_specs=[pl.BlockSpec(memory_space=pltpu.VMEM)] * 5 + [pl.BlockSpec(memory_space=pl.ANY)],
        out_specs=[pl.BlockSpec(memory_space=pl.ANY)] * 6,
        scratch_shapes=[
            pltpu.VMEM(heads.shape, low),
            pltpu.VMEM(tokens.shape, low),
            sems((2,)),
            sems((2,)),
            sems((2 + count,)),
            sems((count, layers, 2)),
            sems((count, layers)),
            sems((count, layers)),
            sems((count, layers)),
            sems((count, layers)),
            sems((count, layers)),
            sems((count, layers, 3)),
            sems((count, layers, 3)),
        ],
        compiler_params=pltpu.CompilerParams(collective_id=0, has_side_effects=True),
        name="gather_all",
    )(*inputs, tokens)


SCATTERED = (
    ("shrink", 0, 768, False),
    ("expand", 0, 3072, True),
    ("heads", 0, 768, False),
    ("heads", 768, 384, True),
    ("merge", 0, 768, True),
)
BITS = 5


def scatter_kernel(
    layers,
    heads_in,
    merge_in,
    expand_in,
    shrink_in,
    small_in,
    heads_out,
    merge_out,
    expand_out,
    shrink_out,
    small_out,
    square_out,
    totals,
    core_rooms,
    first_rooms,
    second_rooms,
    line_rooms,
    heads_last,
    heads_room,
    small_now,
    small_room,
    square_now,
    square_room,
    load_sem,
    core_send,
    core_recv,
    first_send,
    first_recv,
    second_send,
    second_recv,
    line_send,
    line_recv,
    last_send,
    last_recv,
    small_send,
    small_recv,
    square_send,
    square_recv,
):
    z, y, x, core = place()
    partner = device(z, y, x, 1 - core)
    sources = {"heads": heads_in, "merge": merge_in, "expand": expand_in, "shrink": shrink_in}
    results = {"merge": merge_out, "expand": expand_out, "shrink": shrink_out}
    opposite = (
        partner,
        device(z, y, 1 - x, core),
        device(z, 1 - y, x, core),
        device(z + 1 - 2 * (z % 2), y, x, core),
        device((z + 2) % 4, y, x, core),
    )
    greet(layers, opposite[4:])

    pieces = range(len(SCATTERED))
    low, wide = jnp.bfloat16, jnp.float32

    def is_heads(piece):
        return SCATTERED[piece][0] == "heads"

    def y_first(piece):
        return SCATTERED[piece][3]

    def part(piece, zz, plane):
        name, start, width, _ = SCATTERED[piece]
        if name == "heads":
            return sources[name].at[zz, :, :, :, :, pl.ds(start, width)]
        return sources[name].at[zz, :, :, plane]

    def load(piece, zz):
        return pltpu.make_async_copy(
            part(piece, zz, core), totals[piece].at[zz], load_sem.at[piece, zz]
        )

    def core_copy(piece, zz):
        return remote(
            part(piece, zz, 1 - core),
            core_rooms[piece].at[zz],
            core_send.at[piece, zz],
            core_recv.at[piece, zz],
            partner,
        )

    def first_copy(piece, zz):
        if y_first(piece):
            source, to = totals[piece].at[zz, 1 - y], device(z, 1 - y, x, core)
        else:
            source, to = totals[piece].at[zz, :, 1 - x], device(z, y, 1 - x, core)
        return remote(
            source, first_rooms[piece].at[zz], first_send.at[piece, zz], first_recv.at[piece, zz], to
        )

    def second_copy(piece, zz):
        if y_first(piece):
            source, to = totals[piece].at[zz, y, 1 - x], device(z, y, 1 - x, core)
        else:
            source, to = totals[piece].at[zz, 1 - y, x], device(z, 1 - y, x, core)
        return remote(
            source,
            second_rooms[piece].at[zz],
            second_send.at[piece, zz],
            second_recv.at[piece, zz],
            to,
        )

    def line_copy(piece, zz, downward):
        to = z - 1 if downward else z + 1
        return remote(
            totals[piece].at[zz, y, x],
            line_rooms[piece].at[downward, zz],
            line_send.at[piece, zz],
            line_recv.at[piece, downward, zz],
            device(to, y, x, core),
        )

    def add(piece, target, room):
        target[...] = (target[...].astype(wide) + room[...].astype(wide)).astype(low)

    def begin(piece, zz):
        if not is_heads(piece):
            core_copy(piece, zz).start()
        load(piece, zz).start()

    def layer_of(step):
        return jnp.where(step % 2 == 0, step // 2, layers - 1 - step // 2)

    def start_all(step, carry):
        for piece in pieces:
            begin(piece, layer_of(step))
        return carry

    lax.fori_loop(0, layers, start_all, 0)

    def on_first(piece, zz):
        load(piece, zz).wait()
        if not is_heads(piece):
            core_copy(piece, zz).wait_recv()

            def merge_one(index, carry):
                add(
                    piece,
                    totals[piece].at[zz, index // 2, index % 2],
                    core_rooms[piece].at[zz, index // 2, index % 2],
                )
                return carry

            lax.fori_loop(0, 4, merge_one, 0)
        first_copy(piece, zz).start()

    def on_second(piece, zz):
        first_copy(piece, zz).wait_recv()

        def merge_one(index, carry):
            if y_first(piece):
                target = totals[piece].at[zz, y, index]
            else:
                target = totals[piece].at[zz, index, x]
            add(piece, target, first_rooms[piece].at[zz, index])
            return carry

        lax.fori_loop(0, 2, merge_one, 0)
        second_copy(piece, zz).start()

    def on_line(piece, zz):
        second_copy(piece, zz).wait_recv()
        mine = totals[piece].at[zz, y, x]
        add(piece, mine, second_rooms[piece].at[zz])

        @pl.when(zz > z)
        def _():
            @pl.when(z > 0)
            def _():
                line_copy(piece, zz, 0).wait_recv()
                add(piece, mine, line_rooms[piece].at[0, zz])

            line_copy(piece, zz, 0).start()

        @pl.when(zz < z)
        def _():
            @pl.when(z < layers - 1)
            def _():
                line_copy(piece, zz, 1).wait_recv()
                add(piece, mine, line_rooms[piece].at[1, zz])

            line_copy(piece, zz, 1).start()

    def small_copy(bit):
        return remote(
            small_now.at[bit], small_room.at[bit], small_send.at[bit], small_recv.at[bit], opposite[bit]
        )

    small_now[0] = small_in[...]
    small_copy(0).start()

    def step_all(step, carry):
        @pl.when(step < layers)
        def _():
            for piece in pieces:
                on_first(piece, layer_of(step))

        @pl.when(jnp.logical_and(step >= 1, step <= layers))
        def _():
            for piece in pieces:
                on_second(piece, layer_of(step - 1))

        @pl.when(step >= 2)
        def _():
            for piece in pieces:
                on_line(piece, layer_of(step - 2))

        for bit in range(BITS):

            @pl.when(step == bit)
            def _(bit=bit):
                small_copy(bit).wait_recv()
                summed = small_now[bit] + small_room[bit]
                if bit + 1 < BITS:
                    small_now[bit + 1] = summed
                    small_copy(bit + 1).start()
                else:
                    small_out[...] = summed

        return carry

    lax.fori_loop(0, layers + 2, step_all, 0)

    def squares(value):
        rows, columns = value.shape
        by_row = jnp.sum((value * value).reshape(rows // 8, 8, columns), axis=0)
        total = by_row[:, 0:128]
        for start in range(128, columns, 128):
            total = total + by_row[:, start : start + 128]
        return total

    def last_copy(piece):
        _, start, width, _ = SCATTERED[piece]
        return remote(
            heads_last.at[:, pl.ds(start, width)],
            heads_room.at[:, pl.ds(start, width)],
            last_send.at[piece],
            last_recv.at[piece],
            partner,
        )

    square_now[0] = jnp.zeros((8, 128), wide)
    order = sorted(pieces, key=lambda piece: not is_heads(piece))
    for piece in order:
        name, start, width, _ = SCATTERED[piece]
        mine = totals[piece].at[z, y, x]

        @pl.when(z > 0)
        def _(piece=piece, mine=mine):
            line_copy(piece, z, 0).wait_recv()
            add(piece, mine, line_rooms[piece].at[0, z])

        @pl.when(z < layers - 1)
        def _(piece=piece, mine=mine):
            line_copy(piece, z, 1).wait_recv()
            add(piece, mine, line_rooms[piece].at[1, z])

        if is_heads(piece):
            heads_last[:, start : start + width] = mine[1 - core]
            last_copy(piece).start()
            kept = mine[core].astype(wide)
            heads_out[core, :, start : start + width] = kept
        else:
            kept = mine[...].astype(wide)
            results[name][...] = kept
        square_now[0] += squares(kept)
    for piece in pieces:
        if is_heads(piece):
            _, start, width, _ = SCATTERED[piece]
            last_copy(piece).wait_recv()
            theirs = heads_room[:, start : start + width].astype(wide)
            heads_out[1 - core, :, start : start + width] = theirs
            square_now[0] += squares(theirs)

    for bit in range(BITS):
        across = remote(
            square_now.at[bit],
            square_room.at[bit],
            square_send.at[bit],
            square_recv.at[bit],
            opposite[bit],
        )
        across.start()
        across.wait()
        summed = square_now[bit] + square_room[bit]
        if bit + 1 < BITS:
            square_now[bit + 1] = summed
        else:
            square_out[...] = summed

    for bit in range(BITS):
        small_copy(bit).wait_send()

    def settle(zz, carry):
        for piece in pieces:
            if not is_heads(piece):
                core_copy(piece, zz).wait_send()
            first_copy(piece, zz).wait_send()
            second_copy(piece, zz).wait_send()

            @pl.when(zz > z)
            def _(piece=piece):
                line_copy(piece, zz, 0).wait_send()

            @pl.when(zz < z)
            def _(piece=piece):
                line_copy(piece, zz, 1).wait_send()

        return carry

    lax.fori_loop(0, layers, settle, 0)
    for piece in pieces:
        if is_heads(piece):
            last_copy(piece).wait_send()


def scatter_all(layers, heads, merge, expand, shrink, small):
    low, wide = jnp.bfloat16, jnp.float32
    arrays = {"heads": heads, "merge": merge, "expand": expand, "shrink": shrink}
    sems = pltpu.SemaphoreType.DMA

    def rooms(*lead):
        found = []
        for name, _, width, _ in SCATTERED:
            rows = arrays[name].shape[4]
            tail = (2, rows, width) if name == "heads" else (rows, width)
            found.append(pltpu.VMEM(tuple(lead) + tail, low))
        return found

    def core_rooms():
        return [
            pltpu.VMEM((1, 1, 1, 8, 128), low)
            if name == "heads"
            else pltpu.VMEM((layers, 2, 2, arrays[name].shape[4], width), low)
            for name, _, width, _ in SCATTERED
        ]

    count = len(SCATTERED)
    rows, columns = heads.shape[4:]
    return pl.pallas_call(
        functools.partial(scatter_kernel, layers),
        out_shape=[
            jax.ShapeDtypeStruct((2, rows, columns), wide),
            *[jax.ShapeDtypeStruct(part.shape[4:], wide) for part in (merge, expand, shrink)],
            jax.ShapeDtypeStruct(small.shape, wide),
            jax.ShapeDtypeStruct((8, 128), wide),
        ],
        in_specs=[pl.BlockSpec(memory_space=pl.ANY)] * 4 + [pl.BlockSpec(memory_space=pltpu.VMEM)],
        out_specs=[pl.BlockSpec(memory_space=pltpu.VMEM)] * 6,
        scratch_shapes=[
            rooms(layers, 2, 2),
            core_rooms(),
            rooms(layers, 2),
            rooms(layers),
            rooms(2, layers),
            pltpu.VMEM((rows, columns), low),
            pltpu.VMEM((rows, columns), low),
            pltpu.VMEM((BITS,) + small.shape, wide),
            pltpu.VMEM((BITS,) + small.shape, wide),
            pltpu.VMEM((BITS, 8, 128), wide),
            pltpu.VMEM((BITS, 8, 128), wide),
            sems((count, layers)),
            sems((count, layers)),
            sems((count, layers)),
            sems((count, layers)),
            sems((count, layers)),
            sems((count, layers)),
            sems((count, layers)),
            sems((count, layers)),
            sems((count, 2, layers)),
            sems((count,)),
            sems((count,)),
            sems((BITS,)),
            sems((BITS,)),
            sems((BITS,)),
            sems((BITS,)),
        ],
        compiler_params=pltpu.CompilerParams(
            collective_id=1, has_side_effects=True, vmem_limit_bytes=60 * 2**20
        ),
        name="scatter_all",
    )(heads, merge, expand, shrink, small)


FAR = (((1,), (1,)), ((), ()))
NEAR = (((1,), (0,)), ((), ()))


def dot(left, right, dims=NEAR):
    return lax.dot_general(left, right, dims, preferred_element_type=jnp.float32)


def write_bias(bias, seg_key, seg_query):
    @pl.when(pl.program_id(1) == 0)
    def _():
        bias[...] = jnp.where(seg_key[0] == seg_query[0], 0.0, masked_score)


def both_halves(ref):
    halves, rows, length, lanes = ref.shape
    return ref[...].reshape(halves * rows * length, lanes)


def only_head(head, value):
    lane = lax.broadcasted_iota(jnp.int32, value.shape, 1)
    return jnp.where((lane // HEAD_DIM) == head, value, jnp.zeros_like(value))


def softmax_of(keys, query, bias):
    scores = dot(keys, query, FAR) + bias[...]
    unscaled = jnp.exp(scores - jnp.max(scores, axis=0, keepdims=True))
    return unscaled * (1.0 / jnp.sum(unscaled, axis=0, keepdims=True))


def attend_kernel(query_ref, key_ref, value_ref, seg_key, seg_query, out_ref, bias):
    write_bias(bias, seg_key, seg_query)
    query = both_halves(query_ref) * jnp.asarray(HEAD_DIM**-0.5, jnp.bfloat16)
    keys = both_halves(key_ref)
    values = both_halves(value_ref).T
    found = []
    for head in range(2):
        weights = softmax_of(keys, only_head(head, query), bias).astype(jnp.bfloat16)
        found.append(dot(values[head * HEAD_DIM : (head + 1) * HEAD_DIM], weights))
    context = jnp.concatenate(found, axis=0).T.astype(jnp.bfloat16)
    out_ref[...] = context.reshape(out_ref.shape)


def attend_back_kernel(
    query_ref, key_ref, value_ref, upstream_ref, seg_key, seg_query, out_ref, bias
):
    write_bias(bias, seg_key, seg_query)
    scale = HEAD_DIM**-0.5
    query = both_halves(query_ref) * jnp.asarray(scale, jnp.bfloat16)
    keys = both_halves(key_ref)
    values = both_halves(value_ref)
    upstream = both_halves(upstream_ref)
    flipped = keys.T
    found_query, found_key, found_value = [], [], []
    for head in range(2):
        weights = softmax_of(keys, only_head(head, query), bias)
        grad_weights = dot(only_head(head, values), upstream, FAR)
        inner = jnp.sum(weights * grad_weights, axis=0, keepdims=True)
        grad_scores = (weights * (grad_weights - inner)).astype(jnp.bfloat16)
        found_value.append(dot(weights.astype(jnp.bfloat16), upstream))
        found_key.append(dot(grad_scores, query))
        found_query.append(dot(flipped[head * HEAD_DIM : (head + 1) * HEAD_DIM], grad_scores))
    lane = lax.broadcasted_iota(jnp.int32, found_key[0].shape, 1)
    width = out_ref.shape[3] // 3
    block = query_ref.shape
    at = pl.program_id(1) * LANES

    def store(which, value):
        start = pl.multiple_of(at + which * width, LANES)
        out_ref[:, :, :, pl.ds(start, LANES)] = value.astype(jnp.bfloat16).reshape(block)

    store(0, jnp.concatenate(found_query, axis=0).T * scale)
    store(1, jnp.where(lane < HEAD_DIM, found_key[0], found_key[1]))
    store(2, jnp.where(lane < HEAD_DIM, found_value[0], found_value[1]))


LANES = 128


def head_block(length, first):
    return pl.BlockSpec((2, 1, length, LANES), lambda row, pair: (0, row, 0, first + pair))


def attention_specs(rows, length):
    return [
        pl.BlockSpec((1, 2 * length, 1), lambda row, pair: (row, 0, 0)),
        pl.BlockSpec((1, 1, 2 * length), lambda row, pair: (row, 0, 0)),
    ]


def attend(heads, seg_key, seg_query):
    _, rows, length, columns = heads.shape
    width = columns // 3
    pairs = width // LANES
    flops = 4 * rows * width * (2 * length) ** 2
    return pl.pallas_call(
        attend_kernel,
        grid=(rows, pairs),
        out_shape=jax.ShapeDtypeStruct((2, rows, length, width), jnp.bfloat16),
        in_specs=[
            head_block(length, 0),
            head_block(length, pairs),
            head_block(length, 2 * pairs),
            *attention_specs(rows, length),
        ],
        out_specs=head_block(length, 0),
        scratch_shapes=[pltpu.VMEM((2 * length, 2 * length), jnp.float32)],
        cost_estimate=pl.CostEstimate(
            flops=flops, bytes_accessed=8 * heads.size // 3, transcendentals=flops // 256
        ),
        name="attend",
    )(heads, heads, heads, seg_key, seg_query)


def attend_back(heads, upstream, seg_key, seg_query):
    _, rows, length, columns = heads.shape
    width = columns // 3
    pairs = width // LANES
    flops = 10 * rows * width * (2 * length) ** 2
    return pl.pallas_call(
        attend_back_kernel,
        grid=(rows, pairs),
        out_shape=jax.ShapeDtypeStruct(heads.shape, jnp.bfloat16),
        in_specs=[
            head_block(length, 0),
            head_block(length, pairs),
            head_block(length, 2 * pairs),
            head_block(length, 0),
            *attention_specs(rows, length),
        ],
        out_specs=pl.BlockSpec((2, 1, length, columns), lambda row, pair: (0, row, 0, 0)),
        scratch_shapes=[pltpu.VMEM((2 * length, 2 * length), jnp.float32)],
        cost_estimate=pl.CostEstimate(
            flops=flops, bytes_accessed=14 * heads.size // 3, transcendentals=flops // 640
        ),
        name="attend_back",
    )(heads, heads, heads, upstream, seg_key, seg_query)


def normalize(hidden):
    center = hidden - jnp.mean(hidden, axis=-1, keepdims=True)
    inverse_scale = lax.rsqrt(jnp.mean(center * center, axis=-1, keepdims=True) + norm_epsilon)
    return (center * inverse_scale, inverse_scale)


def norm_back(upstream, normed, inverse_scale):
    mean_upstream = jnp.mean(upstream, axis=-1, keepdims=True)
    mean_cross = jnp.mean(upstream * normed, axis=-1, keepdims=True)
    return inverse_scale * (upstream - mean_upstream - normed * mean_cross)


def gelu_value(inputs):
    return 0.5 * inputs * (1.0 + lax.erf(inputs * root_half))


def gelu_slope(inputs):
    return (
        0.5 * (1.0 + lax.erf(inputs * root_half))
        + inputs * jnp.exp(-0.5 * inputs * inputs) * inv_root_tau
    )


def cross_rows(operand_left, operand_right):
    return lax.dot_general(
        operand_left, operand_right, (((0,), (0,)), ((), ())), preferred_element_type=jnp.float32
    )


def cross_cols(operand_left, operand_right):
    return dot(operand_left, operand_right, FAR)


def adamw(weight, moment, square, gradient, factor, step_rate):
    clipped = gradient * factor
    moment_new = decay_first * moment + (1.0 - decay_first) * clipped
    square_new = decay_second * square + (1.0 - decay_second) * clipped * clipped
    corrected = (
        moment_new
        / (1.0 - decay_first**STEP)
        / (jnp.sqrt(square_new / (1.0 - decay_second**STEP)) + adam_epsilon)
    )
    return (weight - step_rate * (corrected + weight_decay * weight), moment_new, square_new)


def swap_cores(value):
    return lax.ppermute(value, "seq", [(0, 1), (1, 0)])


def gather_plain(chips, heads, merge, expand, shrink, small, tokens):
    core = lax.axis_index("seq")

    def full(part):
        return lax.all_gather(part, ("dp", "seq"), axis=0, tiled=False)

    mine = lax.dynamic_index_in_dim(full(heads), core, 1, keepdims=False)
    return [mine, *map(full, (merge, expand, shrink, small)), jnp.stack([tokens, swap_cores(tokens)])]


def scatter_plain(chips, heads, merge, expand, shrink, small):
    def sums(part):
        flat = part.astype(jnp.float32).reshape((-1,) + part.shape[-2:])
        return lax.psum_scatter(flat, ("dp", "seq"), scatter_dimension=0, tiled=False)

    own = heads.astype(jnp.float32).reshape((-1, 2) + heads.shape[-2:])
    own = lax.psum_scatter(own, "dp", scatter_dimension=0, tiled=False)
    own = lax.all_to_all(own, "seq", split_axis=0, concat_axis=0, tiled=True)
    reduced = [own, *map(sums, (merge, expand, shrink))]
    squares = lax.psum(sum(jnp.sum(part * part) for part in reduced), ("dp", "seq"))
    return [*reduced, lax.psum(small, ("dp", "seq")), squares]


def per_device(
    chips,
    layer_input,
    segment_ids,
    cotangent,
    heads_weight,
    heads_first,
    heads_second,
    merge_weight,
    merge_first,
    merge_second,
    expand_weight,
    expand_first,
    expand_second,
    shrink_weight,
    shrink_first,
    shrink_second,
    norm_gains,
    gains_first,
    gains_second,
    branch_bias,
    branch_first,
    branch_second,
    hidden_bias,
    hidden_first,
    hidden_second,
):
    low, wide = jnp.bfloat16, jnp.float32
    core = lax.axis_index("seq")
    index = lax.axis_index("dp") * 2 + core
    row_count, length = layer_input.shape[:2]
    rows = heads_weight.shape[0]
    devices = chips * 2
    hidden_rows = shrink_weight.shape[0]
    half = D // 2
    flat_input = layer_input.reshape(-1, D)
    tokens = flat_input.shape[0]
    kernels = rows % 8 == 0 and chips == 16
    block = (chips // 4, 2, 2, 2) if kernels else (devices,)

    heads_parts = heads_weight.astype(low).reshape(rows, 3, 2, half)
    heads_parts = heads_parts.transpose(2, 0, 1, 3).reshape(2, rows, 3 * half)
    small_rows = -(-rows // 8) * 8 + 8
    small_part = jnp.zeros((small_rows, LANES), wide)
    small_part = small_part.at[:rows, 0:2].set(norm_gains).at[:rows, 2:8].set(branch_bias)
    small_part = small_part.at[small_rows - 8, :hidden_rows].set(hidden_bias).astype(low)
    gather = gather_all if kernels else gather_plain
    heads_all, merge_all, expand_all, shrink_all, small_all, inputs_all = gather(
        chips // 4,
        heads_parts,
        merge_weight.astype(low),
        expand_weight.astype(low),
        shrink_weight.astype(low),
        small_part,
        flat_input,
    )
    heads_low = heads_all.reshape(D, 3 * half)
    merge_low = merge_all.reshape(D, D)
    expand_low = expand_all.reshape(D, -1)
    shrink_low = shrink_all.reshape(-1, D)
    small_all = small_all.reshape(devices, small_rows, LANES).astype(wide)
    vectors = small_all[:, :rows, :8].reshape(D, 8).T
    gain_one, gain_two = vectors[0], vectors[1]
    hidden_full = small_all[:, small_rows - 8, :hidden_rows].reshape(-1)
    heads_bias = jnp.concatenate(
        [
            lax.dynamic_slice(vectors[2], (core * half,), (half,)),
            jnp.zeros((half,), wide),
            lax.dynamic_slice(vectors[3], (core * half,), (half,)),
        ]
    )

    seg_own = lax.dynamic_slice(segment_ids, (0, core * length), (row_count, length))
    seg_other = lax.dynamic_slice(segment_ids, (0, (1 - core) * length), (row_count, length))
    seg_here = jnp.concatenate([seg_own, seg_other], axis=1)
    seg_key, seg_query = seg_here[:, :, None], seg_here[:, None, :]

    inputs_both = inputs_all.reshape(2 * tokens, D)
    projected = (dot(inputs_both, heads_low) + heads_bias).astype(low)
    heads_here = projected.reshape(2, row_count, length, 3 * half)
    context_here = attend(heads_here, seg_key, seg_query).reshape(2, tokens, half)
    context_other = swap_cores(context_here[1])
    first_heads = jnp.where(core == 0, context_here[0], context_other)
    last_heads = jnp.where(core == 0, context_other, context_here[0])
    flat_context = jnp.concatenate([first_heads, last_heads], axis=1)
    attended = dot(flat_context, merge_low) + vectors[4]
    normed_one, inverse_one = normalize(flat_input.astype(wide) + attended)
    first_low = (normed_one * gain_one + vectors[5]).astype(low)
    pre_active = dot(first_low, expand_low) + hidden_full
    active_low = gelu_value(pre_active).astype(low)
    branch_out = dot(active_low, shrink_low) + vectors[6]
    normed_two, inverse_two = normalize(first_low.astype(wide) + branch_out)
    work_output = (normed_two * gain_two + vectors[7]).astype(low).reshape(layer_input.shape)

    upstream = cotangent.reshape(-1, D).astype(wide)
    grad_gain_two = jnp.sum(upstream * normed_two, axis=0)
    grad_shift_two = jnp.sum(upstream, axis=0)
    grad_second = norm_back(upstream * gain_two, normed_two, inverse_two)
    branch_grad = grad_second.astype(low)
    grad_shrink = cross_rows(active_low, branch_grad).astype(low)
    grad_shrink_bias = jnp.sum(branch_grad.astype(wide), axis=0)
    active_grad = (cross_cols(branch_grad, shrink_low) * gelu_slope(pre_active)).astype(low)
    grad_expand = cross_rows(first_low, active_grad).astype(low)
    grad_hidden = jnp.sum(active_grad.astype(wide), axis=0)
    grad_first = grad_second + cross_cols(active_grad, expand_low)
    grad_gain_one = jnp.sum(grad_first * normed_one, axis=0)
    grad_shift_one = jnp.sum(grad_first, axis=0)
    grad_sum_one = norm_back(grad_first * gain_one, normed_one, inverse_one)
    attended_grad = grad_sum_one.astype(low)
    grad_merge = cross_rows(flat_context, attended_grad).astype(low)
    grad_merge_bias = jnp.sum(attended_grad.astype(wide), axis=0)
    context_grad = cross_cols(attended_grad, merge_low).astype(low)
    context_grad_own = jnp.where(core == 0, context_grad[:, :half], context_grad[:, half:])
    context_grad_other = swap_cores(
        jnp.where(core == 0, context_grad[:, half:], context_grad[:, :half])
    )
    grad_here = jnp.stack([context_grad_own, context_grad_other])
    heads_grad = attend_back(
        heads_here, grad_here.reshape(2, row_count, length, half), seg_key, seg_query
    ).reshape(2 * tokens, 3 * half)
    input_parts = cross_cols(heads_grad, heads_low)
    input_other = swap_cores(input_parts[tokens:].astype(low))
    work_gradient = (grad_sum_one + input_parts[:tokens] + input_other.astype(wide)).reshape(
        layer_input.shape
    )
    grad_heads = cross_rows(inputs_both, heads_grad).astype(low)
    heads_bias_grad = jnp.sum(heads_grad.astype(wide), axis=0)

    def own_columns(piece):
        return lax.dynamic_update_slice(jnp.zeros((D,), wide), piece, (core * half,))

    small_grad = jnp.stack(
        [
            grad_gain_one,
            grad_gain_two,
            own_columns(heads_bias_grad[:half]),
            own_columns(heads_bias_grad[2 * half :]),
            grad_merge_bias,
            grad_shift_one,
            grad_shrink_bias,
            grad_shift_two,
        ]
    )
    small_grad = jnp.concatenate([small_grad, grad_hidden.reshape(-1, D)], axis=0)
    small_grad = jnp.pad(small_grad, ((0, -small_grad.shape[0] % 8), (0, 0)))

    scatter = scatter_all if kernels else scatter_plain
    heads_sum, merge_sum, expand_sum, shrink_sum, small_sum, squares = scatter(
        chips // 4,
        grad_heads.reshape(block + (rows, 3 * half)),
        grad_merge.reshape(block + (rows, D)),
        grad_expand.reshape(block + (rows, expand_weight.shape[1])),
        grad_shrink.reshape(block + (hidden_rows, D)),
        small_grad,
    )
    heads_sum = heads_sum.reshape(2, rows, 3, half)
    heads_sum = heads_sum.transpose(1, 2, 0, 3).reshape(rows, 3 * D)
    vector_sum = lax.dynamic_slice(small_sum, (0, index * rows), (8, rows)).T
    hidden_sum = lax.dynamic_slice(
        small_sum[8 : 8 + hidden_rows * devices // D].reshape(-1), (index * hidden_rows,), (hidden_rows,)
    )
    gradient_norm = jnp.sqrt(jnp.sum(squares) + jnp.sum(small_sum * small_sum))
    factor = jnp.minimum(1.0, clip_limit / gradient_norm)
    reduced = (
        heads_sum,
        merge_sum,
        expand_sum,
        shrink_sum,
        vector_sum[:, 0:2],
        vector_sum[:, 2:8],
        hidden_sum,
    )
    states = (
        (heads_weight, heads_first, heads_second, rate_matrix),
        (merge_weight, merge_first, merge_second, rate_matrix),
        (expand_weight, expand_first, expand_second, rate_matrix),
        (shrink_weight, shrink_first, shrink_second, rate_matrix),
        (norm_gains, gains_first, gains_second, rate_vector),
        (branch_bias, branch_first, branch_second, rate_vector),
        (hidden_bias, hidden_first, hidden_second, rate_vector),
    )
    results = [
        adamw(state[0], state[1], state[2], gradient, factor, state[3])
        for state, gradient in zip(states, reduced)
    ]
    return (
        work_output,
        work_gradient,
        gradient_norm,
        *[value for result in results for value in result],
        *[result[0].astype(low) for result in results[:4]],
    )


def solution(mesh):
    matrix, vector = P(("dp", "seq"), None), P(("dp", "seq"))
    tokens = P("dp", "seq", None)
    states = (matrix,) * 18 + (vector,) * 3
    return jax.shard_map(
        functools.partial(per_device, mesh.shape["dp"]),
        mesh=mesh,
        in_specs=(tokens, P("dp", None), tokens) + states,
        out_specs=(tokens, tokens, P()) + states + (matrix,) * 4,
        check_vma=False,
    )
```

```python
import functools

import jax
import jax.numpy as jnp
from jax import lax
from jax.experimental import pallas as pl
from jax.experimental.pallas import tpu as pltpu
from jax.sharding import PartitionSpec as P

D = 768
HEAD_DIM = 64
STEP = 5
LANES = 128
MESH = pl.DeviceIdType.MESH

norm_epsilon = 1e-12
masked_score = -1e30
root_half = 0.7071067811865476
inv_root_tau = 0.3989422804014327
clip_limit = 1.0
decay_first = 0.9
decay_second = 0.999
adam_epsilon = 1e-08
weight_decay = 0.01
rate_matrix = 0.05
rate_vector = 0.5


def place():
    chip, core = lax.axis_index("dp"), lax.axis_index("seq")
    return chip // 4, (chip // 2) % 2, chip % 2, core


def device(z, y, x, core):
    return ((z * 2 + y) * 2 + x, core)


def signal(semaphore, target):
    pl.semaphore_signal(semaphore, inc=1, device_id=target, device_id_type=MESH)


def greet(layers, others=()):
    z, y, x, core = place()
    barrier = pltpu.get_barrier_semaphore()
    across = (device(z, y, x, 1 - core), device(z, y, 1 - x, core), device(z, 1 - y, x, core))
    for target in across + tuple(others):
        signal(barrier, target)

    @pl.when(z > 0)
    def _():
        signal(barrier, device(z - 1, y, x, core))

    @pl.when(z < layers - 1)
    def _():
        signal(barrier, device(z + 1, y, x, core))

    beside = jnp.where(z > 0, 1, 0) + jnp.where(z < layers - 1, 1, 0)
    pl.semaphore_wait(barrier, 3 + len(others) + beside)


def remote(source, target, sent, received, to):
    return pltpu.make_async_remote_copy(
        src_ref=source,
        dst_ref=target,
        send_sem=sent,
        recv_sem=received,
        device_id=to,
        device_id_type=MESH,
    )


GATHERED = (
    ("heads", 0, 768, False),
    ("merge", 0, 768, True),
    ("small", 0, 128, True),
    ("heads", 768, 384, True),
    ("shrink", 0, 768, False),
    ("expand", 0, 3072, True),
)


def gather_kernel(
    layers,
    heads_in,
    merge_in,
    expand_in,
    shrink_in,
    small_in,
    tokens_in,
    heads_all,
    merge_all,
    expand_all,
    shrink_all,
    small_all,
    tokens_all,
    heads_block,
    token_room,
    pair_send,
    pair_recv,
    own_sem,
    line_send,
    line_recv,
    first_send,
    first_recv,
    second_send,
    second_recv,
    core_send,
    core_recv,
):
    z, y, x, core = place()
    partner = device(z, y, x, 1 - core)
    own = {"merge": merge_in, "expand": expand_in, "shrink": shrink_in, "small": small_in}
    full = {
        "merge": merge_all,
        "expand": expand_all,
        "shrink": shrink_all,
        "small": small_all,
        "heads": heads_all,
    }
    greet(layers)

    heads_out = remote(
        heads_in.at[1 - core], heads_block.at[core], pair_send.at[0], pair_recv.at[0], partner
    )
    heads_out.start()
    heads_keep = pltpu.make_async_copy(heads_in.at[core], heads_block.at[core], own_sem.at[0])
    heads_keep.start()
    tokens_load = pltpu.make_async_copy(tokens_in, token_room, own_sem.at[1])
    tokens_load.start()

    def own_block(piece):
        name, start, width, _ = GATHERED[piece]
        if name == "heads":
            return heads_block.at[:, :, pl.ds(start, width)]
        return own[name]

    def block(piece, zz, yy, xx, plane):
        name, start, width, _ = GATHERED[piece]
        if name == "heads":
            return full[name].at[zz, yy, xx, :, :, pl.ds(start, width)]
        return full[name].at[zz, yy, xx, plane]

    def couple(piece, zz, plane, moved):
        name, start, width, y_first = GATHERED[piece]
        yy = y if y_first or not moved else 1 - y
        xx = x if not y_first or not moved else 1 - x
        if name == "heads":
            if y_first:
                return full[name].at[zz, :, xx, :, :, pl.ds(start, width)]
            return full[name].at[zz, yy, :, :, :, pl.ds(start, width)]
        if y_first:
            return full[name].at[zz, :, xx, plane]
        return full[name].at[zz, yy, :, plane]

    def across(piece, second):
        y_turn = GATHERED[piece][3] != second
        return device(z, 1 - y, x, core) if y_turn else device(z, y, 1 - x, core)

    def first_block(piece, zz):
        if GATHERED[piece][3]:
            return (zz, 1 - y, x)
        return (zz, y, 1 - x)

    def line_copy(piece, zz, source, target_z):
        return remote(
            source,
            block(piece, zz, y, x, core),
            line_send.at[piece, zz, jnp.where(target_z > z, 0, 1)],
            line_recv.at[piece, zz],
            device(target_z, y, x, core),
        )

    def first_copy(piece, zz, source):
        return remote(
            source,
            block(piece, zz, y, x, core),
            first_send.at[piece, zz],
            first_recv.at[piece, zz],
            across(piece, False),
        )

    def second_copy(piece, zz):
        both = couple(piece, zz, core, False)
        return remote(
            both, both, second_send.at[piece, zz], second_recv.at[piece, zz], across(piece, True)
        )

    def core_copy(piece, zz, stage, source, target):
        return remote(
            source,
            target,
            core_send.at[piece, zz, stage],
            core_recv.at[piece, zz, stage],
            partner,
        )

    def shared(piece):
        return GATHERED[piece][0] != "heads"

    pieces = range(len(GATHERED))
    order = sorted(pieces, key=lambda piece: (GATHERED[piece][0] == "heads", piece))

    def begin(piece):
        mine = own_block(piece)

        @pl.when(z < layers - 1)
        def _():
            line_copy(piece, z, mine, z + 1).start()

        @pl.when(z > 0)
        def _():
            line_copy(piece, z, mine, z - 1).start()

        first_copy(piece, z, mine).start()
        if shared(piece):
            core_copy(piece, z, 0, mine, block(piece, z, y, x, core)).start()
        pltpu.make_async_copy(
            mine, block(piece, z, y, x, core), own_sem.at[2 + piece]
        ).start()

    for piece in order:
        if piece == order[-2]:
            heads_out.wait_recv()
            heads_keep.wait()
        begin(piece)
    tokens_load.wait()
    tokens_out = remote(
        token_room, tokens_all.at[1], pair_send.at[1], pair_recv.at[1], partner
    )
    tokens_out.start()
    tokens_keep = pltpu.make_async_copy(token_room, tokens_all.at[0], own_sem.at[1])
    tokens_keep.start()
    for piece in order:
        pltpu.make_async_copy(
            own_block(piece), block(piece, z, y, x, core), own_sem.at[2 + piece]
        ).wait()

    def arrive_line(piece, zz, below):
        here = block(piece, zz, y, x, core)
        line_copy(piece, zz, here, z).wait_recv()
        if below:

            @pl.when(z < layers - 1)
            def _():
                line_copy(piece, zz, here, z + 1).start()

        else:

            @pl.when(z > 0)
            def _():
                line_copy(piece, zz, here, z - 1).start()

        first_copy(piece, zz, here).start()
        if shared(piece):
            core_copy(piece, zz, 0, here, here).start()

    def arrive_first(piece, zz):
        here = block(piece, *first_block(piece, zz), core)
        remote(
            here, here, first_send.at[piece, zz], first_recv.at[piece, zz], across(piece, False)
        ).wait_recv()
        second_copy(piece, zz).start()
        if shared(piece):
            core_copy(piece, zz, 1, here, here).start()

    def arrive_second(piece, zz):
        here = couple(piece, zz, core, True)
        remote(
            here, here, second_send.at[piece, zz], second_recv.at[piece, zz], across(piece, True)
        ).wait_recv()
        if shared(piece):
            core_copy(piece, zz, 2, here, here).start()

    def each(distance, action):
        if distance == 0:
            action(z, None)
            return

        @pl.when(z - distance >= 0)
        def _():
            action(z - distance, True)

        @pl.when(z + distance < layers)
        def _():
            action(z + distance, False)

    for step in range(layers + 2):
        for piece in pieces:
            if 0 < step < layers:
                each(step, lambda zz, below, piece=piece: arrive_line(piece, zz, below))
            if 0 <= step - 1 < layers:
                each(step - 1, lambda zz, below, piece=piece: arrive_first(piece, zz))
            if 0 <= step - 2 < layers:
                each(step - 2, lambda zz, below, piece=piece: arrive_second(piece, zz))

    heads_out.wait_send()
    tokens_out.wait_send()
    remote(
        token_room, tokens_all.at[1], pair_send.at[1], pair_recv.at[1], partner
    ).wait_recv()
    tokens_keep.wait()
    other = 1 - core
    for piece in pieces:
        for zz in range(layers):
            mine = block(piece, zz, y, x, core)
            theirs = block(piece, zz, y, x, other)
            crossed = block(piece, *first_block(piece, zz), other)
            first_copy(piece, zz, mine).wait_send()
            second_copy(piece, zz).wait_send()
            if shared(piece):
                core_copy(piece, zz, 0, mine, theirs).wait()
                core_copy(piece, zz, 1, mine, crossed).wait()
                both = couple(piece, zz, other, True)
                core_copy(piece, zz, 2, both, both).wait()

            @pl.when(jnp.logical_and(z < layers - 1, zz <= z))
            def _(piece=piece, zz=zz, mine=mine):
                line_copy(piece, zz, mine, z + 1).wait_send()

            @pl.when(jnp.logical_and(z > 0, zz >= z))
            def _(piece=piece, zz=zz, mine=mine):
                line_copy(piece, zz, mine, z - 1).wait_send()


def gather_all(layers, heads, merge, expand, shrink, small, tokens):
    chips = (layers, 2, 2, 2)
    low = jnp.bfloat16
    count = len(GATHERED)
    sems = pltpu.SemaphoreType.DMA
    inputs = (heads, merge, expand, shrink, small)
    return pl.pallas_call(
        functools.partial(gather_kernel, layers),
        out_shape=[
            jax.ShapeDtypeStruct(chips + heads.shape[1:], low),
            *[jax.ShapeDtypeStruct(chips + part.shape, low) for part in inputs[1:]],
            jax.ShapeDtypeStruct((2,) + tokens.shape, low),
        ],
        in_specs=[pl.BlockSpec(memory_space=pltpu.VMEM)] * 5 + [pl.BlockSpec(memory_space=pl.ANY)],
        out_specs=[pl.BlockSpec(memory_space=pl.ANY)] * 6,
        scratch_shapes=[
            pltpu.VMEM(heads.shape, low),
            pltpu.VMEM(tokens.shape, low),
            sems((2,)),
            sems((2,)),
            sems((2 + count,)),
            sems((count, layers, 2)),
            sems((count, layers)),
            sems((count, layers)),
            sems((count, layers)),
            sems((count, layers)),
            sems((count, layers)),
            sems((count, layers, 3)),
            sems((count, layers, 3)),
        ],
        compiler_params=pltpu.CompilerParams(collective_id=0, has_side_effects=True),
        name="gather_all",
    )(*inputs, tokens)


SCATTERED = (
    ("shrink", 0, 768, False),
    ("expand", 0, 3072, True),
    ("merge", 0, 768, True),
    ("heads", 0, 768, False),
    ("heads", 768, 384, True),
)
BITS = 5


def finish_kernel(
    layers,
    heads_ref,
    upstream_ref,
    seg_key,
    seg_query,
    inputs_ref,
    weight_ref,
    merge_in,
    expand_in,
    shrink_in,
    small_in,
    heads_out,
    merge_out,
    expand_out,
    shrink_out,
    small_out,
    square_out,
    tokens_out,
    heads_here,
    upstream_here,
    heads_grad,
    inputs_here,
    weight_here,
    bias,
    tokens_sent,
    tokens_room,
    totals,
    core_rooms,
    first_rooms,
    second_rooms,
    line_rooms,
    heads_last,
    heads_room,
    small_now,
    small_room,
    square_now,
    square_room,
    bring_sem,
    upstream_send,
    upstream_recv,
    tokens_send,
    tokens_recv,
    load_sem,
    core_send,
    core_recv,
    first_send,
    first_recv,
    second_send,
    second_recv,
    line_send,
    line_recv,
    last_send,
    last_recv,
    small_send,
    small_recv,
    square_send,
    square_recv,
):
    z, y, x, core = place()
    partner = device(z, y, x, 1 - core)
    sources = {"merge": merge_in, "expand": expand_in, "shrink": shrink_in}
    results = {"merge": merge_out, "expand": expand_out, "shrink": shrink_out}
    opposite = (
        partner,
        device(z, y, 1 - x, core),
        device(z, 1 - y, x, core),
        device(z + 1 - 2 * (z % 2), y, x, core),
        device((z + 2) % 4, y, x, core),
    )
    low, wide = jnp.bfloat16, jnp.float32
    _, rows, length, columns = heads_here.shape
    width = columns // 3
    pairs = width // LANES

    def bring_row(row):
        return pltpu.make_async_copy(heads_ref.at[:, row], heads_here.at[:, row], bring_sem.at[row])

    def columns_of(plane):
        return pl.ds(pl.multiple_of(plane * width, LANES), width)

    def upstream_keep(row):
        return pltpu.make_async_copy(
            upstream_ref.at[row, :, columns_of(core)], upstream_here.at[0, row], bring_sem.at[4 + row]
        )

    def upstream_copy(row):
        return remote(
            upstream_ref.at[row, :, columns_of(1 - core)],
            upstream_here.at[1, row],
            upstream_send.at[row],
            upstream_recv.at[row],
            partner,
        )

    bring_inputs = pltpu.make_async_copy(inputs_ref, inputs_here, bring_sem.at[8])
    bring_weight = pltpu.make_async_copy(weight_ref, weight_here, bring_sem.at[9])
    for row in range(rows):
        bring_row(row).start()
        upstream_keep(row).start()

    greet(layers, opposite[4:])
    for row in range(rows):
        upstream_copy(row).start()

    pieces = range(len(SCATTERED))
    early = [piece for piece in pieces if SCATTERED[piece][0] != "heads"]
    late = [piece for piece in pieces if SCATTERED[piece][0] == "heads"]

    def is_heads(piece):
        return SCATTERED[piece][0] == "heads"

    def y_first(piece):
        return SCATTERED[piece][3]

    def load(piece, zz):
        return pltpu.make_async_copy(
            sources[SCATTERED[piece][0]].at[zz, :, :, core], totals[piece].at[zz], load_sem.at[piece, zz]
        )

    def core_copy(piece, zz):
        return remote(
            sources[SCATTERED[piece][0]].at[zz, :, :, 1 - core],
            core_rooms[piece].at[zz],
            core_send.at[piece, zz],
            core_recv.at[piece, zz],
            partner,
        )

    def first_copy(piece, zz):
        if y_first(piece):
            source, to = totals[piece].at[zz, 1 - y], device(z, 1 - y, x, core)
        else:
            source, to = totals[piece].at[zz, :, 1 - x], device(z, y, 1 - x, core)
        return remote(
            source, first_rooms[piece].at[zz], first_send.at[piece, zz], first_recv.at[piece, zz], to
        )

    def second_copy(piece, zz):
        if y_first(piece):
            source, to = totals[piece].at[zz, y, 1 - x], device(z, y, 1 - x, core)
        else:
            source, to = totals[piece].at[zz, 1 - y, x], device(z, 1 - y, x, core)
        return remote(
            source,
            second_rooms[piece].at[zz],
            second_send.at[piece, zz],
            second_recv.at[piece, zz],
            to,
        )

    def line_copy(piece, zz, downward):
        to = z - 1 if downward else z + 1
        return remote(
            totals[piece].at[zz, y, x],
            line_rooms[piece].at[downward, zz],
            line_send.at[piece, zz],
            line_recv.at[piece, downward, zz],
            device(to, y, x, core),
        )

    def add(target, room):
        target[...] = (target[...].astype(wide) + room[...].astype(wide)).astype(low)

    def layer_of(step):
        return jnp.where(step % 2 == 0, step // 2, layers - 1 - step // 2)

    def on_first(piece, zz):
        if not is_heads(piece):
            load(piece, zz).wait()
            core_copy(piece, zz).wait_recv()

            def merge_one(index, carry):
                add(
                    totals[piece].at[zz, index // 2, index % 2],
                    core_rooms[piece].at[zz, index // 2, index % 2],
                )
                return carry

            lax.fori_loop(0, 4, merge_one, 0)
        first_copy(piece, zz).start()

    def on_second(piece, zz):
        first_copy(piece, zz).wait_recv()

        def merge_one(index, carry):
            if y_first(piece):
                target = totals[piece].at[zz, y, index]
            else:
                target = totals[piece].at[zz, index, x]
            add(target, first_rooms[piece].at[zz, index])
            return carry

        lax.fori_loop(0, 2, merge_one, 0)
        second_copy(piece, zz).start()

    def on_line(piece, zz):
        second_copy(piece, zz).wait_recv()
        mine = totals[piece].at[zz, y, x]
        add(mine, second_rooms[piece].at[zz])

        @pl.when(zz > z)
        def _():
            @pl.when(z > 0)
            def _():
                line_copy(piece, zz, 0).wait_recv()
                add(mine, line_rooms[piece].at[0, zz])

            line_copy(piece, zz, 0).start()

        @pl.when(zz < z)
        def _():
            @pl.when(z < layers - 1)
            def _():
                line_copy(piece, zz, 1).wait_recv()
                add(mine, line_rooms[piece].at[1, zz])

            line_copy(piece, zz, 1).start()

    def small_copy(bit):
        return remote(
            small_now.at[bit], small_room.at[bit], small_send.at[bit], small_recv.at[bit], opposite[bit]
        )

    def on_small(bit):
        small_copy(bit).wait_recv()
        summed = small_now[bit] + small_room[bit]
        if bit + 1 < BITS:
            small_now[bit + 1] = summed
            small_copy(bit + 1).start()
        else:
            small_out[...] = summed

    def start_early(step, carry):
        for piece in early:
            core_copy(piece, layer_of(step)).start()
            load(piece, layer_of(step)).start()
        return carry

    lax.fori_loop(0, layers, start_early, 0)
    bring_inputs.start()
    bring_weight.start()

    scale = HEAD_DIM**-0.5

    def attention_step(step, carry):
        row, pair = step // pairs, step % pairs

        @pl.when(pair == 0)
        def _():
            bring_row(row).wait()
            upstream_keep(row).wait()
            upstream_copy(row).wait_recv()
            bias[...] = jnp.where(seg_key[row] == seg_query[row], 0.0, masked_score)

        def part(which):
            start = pl.multiple_of(which * width + pair * LANES, LANES)
            return heads_here[:, row, :, pl.ds(start, LANES)].reshape(2 * length, LANES)

        at = pl.multiple_of(pair * LANES, LANES)
        upstream = upstream_here[:, row, :, pl.ds(at, LANES)].reshape(2 * length, LANES)
        grads = pair_back(part(0), part(1), part(2), upstream, bias)
        for which in range(3):
            start = pl.multiple_of(which * width + pair * LANES, LANES)
            heads_grad[:, row, :, pl.ds(start, LANES)] = grads[which].reshape(2, length, LANES)

        @pl.when(step < layers)
        def _():
            for piece in early:
                on_first(piece, layer_of(step))

        @pl.when(jnp.logical_and(step >= layers, step % 2 == 0))
        def _():
            for piece in early:
                on_second(piece, layer_of((step - layers) // 2))

        @pl.when(jnp.logical_and(step >= 7, step % 2 == 1))
        def _():
            for piece in early:
                on_line(piece, layer_of((step - 7) // 2))

        return carry

    lax.fori_loop(0, rows * pairs, attention_step, 0)

    bring_inputs.wait()
    flat_grad = heads_grad[...].reshape(2 * rows * length, columns)
    ones = jnp.ones((8, 2 * rows * length), low)
    sums = dot(ones, flat_grad)
    small_now[0] = small_in[...]
    small_now[0, 2:3, columns_of(core)] = sums[0:1, 0:width]
    small_now[0, 3:4, columns_of(core)] = sums[0:1, 2 * width : 3 * width]
    small_copy(0).start()
    depth = inputs_here.shape[1] // 2

    def weight_step(step, carry):
        start = pl.multiple_of(step * depth, LANES)
        found = dot(inputs_here[:, pl.ds(start, depth)], flat_grad, (((0,), (0,)), ((), ())))
        for piece in late:
            _, first, wide_by, _ = SCATTERED[piece]
            block = found[:, first : first + wide_by]
            block = block.reshape((layers // 2,) + totals[piece].shape[1:]).astype(low)
            totals[piece][pl.ds(step * (layers // 2), layers // 2)] = block
        for piece in late:
            for which in range(layers // 2):
                on_first(piece, step * (layers // 2) + which)
        return carry

    lax.fori_loop(0, 2, weight_step, 0)
    for piece in early:
        on_line(piece, layer_of(layers - 1))

    bring_weight.wait()

    def tokens_copy(row):
        return remote(
            tokens_sent.at[row], tokens_room.at[row], tokens_send.at[row], tokens_recv.at[row], partner
        )

    def other_step(row, carry):
        tokens_sent[row] = dot(heads_grad[1, row], weight_here[...], FAR).astype(low)
        tokens_copy(row).start()
        for bit in range(BITS - 1):

            @pl.when(row == bit)
            def _(bit=bit):
                on_small(bit)

        return carry

    def own_step(row, carry):
        found = dot(heads_grad[0, row], weight_here[...], FAR)
        tokens_copy(row).wait_recv()
        tokens_out[row] = found + tokens_room[row].astype(wide)
        for piece in late:
            on_second(piece, layer_of(row))
        return carry

    lax.fori_loop(0, rows, other_step, 0)
    lax.fori_loop(0, rows, own_step, 0)
    on_small(BITS - 1)

    def line_step(step, carry):
        for piece in late:
            on_line(piece, layer_of(step))
        return carry

    lax.fori_loop(0, layers, line_step, 0)

    def squares(value):
        by_row = jnp.sum((value * value).reshape(value.shape[0] // 8, 8, value.shape[1]), axis=0)
        total = by_row[:, 0:LANES]
        for start in range(LANES, value.shape[1], LANES):
            total = total + by_row[:, start : start + LANES]
        return total

    def last_copy(piece):
        _, start, wide_by, _ = SCATTERED[piece]
        return remote(
            heads_last.at[:, pl.ds(start, wide_by)],
            heads_room.at[:, pl.ds(start, wide_by)],
            last_send.at[piece],
            last_recv.at[piece],
            partner,
        )

    square_now[0] = jnp.zeros((8, LANES), wide)
    for piece in early + late:
        name, start, wide_by, _ = SCATTERED[piece]
        mine = totals[piece].at[z, y, x]

        @pl.when(z > 0)
        def _(piece=piece, mine=mine):
            line_copy(piece, z, 0).wait_recv()
            add(mine, line_rooms[piece].at[0, z])

        @pl.when(z < layers - 1)
        def _(piece=piece, mine=mine):
            line_copy(piece, z, 1).wait_recv()
            add(mine, line_rooms[piece].at[1, z])

        if is_heads(piece):
            heads_last[:, start : start + wide_by] = mine[1 - core]
            last_copy(piece).start()
            kept = mine[core].astype(wide)
            heads_out[core, :, start : start + wide_by] = kept
        else:
            kept = mine[...].astype(wide)
            results[name][...] = kept
        square_now[0] += squares(kept)
    for piece in late:
        _, start, wide_by, _ = SCATTERED[piece]
        last_copy(piece).wait_recv()
        theirs = heads_room[:, start : start + wide_by].astype(wide)
        heads_out[1 - core, :, start : start + wide_by] = theirs
        square_now[0] += squares(theirs)

    for bit in range(BITS):
        across = remote(
            square_now.at[bit],
            square_room.at[bit],
            square_send.at[bit],
            square_recv.at[bit],
            opposite[bit],
        )
        across.start()
        across.wait()
        summed = square_now[bit] + square_room[bit]
        if bit + 1 < BITS:
            square_now[bit + 1] = summed
        else:
            square_out[...] = summed

    for bit in range(BITS):
        small_copy(bit).wait_send()
    for row in range(rows):
        upstream_copy(row).wait_send()
        tokens_copy(row).wait_send()

    def settle(zz, carry):
        for piece in pieces:
            if not is_heads(piece):
                core_copy(piece, zz).wait_send()
            first_copy(piece, zz).wait_send()
            second_copy(piece, zz).wait_send()

            @pl.when(zz > z)
            def _(piece=piece):
                line_copy(piece, zz, 0).wait_send()

            @pl.when(zz < z)
            def _(piece=piece):
                line_copy(piece, zz, 1).wait_send()

        return carry

    lax.fori_loop(0, layers, settle, 0)
    for piece in late:
        last_copy(piece).wait_send()


def finish_all(layers, heads, upstream, seg_key, seg_query, inputs, weight, merge, expand, shrink, small):
    low, wide = jnp.bfloat16, jnp.float32
    block_rows = merge.shape[4]
    _, rows, length, columns = heads.shape
    width = columns // 3
    sums_rows = {"merge": block_rows, "expand": block_rows, "shrink": shrink.shape[4]}
    sems = pltpu.SemaphoreType.DMA

    def rooms(*lead, some=SCATTERED):
        return [
            pltpu.VMEM(
                tuple(lead)
                + ((2, block_rows, wide_by) if name == "heads" else (sums_rows[name], wide_by)),
                low,
            )
            for name, _, wide_by, _ in some
        ]

    count = len(SCATTERED)
    early = [piece for piece in SCATTERED if piece[0] != "heads"]
    vmem, anywhere = pl.BlockSpec(memory_space=pltpu.VMEM), pl.BlockSpec(memory_space=pl.ANY)
    return pl.pallas_call(
        functools.partial(finish_kernel, layers),
        out_shape=[
            jax.ShapeDtypeStruct((2, block_rows, columns), wide),
            *[jax.ShapeDtypeStruct(part.shape[4:], wide) for part in (merge, expand, shrink)],
            jax.ShapeDtypeStruct(small.shape, wide),
            jax.ShapeDtypeStruct((8, LANES), wide),
            jax.ShapeDtypeStruct((rows, length, inputs.shape[1]), wide),
        ],
        in_specs=[anywhere, anywhere, vmem, vmem] + [anywhere] * 5 + [vmem],
        out_specs=[vmem] * 7,
        scratch_shapes=[
            pltpu.VMEM(heads.shape, low),
            pltpu.VMEM((2, rows, length, width), low),
            pltpu.VMEM(heads.shape, low),
            pltpu.VMEM(inputs.shape, low),
            pltpu.VMEM(weight.shape, low),
            pltpu.VMEM((2 * length, 2 * length), wide),
            pltpu.VMEM((rows, length, inputs.shape[1]), low),
            pltpu.VMEM((rows, length, inputs.shape[1]), low),
            rooms(layers, 2, 2),
            rooms(layers, 2, 2, some=early),
            rooms(layers, 2),
            rooms(layers),
            rooms(2, layers),
            pltpu.VMEM((block_rows, columns), low),
            pltpu.VMEM((block_rows, columns), low),
            pltpu.VMEM((BITS,) + small.shape, wide),
            pltpu.VMEM((BITS,) + small.shape, wide),
            pltpu.VMEM((BITS, 8, LANES), wide),
            pltpu.VMEM((BITS, 8, LANES), wide),
            sems((10,)),
            sems((rows,)),
            sems((rows,)),
            sems((rows,)),
            sems((rows,)),
            sems((count, layers)),
            sems((count, layers)),
            sems((count, layers)),
            sems((count, layers)),
            sems((count, layers)),
            sems((count, layers)),
            sems((count, layers)),
            sems((count, layers)),
            sems((count, 2, layers)),
            sems((count,)),
            sems((count,)),
            sems((BITS,)),
            sems((BITS,)),
            sems((BITS,)),
            sems((BITS,)),
        ],
        compiler_params=pltpu.CompilerParams(
            collective_id=1, has_side_effects=True, vmem_limit_bytes=63 * 2**20
        ),
        name="finish_all",
    )(heads, upstream, seg_key, seg_query, inputs, weight, merge, expand, shrink, small)


def update_kernel(factor, *refs):
    count = len(refs) // 8
    for which in range(count):
        gradient, weight, moment, square = (refs[which * 4 + i] for i in range(4))
        outs = refs[count * 4 + which * 4 : count * 4 + which * 4 + 4]
        updated, first, second = adamw(
            weight[...], moment[...], square[...], gradient[...], factor[0, 0], rate_matrix
        )
        outs[0][...] = updated
        outs[1][...] = first
        outs[2][...] = second
        outs[3][...] = updated.astype(jnp.bfloat16)


def update_all(factor, states):
    whole = pl.BlockSpec(memory_space=pltpu.VMEM)
    flat = [part for state in states for part in state]
    shapes = []
    for state in states:
        shapes += [jax.ShapeDtypeStruct(state[1].shape, jnp.float32)] * 3
        shapes += [jax.ShapeDtypeStruct(state[1].shape, jnp.bfloat16)]
    found = pl.pallas_call(
        update_kernel,
        out_shape=shapes,
        in_specs=[pl.BlockSpec(memory_space=pltpu.SMEM)] + [whole] * len(flat),
        out_specs=[whole] * len(shapes),
        name="update_all",
    )(factor.reshape(1, 1), *flat)
    return [found[4 * which : 4 * which + 4] for which in range(len(states))]


FAR = (((1,), (1,)), ((), ()))
NEAR = (((1,), (0,)), ((), ()))


def dot(left, right, dims=NEAR):
    return lax.dot_general(left, right, dims, preferred_element_type=jnp.float32)


def write_bias(bias, seg_key, seg_query):
    @pl.when(pl.program_id(1) == 0)
    def _():
        bias[...] = jnp.where(seg_key[0] == seg_query[0], 0.0, masked_score)


def both_halves(ref):
    halves, rows, length, lanes = ref.shape
    return ref[...].reshape(halves * rows * length, lanes)


def only_head(head, value):
    lane = lax.broadcasted_iota(jnp.int32, value.shape, 1)
    return jnp.where((lane // HEAD_DIM) == head, value, jnp.zeros_like(value))


def softmax_of(keys, query, bias):
    scores = dot(keys, query, FAR) + bias[...]
    unscaled = jnp.exp(scores - jnp.max(scores, axis=0, keepdims=True))
    return unscaled * (1.0 / jnp.sum(unscaled, axis=0, keepdims=True))


def attend_kernel(query_ref, key_ref, value_ref, seg_key, seg_query, out_ref, bias):
    write_bias(bias, seg_key, seg_query)
    query = both_halves(query_ref) * jnp.asarray(HEAD_DIM**-0.5, jnp.bfloat16)
    keys = both_halves(key_ref)
    values = both_halves(value_ref).T
    found = []
    for head in range(2):
        weights = softmax_of(keys, only_head(head, query), bias).astype(jnp.bfloat16)
        found.append(dot(values[head * HEAD_DIM : (head + 1) * HEAD_DIM], weights))
    context = jnp.concatenate(found, axis=0).T.astype(jnp.bfloat16)
    out_ref[...] = context.reshape(out_ref.shape)


def pair_back(query, keys, values, upstream, bias):
    scale = HEAD_DIM**-0.5
    query = query * jnp.asarray(scale, jnp.bfloat16)
    flipped = keys.T
    found_query, found_key, found_value = [], [], []
    for head in range(2):
        weights = softmax_of(keys, only_head(head, query), bias)
        grad_weights = dot(only_head(head, values), upstream, FAR)
        inner = jnp.sum(weights * grad_weights, axis=0, keepdims=True)
        grad_scores = (weights * (grad_weights - inner)).astype(jnp.bfloat16)
        found_value.append(dot(weights.astype(jnp.bfloat16), upstream))
        found_key.append(dot(grad_scores, query))
        found_query.append(dot(flipped[head * HEAD_DIM : (head + 1) * HEAD_DIM], grad_scores))
    lane = lax.broadcasted_iota(jnp.int32, found_key[0].shape, 1)
    return (
        (jnp.concatenate(found_query, axis=0).T * scale).astype(jnp.bfloat16),
        jnp.where(lane < HEAD_DIM, found_key[0], found_key[1]).astype(jnp.bfloat16),
        jnp.where(lane < HEAD_DIM, found_value[0], found_value[1]).astype(jnp.bfloat16),
    )


def attend_back_kernel(
    query_ref, key_ref, value_ref, upstream_ref, seg_key, seg_query, out_ref, bias
):
    write_bias(bias, seg_key, seg_query)
    refs = (query_ref, key_ref, value_ref, upstream_ref)
    grads = pair_back(*[both_halves(ref) for ref in refs], bias)
    width = out_ref.shape[3] // 3
    for which in range(3):
        start = pl.multiple_of(pl.program_id(1) * LANES + which * width, LANES)
        out_ref[:, :, :, pl.ds(start, LANES)] = grads[which].reshape(query_ref.shape)


def head_block(length, first):
    return pl.BlockSpec((2, 1, length, LANES), lambda row, pair: (0, row, 0, first + pair))


def attention_specs(rows, length):
    return [
        pl.BlockSpec((1, 2 * length, 1), lambda row, pair: (row, 0, 0)),
        pl.BlockSpec((1, 1, 2 * length), lambda row, pair: (row, 0, 0)),
    ]


def attend(heads, seg_key, seg_query):
    _, rows, length, columns = heads.shape
    width = columns // 3
    pairs = width // LANES
    flops = 4 * rows * width * (2 * length) ** 2
    return pl.pallas_call(
        attend_kernel,
        grid=(rows, pairs),
        out_shape=jax.ShapeDtypeStruct((2, rows, length, width), jnp.bfloat16),
        in_specs=[
            head_block(length, 0),
            head_block(length, pairs),
            head_block(length, 2 * pairs),
            *attention_specs(rows, length),
        ],
        out_specs=head_block(length, 0),
        scratch_shapes=[pltpu.VMEM((2 * length, 2 * length), jnp.float32)],
        cost_estimate=pl.CostEstimate(
            flops=flops, bytes_accessed=8 * heads.size // 3, transcendentals=flops // 256
        ),
        name="attend",
    )(heads, heads, heads, seg_key, seg_query)


def attend_back(heads, upstream, seg_key, seg_query):
    _, rows, length, columns = heads.shape
    width = columns // 3
    pairs = width // LANES
    flops = 10 * rows * width * (2 * length) ** 2
    return pl.pallas_call(
        attend_back_kernel,
        grid=(rows, pairs),
        out_shape=jax.ShapeDtypeStruct(heads.shape, jnp.bfloat16),
        in_specs=[
            head_block(length, 0),
            head_block(length, pairs),
            head_block(length, 2 * pairs),
            head_block(length, 0),
            *attention_specs(rows, length),
        ],
        out_specs=pl.BlockSpec((2, 1, length, columns), lambda row, pair: (0, row, 0, 0)),
        scratch_shapes=[pltpu.VMEM((2 * length, 2 * length), jnp.float32)],
        cost_estimate=pl.CostEstimate(
            flops=flops, bytes_accessed=14 * heads.size // 3, transcendentals=flops // 640
        ),
        name="attend_back",
    )(heads, heads, heads, upstream, seg_key, seg_query)


def normalize(hidden):
    center = hidden - jnp.mean(hidden, axis=-1, keepdims=True)
    inverse_scale = lax.rsqrt(jnp.mean(center * center, axis=-1, keepdims=True) + norm_epsilon)
    return (center * inverse_scale, inverse_scale)


def norm_back(upstream, normed, inverse_scale):
    mean_upstream = jnp.mean(upstream, axis=-1, keepdims=True)
    mean_cross = jnp.mean(upstream * normed, axis=-1, keepdims=True)
    return inverse_scale * (upstream - mean_upstream - normed * mean_cross)


def gelu_value(inputs):
    return 0.5 * inputs * (1.0 + lax.erf(inputs * root_half))


def gelu_slope(inputs):
    return (
        0.5 * (1.0 + lax.erf(inputs * root_half))
        + inputs * jnp.exp(-0.5 * inputs * inputs) * inv_root_tau
    )


def cross_rows(operand_left, operand_right):
    return lax.dot_general(
        operand_left, operand_right, (((0,), (0,)), ((), ())), preferred_element_type=jnp.float32
    )


def cross_cols(operand_left, operand_right):
    return dot(operand_left, operand_right, FAR)


def adamw(weight, moment, square, gradient, factor, step_rate):
    clipped = gradient * factor
    moment_new = decay_first * moment + (1.0 - decay_first) * clipped
    square_new = decay_second * square + (1.0 - decay_second) * clipped * clipped
    corrected = (
        moment_new
        / (1.0 - decay_first**STEP)
        / (jnp.sqrt(square_new / (1.0 - decay_second**STEP)) + adam_epsilon)
    )
    return (weight - step_rate * (corrected + weight_decay * weight), moment_new, square_new)


def swap_cores(value):
    return lax.ppermute(value, "seq", [(0, 1), (1, 0)])


def gather_plain(chips, heads, merge, expand, shrink, small, tokens):
    core = lax.axis_index("seq")

    def full(part):
        return lax.all_gather(part, ("dp", "seq"), axis=0, tiled=False)

    mine = lax.dynamic_index_in_dim(full(heads), core, 1, keepdims=False)
    return [mine, *map(full, (merge, expand, shrink, small)), jnp.stack([tokens, swap_cores(tokens)])]


def scatter_plain(heads, merge, expand, shrink, small):
    def sums(part):
        flat = part.astype(jnp.float32).reshape((-1,) + part.shape[-2:])
        return lax.psum_scatter(flat, ("dp", "seq"), scatter_dimension=0, tiled=False)

    own = heads.astype(jnp.float32).reshape((-1, 2) + heads.shape[-2:])
    own = lax.psum_scatter(own, "dp", scatter_dimension=0, tiled=False)
    own = lax.all_to_all(own, "seq", split_axis=0, concat_axis=0, tiled=True)
    reduced = [own, *map(sums, (merge, expand, shrink))]
    squares = lax.psum(sum(jnp.sum(part * part) for part in reduced), ("dp", "seq"))
    return [*reduced, lax.psum(small, ("dp", "seq")), squares]


def per_device(
    chips,
    layer_input,
    segment_ids,
    cotangent,
    heads_weight,
    heads_first,
    heads_second,
    merge_weight,
    merge_first,
    merge_second,
    expand_weight,
    expand_first,
    expand_second,
    shrink_weight,
    shrink_first,
    shrink_second,
    norm_gains,
    gains_first,
    gains_second,
    branch_bias,
    branch_first,
    branch_second,
    hidden_bias,
    hidden_first,
    hidden_second,
):
    low, wide = jnp.bfloat16, jnp.float32
    core = lax.axis_index("seq")
    index = lax.axis_index("dp") * 2 + core
    row_count, length = layer_input.shape[:2]
    rows = heads_weight.shape[0]
    devices = chips * 2
    hidden_rows = shrink_weight.shape[0]
    half = D // 2
    flat_input = layer_input.reshape(-1, D)
    tokens = flat_input.shape[0]
    kernels = rows % 8 == 0 and chips == 16
    block = (chips // 4, 2, 2, 2) if kernels else (devices,)

    heads_parts = heads_weight.astype(low).reshape(rows, 3, 2, half)
    heads_parts = heads_parts.transpose(2, 0, 1, 3).reshape(2, rows, 3 * half)
    small_rows = -(-rows // 8) * 8 + 8
    small_part = jnp.zeros((small_rows, LANES), wide)
    small_part = small_part.at[:rows, 0:2].set(norm_gains).at[:rows, 2:8].set(branch_bias)
    small_part = small_part.at[small_rows - 8, :hidden_rows].set(hidden_bias).astype(low)
    gather = gather_all if kernels else gather_plain
    heads_all, merge_all, expand_all, shrink_all, small_all, inputs_all = gather(
        chips // 4,
        heads_parts,
        merge_weight.astype(low),
        expand_weight.astype(low),
        shrink_weight.astype(low),
        small_part,
        flat_input,
    )
    heads_low = heads_all.reshape(D, 3 * half)
    merge_low = merge_all.reshape(D, D)
    expand_low = expand_all.reshape(D, -1)
    shrink_low = shrink_all.reshape(-1, D)
    small_all = small_all.reshape(devices, small_rows, LANES).astype(wide)
    vectors = small_all[:, :rows, :8].reshape(D, 8).T
    gain_one, gain_two = vectors[0], vectors[1]
    hidden_full = small_all[:, small_rows - 8, :hidden_rows].reshape(-1)
    heads_bias = jnp.concatenate(
        [
            lax.dynamic_slice(vectors[2], (core * half,), (half,)),
            jnp.zeros((half,), wide),
            lax.dynamic_slice(vectors[3], (core * half,), (half,)),
        ]
    )

    seg_own = lax.dynamic_slice(segment_ids, (0, core * length), (row_count, length))
    seg_other = lax.dynamic_slice(segment_ids, (0, (1 - core) * length), (row_count, length))
    seg_here = jnp.concatenate([seg_own, seg_other], axis=1)
    seg_key, seg_query = seg_here[:, :, None], seg_here[:, None, :]

    inputs_both = inputs_all.reshape(2 * tokens, D)
    projected = (dot(inputs_both, heads_low) + heads_bias).astype(low)
    heads_here = projected.reshape(2, row_count, length, 3 * half)
    context_here = attend(heads_here, seg_key, seg_query).reshape(2, tokens, half)
    context_other = swap_cores(context_here[1])
    first_heads = jnp.where(core == 0, context_here[0], context_other)
    last_heads = jnp.where(core == 0, context_other, context_here[0])
    flat_context = jnp.concatenate([first_heads, last_heads], axis=1)
    attended = dot(flat_context, merge_low) + vectors[4]
    normed_one, inverse_one = normalize(flat_input.astype(wide) + attended)
    first_low = (normed_one * gain_one + vectors[5]).astype(low)
    pre_active = dot(first_low, expand_low) + hidden_full
    active_low = gelu_value(pre_active).astype(low)
    branch_out = dot(active_low, shrink_low) + vectors[6]
    normed_two, inverse_two = normalize(first_low.astype(wide) + branch_out)
    work_output = (normed_two * gain_two + vectors[7]).astype(low).reshape(layer_input.shape)

    upstream = cotangent.reshape(-1, D).astype(wide)
    grad_gain_two = jnp.sum(upstream * normed_two, axis=0)
    grad_shift_two = jnp.sum(upstream, axis=0)
    grad_second = norm_back(upstream * gain_two, normed_two, inverse_two)
    branch_grad = grad_second.astype(low)
    grad_shrink = cross_rows(active_low, branch_grad).astype(low)
    grad_shrink_bias = jnp.sum(branch_grad.astype(wide), axis=0)
    active_grad = (cross_cols(branch_grad, shrink_low) * gelu_slope(pre_active)).astype(low)
    grad_expand = cross_rows(first_low, active_grad).astype(low)
    grad_hidden = jnp.sum(active_grad.astype(wide), axis=0)
    grad_first = grad_second + cross_cols(active_grad, expand_low)
    grad_gain_one = jnp.sum(grad_first * normed_one, axis=0)
    grad_shift_one = jnp.sum(grad_first, axis=0)
    grad_sum_one = norm_back(grad_first * gain_one, normed_one, inverse_one)
    attended_grad = grad_sum_one.astype(low)
    grad_merge = cross_rows(flat_context, attended_grad).astype(low)
    grad_merge_bias = jnp.sum(attended_grad.astype(wide), axis=0)
    context_grad = cross_cols(attended_grad, merge_low).astype(low)

    def own_columns(piece):
        return lax.dynamic_update_slice(jnp.zeros((D,), wide), piece, (core * half,))

    def small_grads(heads_bias_grad):
        if heads_bias_grad is None:
            nothing = jnp.zeros((D,), wide)
            query_bias, value_bias = nothing, nothing
        else:
            query_bias = own_columns(heads_bias_grad[:half])
            value_bias = own_columns(heads_bias_grad[2 * half :])
        found = jnp.stack(
            [
                grad_gain_one,
                grad_gain_two,
                query_bias,
                value_bias,
                grad_merge_bias,
                grad_shift_one,
                grad_shrink_bias,
                grad_shift_two,
            ]
        )
        found = jnp.concatenate([found, grad_hidden.reshape(-1, D)], axis=0)
        return jnp.pad(found, ((0, -found.shape[0] % 8), (0, 0)))

    grad_merge = grad_merge.reshape(block + (rows, D))
    grad_expand = grad_expand.reshape(block + (rows, expand_weight.shape[1]))
    grad_shrink = grad_shrink.reshape(block + (hidden_rows, D))
    if kernels:
        *sums, input_parts = finish_all(
            chips // 4,
            heads_here,
            context_grad.reshape(row_count, length, D),
            seg_key,
            seg_query,
            inputs_both,
            heads_low,
            grad_merge,
            grad_expand,
            grad_shrink,
            small_grads(None),
        )
        input_parts = input_parts.reshape(tokens, D)
    else:
        own = jnp.where(core == 0, context_grad[:, :half], context_grad[:, half:])
        other = swap_cores(jnp.where(core == 0, context_grad[:, half:], context_grad[:, :half]))
        grad_here = jnp.stack([own, other]).reshape(2, row_count, length, half)
        heads_grad = attend_back(heads_here, grad_here, seg_key, seg_query)
        heads_grad = heads_grad.reshape(2 * tokens, 3 * half)
        input_parts = cross_cols(heads_grad, heads_low)
        input_parts = input_parts[:tokens] + swap_cores(input_parts[tokens:].astype(low))
        grad_heads = cross_rows(inputs_both, heads_grad).astype(low)
        small_grad = small_grads(jnp.sum(heads_grad.astype(wide), axis=0))
        grad_heads = grad_heads.reshape(block + (rows, 3 * half))
        sums = scatter_plain(grad_heads, grad_merge, grad_expand, grad_shrink, small_grad)
    work_gradient = (grad_sum_one + input_parts).reshape(layer_input.shape)
    heads_sum, merge_sum, expand_sum, shrink_sum, small_sum, squares = sums
    heads_sum = heads_sum.reshape(2, rows, 3, half)
    heads_sum = heads_sum.transpose(1, 2, 0, 3).reshape(rows, 3 * D)
    vector_sum = lax.dynamic_slice(small_sum, (0, index * rows), (8, rows)).T
    hidden_sum = lax.dynamic_slice(
        small_sum[8 : 8 + hidden_rows * devices // D].reshape(-1), (index * hidden_rows,), (hidden_rows,)
    )
    gradient_norm = jnp.sqrt(jnp.sum(squares) + jnp.sum(small_sum * small_sum))
    factor = jnp.minimum(1.0, clip_limit / gradient_norm)
    reduced = (
        heads_sum,
        merge_sum,
        expand_sum,
        shrink_sum,
        vector_sum[:, 0:2],
        vector_sum[:, 2:8],
        hidden_sum,
    )
    states = (
        (heads_weight, heads_first, heads_second, rate_matrix),
        (merge_weight, merge_first, merge_second, rate_matrix),
        (expand_weight, expand_first, expand_second, rate_matrix),
        (shrink_weight, shrink_first, shrink_second, rate_matrix),
        (norm_gains, gains_first, gains_second, rate_vector),
        (branch_bias, branch_first, branch_second, rate_vector),
        (hidden_bias, hidden_first, hidden_second, rate_vector),
    )
    if kernels:
        matrices = update_all(
            factor, [(reduced[i], *states[i][:3]) for i in range(4)]
        )
    else:
        matrices = []
        for i in range(4):
            found = adamw(*states[i][:3], reduced[i], factor, rate_matrix)
            matrices.append([*found, found[0].astype(low)])
    vectors_new = [adamw(*states[i][:3], reduced[i], factor, rate_vector) for i in range(4, 7)]
    return (
        work_output,
        work_gradient,
        gradient_norm,
        *[value for found in matrices for value in found[:3]],
        *[value for found in vectors_new for value in found],
        *[found[3] for found in matrices],
    )


def solution(mesh):
    matrix, vector = P(("dp", "seq"), None), P(("dp", "seq"))
    tokens = P("dp", "seq", None)
    states = (matrix,) * 18 + (vector,) * 3
    return jax.shard_map(
        functools.partial(per_device, mesh.shape["dp"]),
        mesh=mesh,
        in_specs=(tokens, P("dp", None), tokens) + states,
        out_specs=(tokens, tokens, P()) + states + (matrix,) * 4,
        check_vma=False,
    )
```

```python
import functools

import jax
import jax.numpy as jnp
from jax import lax
from jax.experimental import pallas as pl
from jax.experimental.pallas import tpu as pltpu
from jax.sharding import PartitionSpec as P

D = 768
HEAD_DIM = 64
STEP = 5
LANES = 128
MESH = pl.DeviceIdType.MESH

norm_epsilon = 1e-12
masked_score = -1e30
root_half = 0.7071067811865476
inv_root_tau = 0.3989422804014327
clip_limit = 1.0
decay_first = 0.9
decay_second = 0.999
adam_epsilon = 1e-08
weight_decay = 0.01
rate_matrix = 0.05
rate_vector = 0.5


def place():
    chip, core = lax.axis_index("dp"), lax.axis_index("seq")
    return chip // 4, (chip // 2) % 2, chip % 2, core


def device(z, y, x, core):
    return ((z * 2 + y) * 2 + x, core)


def signal(semaphore, target):
    pl.semaphore_signal(semaphore, inc=1, device_id=target, device_id_type=MESH)


def greet(layers, others=()):
    z, y, x, core = place()
    barrier = pltpu.get_barrier_semaphore()
    across = (device(z, y, x, 1 - core), device(z, y, 1 - x, core), device(z, 1 - y, x, core))
    for target in across + tuple(others):
        signal(barrier, target)

    @pl.when(z > 0)
    def _():
        signal(barrier, device(z - 1, y, x, core))

    @pl.when(z < layers - 1)
    def _():
        signal(barrier, device(z + 1, y, x, core))

    beside = jnp.where(z > 0, 1, 0) + jnp.where(z < layers - 1, 1, 0)
    pl.semaphore_wait(barrier, 3 + len(others) + beside)


def others_of(layers):
    z, y, x, core = place()
    line = [device((z + step) % layers, y, x, core) for step in range(1, layers)]
    plane = [
        device(
            z,
            1 - y if bits & 4 else y,
            1 - x if bits & 2 else x,
            1 - core if bits & 1 else core,
        )
        for bits in range(1, 8)
    ]
    return line, plane


def greet_line_and_plane(layers):
    barrier = pltpu.get_barrier_semaphore()
    line, plane = others_of(layers)
    for target in line + plane:
        signal(barrier, target)
    pl.semaphore_wait(barrier, len(line) + len(plane))


class Summed:
    def __init__(self, layers, line, plane, line_send, line_recv, plane_send, plane_recv):
        z, y, x, core = place()
        self.rooms = (line, plane)
        self.sems = ((line_send, line_recv), (plane_send, plane_recv))
        self.others = others_of(layers)
        at = y * 4 + x * 2 + core
        self.own = (z, at)
        self.sources = (
            [(z + layers - step) % layers for step in range(1, layers)],
            [
                (1 - y if bits & 4 else y) * 4
                + (1 - x if bits & 2 else x) * 2
                + (1 - core if bits & 1 else core)
                for bits in range(1, 8)
            ],
        )

    def copy(self, stage, which, slot):
        here = self.rooms[stage].at[slot]
        send, recv = self.sems[stage]
        return remote(here, here, send.at[which], recv.at[which], self.others[stage][which])

    def start(self, stage, value):
        self.rooms[stage][self.own[stage]] = value
        for which in range(len(self.others[stage])):
            self.copy(stage, which, self.own[stage]).start()

    def finish(self, stage):
        for which, slot in enumerate(self.sources[stage]):
            self.copy(stage, which, slot).wait_recv()
        room = self.rooms[stage]
        total = room[0]
        for slot in range(1, room.shape[0]):
            total = total + room[slot]
        return total

    def settle(self):
        for stage in range(2):
            for which in range(len(self.others[stage])):
                self.copy(stage, which, self.own[stage]).wait_send()


def remote(source, target, sent, received, to):
    return pltpu.make_async_remote_copy(
        src_ref=source,
        dst_ref=target,
        send_sem=sent,
        recv_sem=received,
        device_id=to,
        device_id_type=MESH,
    )


GATHERED = (
    ("heads", 0, 768, False),
    ("merge", 0, 768, True),
    ("small", 0, 128, True),
    ("heads", 768, 384, True),
    ("shrink", 0, 768, False),
    ("expand", 0, 3072, True),
)


def gather_kernel(
    layers,
    heads_in,
    merge_in,
    expand_in,
    shrink_in,
    small_in,
    tokens_in,
    heads_all,
    merge_all,
    expand_all,
    shrink_all,
    small_all,
    tokens_all,
    heads_block,
    token_room,
    pair_send,
    pair_recv,
    own_sem,
    line_send,
    line_recv,
    first_send,
    first_recv,
    second_send,
    second_recv,
    core_send,
    core_recv,
):
    z, y, x, core = place()
    partner = device(z, y, x, 1 - core)
    own = {"merge": merge_in, "expand": expand_in, "shrink": shrink_in, "small": small_in}
    full = {
        "merge": merge_all,
        "expand": expand_all,
        "shrink": shrink_all,
        "small": small_all,
        "heads": heads_all,
    }
    greet(layers)

    heads_out = remote(
        heads_in.at[1 - core], heads_block.at[core], pair_send.at[0], pair_recv.at[0], partner
    )
    heads_out.start()
    heads_keep = pltpu.make_async_copy(heads_in.at[core], heads_block.at[core], own_sem.at[0])
    heads_keep.start()
    tokens_load = pltpu.make_async_copy(tokens_in, token_room, own_sem.at[1])
    tokens_load.start()

    def own_block(piece):
        name, start, width, _ = GATHERED[piece]
        if name == "heads":
            return heads_block.at[:, :, pl.ds(start, width)]
        return own[name]

    def block(piece, zz, yy, xx, plane):
        name, start, width, _ = GATHERED[piece]
        if name == "heads":
            return full[name].at[zz, yy, xx, :, :, pl.ds(start, width)]
        return full[name].at[zz, yy, xx, plane]

    def couple(piece, zz, plane, moved):
        name, start, width, y_first = GATHERED[piece]
        yy = y if y_first or not moved else 1 - y
        xx = x if not y_first or not moved else 1 - x
        if name == "heads":
            if y_first:
                return full[name].at[zz, :, xx, :, :, pl.ds(start, width)]
            return full[name].at[zz, yy, :, :, :, pl.ds(start, width)]
        if y_first:
            return full[name].at[zz, :, xx, plane]
        return full[name].at[zz, yy, :, plane]

    def across(piece, second):
        y_turn = GATHERED[piece][3] != second
        return device(z, 1 - y, x, core) if y_turn else device(z, y, 1 - x, core)

    def first_block(piece, zz):
        if GATHERED[piece][3]:
            return (zz, 1 - y, x)
        return (zz, y, 1 - x)

    def line_copy(piece, zz, source, target_z):
        return remote(
            source,
            block(piece, zz, y, x, core),
            line_send.at[piece, zz, jnp.where(target_z > z, 0, 1)],
            line_recv.at[piece, zz],
            device(target_z, y, x, core),
        )

    def first_copy(piece, zz, source):
        return remote(
            source,
            block(piece, zz, y, x, core),
            first_send.at[piece, zz],
            first_recv.at[piece, zz],
            across(piece, False),
        )

    def second_copy(piece, zz):
        both = couple(piece, zz, core, False)
        return remote(
            both, both, second_send.at[piece, zz], second_recv.at[piece, zz], across(piece, True)
        )

    def core_copy(piece, zz, stage, source, target):
        return remote(
            source,
            target,
            core_send.at[piece, zz, stage],
            core_recv.at[piece, zz, stage],
            partner,
        )

    def shared(piece):
        return GATHERED[piece][0] != "heads"

    pieces = range(len(GATHERED))
    order = sorted(pieces, key=lambda piece: (GATHERED[piece][0] == "heads", piece))

    def begin(piece):
        mine = own_block(piece)

        @pl.when(z < layers - 1)
        def _():
            line_copy(piece, z, mine, z + 1).start()

        @pl.when(z > 0)
        def _():
            line_copy(piece, z, mine, z - 1).start()

        first_copy(piece, z, mine).start()
        if shared(piece):
            core_copy(piece, z, 0, mine, block(piece, z, y, x, core)).start()
        pltpu.make_async_copy(
            mine, block(piece, z, y, x, core), own_sem.at[2 + piece]
        ).start()

    for piece in order:
        if piece == order[-2]:
            heads_out.wait_recv()
            heads_keep.wait()
        begin(piece)
    tokens_load.wait()
    tokens_out = remote(
        token_room, tokens_all.at[1], pair_send.at[1], pair_recv.at[1], partner
    )
    tokens_out.start()
    tokens_keep = pltpu.make_async_copy(token_room, tokens_all.at[0], own_sem.at[1])
    tokens_keep.start()
    for piece in order:
        pltpu.make_async_copy(
            own_block(piece), block(piece, z, y, x, core), own_sem.at[2 + piece]
        ).wait()

    def arrive_line(piece, zz, below):
        here = block(piece, zz, y, x, core)
        line_copy(piece, zz, here, z).wait_recv()
        if below:

            @pl.when(z < layers - 1)
            def _():
                line_copy(piece, zz, here, z + 1).start()

        else:

            @pl.when(z > 0)
            def _():
                line_copy(piece, zz, here, z - 1).start()

        first_copy(piece, zz, here).start()
        if shared(piece):
            core_copy(piece, zz, 0, here, here).start()

    def arrive_first(piece, zz):
        here = block(piece, *first_block(piece, zz), core)
        remote(
            here, here, first_send.at[piece, zz], first_recv.at[piece, zz], across(piece, False)
        ).wait_recv()
        second_copy(piece, zz).start()
        if shared(piece):
            core_copy(piece, zz, 1, here, here).start()

    def arrive_second(piece, zz):
        here = couple(piece, zz, core, True)
        remote(
            here, here, second_send.at[piece, zz], second_recv.at[piece, zz], across(piece, True)
        ).wait_recv()
        if shared(piece):
            core_copy(piece, zz, 2, here, here).start()

    def each(distance, action):
        if distance == 0:
            action(z, None)
            return

        @pl.when(z - distance >= 0)
        def _():
            action(z - distance, True)

        @pl.when(z + distance < layers)
        def _():
            action(z + distance, False)

    for step in range(layers + 2):
        for piece in pieces:
            if 0 < step < layers:
                each(step, lambda zz, below, piece=piece: arrive_line(piece, zz, below))
            if 0 <= step - 1 < layers:
                each(step - 1, lambda zz, below, piece=piece: arrive_first(piece, zz))
            if 0 <= step - 2 < layers:
                each(step - 2, lambda zz, below, piece=piece: arrive_second(piece, zz))

    heads_out.wait_send()
    tokens_out.wait_send()
    remote(
        token_room, tokens_all.at[1], pair_send.at[1], pair_recv.at[1], partner
    ).wait_recv()
    tokens_keep.wait()
    other = 1 - core
    for piece in pieces:
        for zz in range(layers):
            mine = block(piece, zz, y, x, core)
            theirs = block(piece, zz, y, x, other)
            crossed = block(piece, *first_block(piece, zz), other)
            first_copy(piece, zz, mine).wait_send()
            second_copy(piece, zz).wait_send()
            if shared(piece):
                core_copy(piece, zz, 0, mine, theirs).wait()
                core_copy(piece, zz, 1, mine, crossed).wait()
                both = couple(piece, zz, other, True)
                core_copy(piece, zz, 2, both, both).wait()

            @pl.when(jnp.logical_and(z < layers - 1, zz <= z))
            def _(piece=piece, zz=zz, mine=mine):
                line_copy(piece, zz, mine, z + 1).wait_send()

            @pl.when(jnp.logical_and(z > 0, zz >= z))
            def _(piece=piece, zz=zz, mine=mine):
                line_copy(piece, zz, mine, z - 1).wait_send()


def gather_all(layers, heads, merge, expand, shrink, small, tokens):
    chips = (layers, 2, 2, 2)
    low = jnp.bfloat16
    count = len(GATHERED)
    sems = pltpu.SemaphoreType.DMA
    inputs = (heads, merge, expand, shrink, small)
    return pl.pallas_call(
        functools.partial(gather_kernel, layers),
        out_shape=[
            jax.ShapeDtypeStruct(chips + heads.shape[1:], low),
            *[jax.ShapeDtypeStruct(chips + part.shape, low) for part in inputs[1:]],
            jax.ShapeDtypeStruct((2,) + tokens.shape, low),
        ],
        in_specs=[pl.BlockSpec(memory_space=pltpu.VMEM)] * 5 + [pl.BlockSpec(memory_space=pl.ANY)],
        out_specs=[pl.BlockSpec(memory_space=pl.ANY)] * 6,
        scratch_shapes=[
            pltpu.VMEM(heads.shape, low),
            pltpu.VMEM(tokens.shape, low),
            sems((2,)),
            sems((2,)),
            sems((2 + count,)),
            sems((count, layers, 2)),
            sems((count, layers)),
            sems((count, layers)),
            sems((count, layers)),
            sems((count, layers)),
            sems((count, layers)),
            sems((count, layers, 3)),
            sems((count, layers, 3)),
        ],
        compiler_params=pltpu.CompilerParams(collective_id=0, has_side_effects=True),
        name="gather_all",
    )(*inputs, tokens)


SCATTERED = (
    ("shrink", 0, 768, False),
    ("expand", 0, 3072, True),
    ("merge", 0, 768, True),
    ("heads", 0, 768, False),
    ("heads", 768, 384, True),
)


def finish_kernel(
    layers,
    heads_ref,
    upstream_ref,
    seg_key,
    seg_query,
    inputs_ref,
    weight_ref,
    merge_in,
    expand_in,
    shrink_in,
    small_in,
    heads_out,
    merge_out,
    expand_out,
    shrink_out,
    small_out,
    square_out,
    tokens_out,
    heads_here,
    upstream_here,
    heads_grad,
    inputs_here,
    weight_here,
    bias,
    tokens_sent,
    tokens_room,
    totals,
    core_rooms,
    first_rooms,
    second_rooms,
    line_rooms,
    heads_last,
    heads_room,
    small_line,
    small_plane,
    square_line,
    square_plane,
    bring_sem,
    upstream_send,
    upstream_recv,
    tokens_send,
    tokens_recv,
    load_sem,
    core_send,
    core_recv,
    first_send,
    first_recv,
    second_send,
    second_recv,
    line_send,
    line_recv,
    last_send,
    last_recv,
    small_sems,
    square_sems,
):
    z, y, x, core = place()
    partner = device(z, y, x, 1 - core)
    sources = {"merge": merge_in, "expand": expand_in, "shrink": shrink_in}
    results = {"merge": merge_out, "expand": expand_out, "shrink": shrink_out}
    small_sum = Summed(layers, small_line, small_plane, *small_sems)
    square_sum = Summed(layers, square_line, square_plane, *square_sems)
    low, wide = jnp.bfloat16, jnp.float32
    _, rows, length, columns = heads_here.shape
    width = columns // 3
    pairs = width // LANES

    def bring_row(row):
        return pltpu.make_async_copy(heads_ref.at[:, row], heads_here.at[:, row], bring_sem.at[row])

    def columns_of(plane):
        return pl.ds(pl.multiple_of(plane * width, LANES), width)

    def upstream_keep(row):
        return pltpu.make_async_copy(
            upstream_ref.at[row, :, columns_of(core)], upstream_here.at[0, row], bring_sem.at[4 + row]
        )

    def upstream_copy(row):
        return remote(
            upstream_ref.at[row, :, columns_of(1 - core)],
            upstream_here.at[1, row],
            upstream_send.at[row],
            upstream_recv.at[row],
            partner,
        )

    bring_inputs = pltpu.make_async_copy(inputs_ref, inputs_here, bring_sem.at[8])
    bring_weight = pltpu.make_async_copy(weight_ref, weight_here, bring_sem.at[9])
    for row in range(rows):
        bring_row(row).start()
        upstream_keep(row).start()

    greet_line_and_plane(layers)
    for row in range(rows):
        upstream_copy(row).start()

    pieces = range(len(SCATTERED))
    early = [piece for piece in pieces if SCATTERED[piece][0] != "heads"]
    late = [piece for piece in pieces if SCATTERED[piece][0] == "heads"]

    def is_heads(piece):
        return SCATTERED[piece][0] == "heads"

    def y_first(piece):
        return SCATTERED[piece][3]

    def load(piece, zz):
        return pltpu.make_async_copy(
            sources[SCATTERED[piece][0]].at[zz, :, :, core], totals[piece].at[zz], load_sem.at[piece, zz]
        )

    def core_copy(piece, zz):
        return remote(
            sources[SCATTERED[piece][0]].at[zz, :, :, 1 - core],
            core_rooms[piece].at[zz],
            core_send.at[piece, zz],
            core_recv.at[piece, zz],
            partner,
        )

    def first_copy(piece, zz):
        if y_first(piece):
            source, to = totals[piece].at[zz, 1 - y], device(z, 1 - y, x, core)
        else:
            source, to = totals[piece].at[zz, :, 1 - x], device(z, y, 1 - x, core)
        return remote(
            source, first_rooms[piece].at[zz], first_send.at[piece, zz], first_recv.at[piece, zz], to
        )

    def second_copy(piece, zz):
        if y_first(piece):
            source, to = totals[piece].at[zz, y, 1 - x], device(z, y, 1 - x, core)
        else:
            source, to = totals[piece].at[zz, 1 - y, x], device(z, 1 - y, x, core)
        return remote(
            source,
            second_rooms[piece].at[zz],
            second_send.at[piece, zz],
            second_recv.at[piece, zz],
            to,
        )

    def line_copy(piece, zz, downward):
        to = z - 1 if downward else z + 1
        return remote(
            totals[piece].at[zz, y, x],
            line_rooms[piece].at[downward, zz],
            line_send.at[piece, zz],
            line_recv.at[piece, downward, zz],
            device(to, y, x, core),
        )

    def add(target, room):
        target[...] = (target[...].astype(wide) + room[...].astype(wide)).astype(low)

    def layer_of(step):
        upward = jnp.where(z < layers // 2, 1, 0)
        turned = jnp.where(jnp.logical_and(step >= 2, jnp.logical_or(z == 1, z == 2)), 5 - step, step)
        return jnp.where(upward == 1, layers - 1 - turned, turned)

    def on_first(piece, zz):
        if not is_heads(piece):
            load(piece, zz).wait()
            core_copy(piece, zz).wait_recv()

            def merge_one(index, carry):
                add(
                    totals[piece].at[zz, index // 2, index % 2],
                    core_rooms[piece].at[zz, index // 2, index % 2],
                )
                return carry

            lax.fori_loop(0, 4, merge_one, 0)
        first_copy(piece, zz).start()

    def on_second(piece, zz):
        first_copy(piece, zz).wait_recv()

        def merge_one(index, carry):
            if y_first(piece):
                target = totals[piece].at[zz, y, index]
            else:
                target = totals[piece].at[zz, index, x]
            add(target, first_rooms[piece].at[zz, index])
            return carry

        lax.fori_loop(0, 2, merge_one, 0)
        second_copy(piece, zz).start()

    def on_line(piece, zz):
        second_copy(piece, zz).wait_recv()
        mine = totals[piece].at[zz, y, x]
        add(mine, second_rooms[piece].at[zz])

        @pl.when(zz > z)
        def _():
            @pl.when(z > 0)
            def _():
                line_copy(piece, zz, 0).wait_recv()
                add(mine, line_rooms[piece].at[0, zz])

            line_copy(piece, zz, 0).start()

        @pl.when(zz < z)
        def _():
            @pl.when(z < layers - 1)
            def _():
                line_copy(piece, zz, 1).wait_recv()
                add(mine, line_rooms[piece].at[1, zz])

            line_copy(piece, zz, 1).start()

    def start_early(step, carry):
        for piece in early:
            core_copy(piece, layer_of(step)).start()
            load(piece, layer_of(step)).start()
        return carry

    lax.fori_loop(0, layers, start_early, 0)
    bring_inputs.start()
    bring_weight.start()

    scale = HEAD_DIM**-0.5

    def attention_step(step, carry):
        row, pair = step // pairs, step % pairs

        @pl.when(pair == 0)
        def _():
            bring_row(row).wait()
            upstream_keep(row).wait()
            upstream_copy(row).wait_recv()
            bias[...] = jnp.where(seg_key[row] == seg_query[row], 0.0, masked_score)

        def part(which):
            start = pl.multiple_of(which * width + pair * LANES, LANES)
            return heads_here[:, row, :, pl.ds(start, LANES)].reshape(2 * length, LANES)

        at = pl.multiple_of(pair * LANES, LANES)
        upstream = upstream_here[:, row, :, pl.ds(at, LANES)].reshape(2 * length, LANES)
        grads = pair_back(part(0), part(1), part(2), upstream, bias)
        for which in range(3):
            start = pl.multiple_of(which * width + pair * LANES, LANES)
            heads_grad[:, row, :, pl.ds(start, LANES)] = grads[which].reshape(2, length, LANES)

        @pl.when(jnp.logical_and(step >= 4, step % 3 == 1))
        def _():
            for piece in early:
                on_second(piece, layer_of((step - 4) // 3))

        @pl.when(jnp.logical_or(step == 0, jnp.logical_and(step < 9, step % 3 == 1)))
        def _():
            for piece in early:
                on_first(piece, layer_of((step + 2) // 3))

        @pl.when(jnp.logical_or(step == 9, step == 11))
        def _():
            for piece in early:
                on_line(piece, layer_of((step - 9) // 2))

        return carry

    lax.fori_loop(0, rows * pairs, attention_step, 0)

    bring_inputs.wait()
    flat_grad = heads_grad[...].reshape(2 * rows * length, columns)
    ones = jnp.ones((8, 2 * rows * length), low)
    sums = dot(ones, flat_grad)
    small_out[...] = small_in[...]
    small_out[2:3, columns_of(core)] = sums[0:1, 0:width]
    small_out[3:4, columns_of(core)] = sums[0:1, 2 * width : 3 * width]
    small_sum.start(0, small_out[...])
    depth = inputs_here.shape[1] // 2

    def weight_step(turn, carry):
        step = jnp.where(z < layers // 2, 1 - turn, turn)
        start = pl.multiple_of(step * depth, LANES)
        found = dot(inputs_here[:, pl.ds(start, depth)], flat_grad, (((0,), (0,)), ((), ())))
        for piece in late:
            _, first, wide_by, _ = SCATTERED[piece]
            block = found[:, first : first + wide_by]
            block = block.reshape((layers // 2,) + totals[piece].shape[1:]).astype(low)
            totals[piece][pl.ds(step * (layers // 2), layers // 2)] = block

        @pl.when(turn == 0)
        def _():
            for piece in early:
                on_second(piece, layer_of(layers - 1))

        for which in range(layers // 2):
            for piece in late:
                on_first(piece, layer_of(turn * (layers // 2) + which))
        return carry

    lax.fori_loop(0, 2, weight_step, 0)

    bring_weight.wait()

    def tokens_copy(row):
        return remote(
            tokens_sent.at[row], tokens_room.at[row], tokens_send.at[row], tokens_recv.at[row], partner
        )

    def other_step(row, carry):
        tokens_sent[row] = dot(heads_grad[1, row], weight_here[...], FAR).astype(low)
        tokens_copy(row).start()

        @pl.when(row >= 1)
        def _():
            for piece in late:
                on_second(piece, layer_of(row - 1))

        @pl.when(row % 2 == 0)
        def _():
            for piece in early:
                on_line(piece, layer_of(2 + row // 2))

        @pl.when(row == 2)
        def _():
            small_sum.start(1, small_sum.finish(0))

        return carry

    def own_step(row, carry):
        found = dot(heads_grad[0, row], weight_here[...], FAR)
        tokens_copy(row).wait_recv()
        tokens_out[row] = found + tokens_room[row].astype(wide)

        @pl.when(row == 0)
        def _():
            for piece in late:
                on_second(piece, layer_of(layers - 1))

        for piece in late:
            on_line(piece, layer_of(row))
        return carry

    lax.fori_loop(0, rows, other_step, 0)
    lax.fori_loop(0, rows, own_step, 0)
    small_out[...] = small_sum.finish(1)

    def squares(value):
        by_row = jnp.sum((value * value).reshape(value.shape[0] // 8, 8, value.shape[1]), axis=0)
        total = by_row[:, 0:LANES]
        for start in range(LANES, value.shape[1], LANES):
            total = total + by_row[:, start : start + LANES]
        return total

    def last_copy(piece):
        _, start, wide_by, _ = SCATTERED[piece]
        return remote(
            heads_last.at[:, pl.ds(start, wide_by)],
            heads_room.at[:, pl.ds(start, wide_by)],
            last_send.at[piece],
            last_recv.at[piece],
            partner,
        )

    found_squares = jnp.zeros((8, LANES), wide)
    for piece in early + late:
        name, start, wide_by, _ = SCATTERED[piece]
        mine = totals[piece].at[z, y, x]

        @pl.when(z > 0)
        def _(piece=piece, mine=mine):
            line_copy(piece, z, 0).wait_recv()
            add(mine, line_rooms[piece].at[0, z])

        @pl.when(z < layers - 1)
        def _(piece=piece, mine=mine):
            line_copy(piece, z, 1).wait_recv()
            add(mine, line_rooms[piece].at[1, z])

        if is_heads(piece):
            heads_last[:, start : start + wide_by] = mine[1 - core]
            last_copy(piece).start()
            kept = mine[core].astype(wide)
            heads_out[core, :, start : start + wide_by] = kept
        else:
            kept = mine[...].astype(wide)
            results[name][...] = kept
        found_squares = found_squares + squares(kept)
    for piece in late:
        _, start, wide_by, _ = SCATTERED[piece]
        last_copy(piece).wait_recv()
        theirs = heads_room[:, start : start + wide_by].astype(wide)
        heads_out[1 - core, :, start : start + wide_by] = theirs
        found_squares = found_squares + squares(theirs)

    square_sum.start(0, found_squares)
    square_sum.start(1, square_sum.finish(0))
    square_out[...] = square_sum.finish(1)

    small_sum.settle()
    square_sum.settle()
    for row in range(rows):
        upstream_copy(row).wait_send()
        tokens_copy(row).wait_send()

    def settle(zz, carry):
        for piece in pieces:
            if not is_heads(piece):
                core_copy(piece, zz).wait_send()
            first_copy(piece, zz).wait_send()
            second_copy(piece, zz).wait_send()

            @pl.when(zz > z)
            def _(piece=piece):
                line_copy(piece, zz, 0).wait_send()

            @pl.when(zz < z)
            def _(piece=piece):
                line_copy(piece, zz, 1).wait_send()

        return carry

    lax.fori_loop(0, layers, settle, 0)
    for piece in late:
        last_copy(piece).wait_send()


def finish_all(layers, heads, upstream, seg_key, seg_query, inputs, weight, merge, expand, shrink, small):
    low, wide = jnp.bfloat16, jnp.float32
    block_rows = merge.shape[4]
    _, rows, length, columns = heads.shape
    width = columns // 3
    sums_rows = {"merge": block_rows, "expand": block_rows, "shrink": shrink.shape[4]}
    sems = pltpu.SemaphoreType.DMA

    def rooms(*lead, some=SCATTERED):
        return [
            pltpu.VMEM(
                tuple(lead)
                + ((2, block_rows, wide_by) if name == "heads" else (sums_rows[name], wide_by)),
                low,
            )
            for name, _, wide_by, _ in some
        ]

    count = len(SCATTERED)
    early = [piece for piece in SCATTERED if piece[0] != "heads"]
    vmem, anywhere = pl.BlockSpec(memory_space=pltpu.VMEM), pl.BlockSpec(memory_space=pl.ANY)
    return pl.pallas_call(
        functools.partial(finish_kernel, layers),
        out_shape=[
            jax.ShapeDtypeStruct((2, block_rows, columns), wide),
            *[jax.ShapeDtypeStruct(part.shape[4:], wide) for part in (merge, expand, shrink)],
            jax.ShapeDtypeStruct(small.shape, wide),
            jax.ShapeDtypeStruct((8, LANES), wide),
            jax.ShapeDtypeStruct((rows, length, inputs.shape[1]), wide),
        ],
        in_specs=[anywhere, anywhere, vmem, vmem] + [anywhere] * 5 + [vmem],
        out_specs=[vmem] * 7,
        scratch_shapes=[
            pltpu.VMEM(heads.shape, low),
            pltpu.VMEM((2, rows, length, width), low),
            pltpu.VMEM(heads.shape, low),
            pltpu.VMEM(inputs.shape, low),
            pltpu.VMEM(weight.shape, low),
            pltpu.VMEM((2 * length, 2 * length), wide),
            pltpu.VMEM((rows, length, inputs.shape[1]), low),
            pltpu.VMEM((rows, length, inputs.shape[1]), low),
            rooms(layers, 2, 2),
            rooms(layers, 2, 2, some=early),
            rooms(layers, 2),
            rooms(layers),
            rooms(2, layers),
            pltpu.VMEM((block_rows, columns), low),
            pltpu.VMEM((block_rows, columns), low),
            pltpu.VMEM((layers,) + small.shape, wide),
            pltpu.VMEM((8,) + small.shape, wide),
            pltpu.VMEM((layers, 8, LANES), wide),
            pltpu.VMEM((8, 8, LANES), wide),
            sems((10,)),
            sems((rows,)),
            sems((rows,)),
            sems((rows,)),
            sems((rows,)),
            sems((count, layers)),
            sems((count, layers)),
            sems((count, layers)),
            sems((count, layers)),
            sems((count, layers)),
            sems((count, layers)),
            sems((count, layers)),
            sems((count, layers)),
            sems((count, 2, layers)),
            sems((count,)),
            sems((count,)),
            [sems((layers - 1,)), sems((layers - 1,)), sems((7,)), sems((7,))],
            [sems((layers - 1,)), sems((layers - 1,)), sems((7,)), sems((7,))],
        ],
        compiler_params=pltpu.CompilerParams(
            collective_id=1, has_side_effects=True, vmem_limit_bytes=63 * 2**20
        ),
        name="finish_all",
    )(heads, upstream, seg_key, seg_query, inputs, weight, merge, expand, shrink, small)


def update_kernel(squares, small, *refs):
    count = len(refs) // 8
    total = jnp.sum(squares[...], keepdims=True) + jnp.sum(small[...] * small[...], keepdims=True)
    norm = jnp.sqrt(total)
    factor = jnp.minimum(1.0, clip_limit / norm)
    refs[-1][...] = norm
    for which in range(count):
        gradient, weight, moment, square = (refs[which * 4 + i] for i in range(4))
        outs = refs[count * 4 + which * 4 : count * 4 + which * 4 + 4]
        half = weight.shape[1] // 6
        if len(gradient.shape) == 3:
            spans = [
                (slice((part * 2 + core) * half, (part * 2 + core + 1) * half), part, core)
                for part in range(3)
                for core in range(2)
            ]
        else:
            spans = [(slice(0, weight.shape[1]), None, None)]
        for span, part, core in spans:
            if part is None:
                slope = gradient[...]
            else:
                slope = gradient[core, :, part * half : (part + 1) * half]
            updated, first, second = adamw(
                weight[:, span], moment[:, span], square[:, span], slope, factor, rate_matrix
            )
            outs[0][:, span] = updated
            outs[1][:, span] = first
            outs[2][:, span] = second
            outs[3][:, span] = updated.astype(jnp.bfloat16)


def update_all(squares, small, states):
    whole = pl.BlockSpec(memory_space=pltpu.VMEM)
    flat = [part for state in states for part in state]
    shapes = []
    for state in states:
        shapes += [jax.ShapeDtypeStruct(state[1].shape, jnp.float32)] * 3
        shapes += [jax.ShapeDtypeStruct(state[1].shape, jnp.bfloat16)]
    shapes.append(jax.ShapeDtypeStruct((1, 1), jnp.float32))
    found = pl.pallas_call(
        update_kernel,
        out_shape=shapes,
        in_specs=[whole] * (2 + len(flat)),
        out_specs=[whole] * len(shapes),
        name="update_all",
    )(squares, small, *flat)
    return [found[4 * which : 4 * which + 4] for which in range(len(states))], found[-1][0, 0]


FAR = (((1,), (1,)), ((), ()))
NEAR = (((1,), (0,)), ((), ()))


def dot(left, right, dims=NEAR):
    return lax.dot_general(left, right, dims, preferred_element_type=jnp.float32)


def write_bias(bias, seg_key, seg_query):
    @pl.when(pl.program_id(1) == 0)
    def _():
        bias[...] = jnp.where(seg_key[0] == seg_query[0], 0.0, masked_score)


def both_halves(ref):
    halves, rows, length, lanes = ref.shape
    return ref[...].reshape(halves * rows * length, lanes)


def only_head(head, value):
    lane = lax.broadcasted_iota(jnp.int32, value.shape, 1)
    return jnp.where((lane // HEAD_DIM) == head, value, jnp.zeros_like(value))


def softmax_of(keys, query, bias):
    scores = dot(keys, query, FAR) + bias[...]
    unscaled = jnp.exp(scores - jnp.max(scores, axis=0, keepdims=True))
    return unscaled * (1.0 / jnp.sum(unscaled, axis=0, keepdims=True))


def attend_kernel(query_ref, key_ref, value_ref, seg_key, seg_query, out_ref, bias):
    write_bias(bias, seg_key, seg_query)
    query = both_halves(query_ref) * jnp.asarray(HEAD_DIM**-0.5, jnp.bfloat16)
    keys = both_halves(key_ref)
    values = both_halves(value_ref).T
    found = []
    for head in range(2):
        weights = softmax_of(keys, only_head(head, query), bias).astype(jnp.bfloat16)
        found.append(dot(values[head * HEAD_DIM : (head + 1) * HEAD_DIM], weights))
    context = jnp.concatenate(found, axis=0).T.astype(jnp.bfloat16)
    out_ref[...] = context.reshape(out_ref.shape)


def pair_back(query, keys, values, upstream, bias):
    scale = HEAD_DIM**-0.5
    query = query * jnp.asarray(scale, jnp.bfloat16)
    flipped = keys.T
    found_query, found_key, found_value = [], [], []
    for head in range(2):
        weights = softmax_of(keys, only_head(head, query), bias)
        grad_weights = dot(only_head(head, values), upstream, FAR)
        inner = jnp.sum(weights * grad_weights, axis=0, keepdims=True)
        grad_scores = (weights * (grad_weights - inner)).astype(jnp.bfloat16)
        found_value.append(dot(weights.astype(jnp.bfloat16), upstream))
        found_key.append(dot(grad_scores, query))
        found_query.append(dot(flipped[head * HEAD_DIM : (head + 1) * HEAD_DIM], grad_scores))
    lane = lax.broadcasted_iota(jnp.int32, found_key[0].shape, 1)
    return (
        (jnp.concatenate(found_query, axis=0).T * scale).astype(jnp.bfloat16),
        jnp.where(lane < HEAD_DIM, found_key[0], found_key[1]).astype(jnp.bfloat16),
        jnp.where(lane < HEAD_DIM, found_value[0], found_value[1]).astype(jnp.bfloat16),
    )


def attend_back_kernel(
    query_ref, key_ref, value_ref, upstream_ref, seg_key, seg_query, out_ref, bias
):
    write_bias(bias, seg_key, seg_query)
    refs = (query_ref, key_ref, value_ref, upstream_ref)
    grads = pair_back(*[both_halves(ref) for ref in refs], bias)
    width = out_ref.shape[3] // 3
    for which in range(3):
        start = pl.multiple_of(pl.program_id(1) * LANES + which * width, LANES)
        out_ref[:, :, :, pl.ds(start, LANES)] = grads[which].reshape(query_ref.shape)


def head_block(length, first):
    return pl.BlockSpec((2, 1, length, LANES), lambda row, pair: (0, row, 0, first + pair))


def attention_specs(rows, length):
    return [
        pl.BlockSpec((1, 2 * length, 1), lambda row, pair: (row, 0, 0)),
        pl.BlockSpec((1, 1, 2 * length), lambda row, pair: (row, 0, 0)),
    ]


def attend(heads, seg_key, seg_query):
    _, rows, length, columns = heads.shape
    width = columns // 3
    pairs = width // LANES
    flops = 4 * rows * width * (2 * length) ** 2
    return pl.pallas_call(
        attend_kernel,
        grid=(rows, pairs),
        out_shape=jax.ShapeDtypeStruct((2, rows, length, width), jnp.bfloat16),
        in_specs=[
            head_block(length, 0),
            head_block(length, pairs),
            head_block(length, 2 * pairs),
            *attention_specs(rows, length),
        ],
        out_specs=head_block(length, 0),
        scratch_shapes=[pltpu.VMEM((2 * length, 2 * length), jnp.float32)],
        cost_estimate=pl.CostEstimate(
            flops=flops, bytes_accessed=8 * heads.size // 3, transcendentals=flops // 256
        ),
        name="attend",
    )(heads, heads, heads, seg_key, seg_query)


def attend_back(heads, upstream, seg_key, seg_query):
    _, rows, length, columns = heads.shape
    width = columns // 3
    pairs = width // LANES
    flops = 10 * rows * width * (2 * length) ** 2
    return pl.pallas_call(
        attend_back_kernel,
        grid=(rows, pairs),
        out_shape=jax.ShapeDtypeStruct(heads.shape, jnp.bfloat16),
        in_specs=[
            head_block(length, 0),
            head_block(length, pairs),
            head_block(length, 2 * pairs),
            head_block(length, 0),
            *attention_specs(rows, length),
        ],
        out_specs=pl.BlockSpec((2, 1, length, columns), lambda row, pair: (0, row, 0, 0)),
        scratch_shapes=[pltpu.VMEM((2 * length, 2 * length), jnp.float32)],
        cost_estimate=pl.CostEstimate(
            flops=flops, bytes_accessed=14 * heads.size // 3, transcendentals=flops // 640
        ),
        name="attend_back",
    )(heads, heads, heads, upstream, seg_key, seg_query)


def normalize(hidden):
    center = hidden - jnp.mean(hidden, axis=-1, keepdims=True)
    inverse_scale = lax.rsqrt(jnp.mean(center * center, axis=-1, keepdims=True) + norm_epsilon)
    return (center * inverse_scale, inverse_scale)


def norm_back(upstream, normed, inverse_scale):
    mean_upstream = jnp.mean(upstream, axis=-1, keepdims=True)
    mean_cross = jnp.mean(upstream * normed, axis=-1, keepdims=True)
    return inverse_scale * (upstream - mean_upstream - normed * mean_cross)


def gelu_value(inputs):
    return 0.5 * inputs * (1.0 + lax.erf(inputs * root_half))


def gelu_slope(inputs):
    return (
        0.5 * (1.0 + lax.erf(inputs * root_half))
        + inputs * jnp.exp(-0.5 * inputs * inputs) * inv_root_tau
    )


def cross_rows(operand_left, operand_right):
    return lax.dot_general(
        operand_left, operand_right, (((0,), (0,)), ((), ())), preferred_element_type=jnp.float32
    )


def cross_cols(operand_left, operand_right):
    return dot(operand_left, operand_right, FAR)


def adamw(weight, moment, square, gradient, factor, step_rate):
    clipped = gradient * factor
    moment_new = decay_first * moment + (1.0 - decay_first) * clipped
    square_new = decay_second * square + (1.0 - decay_second) * clipped * clipped
    corrected = (
        moment_new
        / (1.0 - decay_first**STEP)
        / (jnp.sqrt(square_new / (1.0 - decay_second**STEP)) + adam_epsilon)
    )
    return (weight - step_rate * (corrected + weight_decay * weight), moment_new, square_new)


def swap_cores(value):
    return lax.ppermute(value, "seq", [(0, 1), (1, 0)])


def gather_plain(chips, heads, merge, expand, shrink, small, tokens):
    core = lax.axis_index("seq")

    def full(part):
        return lax.all_gather(part, ("dp", "seq"), axis=0, tiled=False)

    mine = lax.dynamic_index_in_dim(full(heads), core, 1, keepdims=False)
    return [mine, *map(full, (merge, expand, shrink, small)), jnp.stack([tokens, swap_cores(tokens)])]


def scatter_plain(heads, merge, expand, shrink, small):
    def sums(part):
        flat = part.astype(jnp.float32).reshape((-1,) + part.shape[-2:])
        return lax.psum_scatter(flat, ("dp", "seq"), scatter_dimension=0, tiled=False)

    own = heads.astype(jnp.float32).reshape((-1, 2) + heads.shape[-2:])
    own = lax.psum_scatter(own, "dp", scatter_dimension=0, tiled=False)
    own = lax.all_to_all(own, "seq", split_axis=0, concat_axis=0, tiled=True)
    reduced = [own, *map(sums, (merge, expand, shrink))]
    squares = lax.psum(sum(jnp.sum(part * part) for part in reduced), ("dp", "seq"))
    return [*reduced, lax.psum(small, ("dp", "seq")), squares]


def per_device(
    chips,
    layer_input,
    segment_ids,
    cotangent,
    heads_weight,
    heads_first,
    heads_second,
    merge_weight,
    merge_first,
    merge_second,
    expand_weight,
    expand_first,
    expand_second,
    shrink_weight,
    shrink_first,
    shrink_second,
    norm_gains,
    gains_first,
    gains_second,
    branch_bias,
    branch_first,
    branch_second,
    hidden_bias,
    hidden_first,
    hidden_second,
):
    low, wide = jnp.bfloat16, jnp.float32
    core = lax.axis_index("seq")
    index = lax.axis_index("dp") * 2 + core
    row_count, length = layer_input.shape[:2]
    rows = heads_weight.shape[0]
    devices = chips * 2
    hidden_rows = shrink_weight.shape[0]
    half = D // 2
    flat_input = layer_input.reshape(-1, D)
    tokens = flat_input.shape[0]
    kernels = rows % 8 == 0 and chips == 16
    block = (chips // 4, 2, 2, 2) if kernels else (devices,)

    heads_parts = heads_weight.astype(low).reshape(rows, 3, 2, half)
    heads_parts = heads_parts.transpose(2, 0, 1, 3).reshape(2, rows, 3 * half)
    small_rows = -(-rows // 8) * 8 + 8
    small_part = jnp.concatenate([norm_gains, branch_bias, jnp.zeros((rows, LANES - 8), wide)], axis=1)
    bottom = jnp.pad(hidden_bias[None], ((0, small_rows - rows - 1), (0, LANES - hidden_rows)))
    small_part = jnp.concatenate([small_part, bottom], axis=0).astype(low)
    gather = gather_all if kernels else gather_plain
    heads_all, merge_all, expand_all, shrink_all, small_all, inputs_all = gather(
        chips // 4,
        heads_parts,
        merge_weight.astype(low),
        expand_weight.astype(low),
        shrink_weight.astype(low),
        small_part,
        flat_input,
    )
    heads_low = heads_all.reshape(D, 3 * half)
    merge_low = merge_all.reshape(D, D)
    expand_low = expand_all.reshape(D, -1)
    shrink_low = shrink_all.reshape(-1, D)
    small_all = small_all.reshape(devices, small_rows, LANES).astype(wide)
    vectors = small_all[:, :rows, :8].reshape(D, 8).T
    gain_one, gain_two = vectors[0], vectors[1]
    hidden_full = small_all[:, rows, :hidden_rows].reshape(-1)
    heads_bias = jnp.concatenate(
        [
            lax.dynamic_slice(vectors[2], (core * half,), (half,)),
            jnp.zeros((half,), wide),
            lax.dynamic_slice(vectors[3], (core * half,), (half,)),
        ]
    )

    seg_own = lax.dynamic_slice(segment_ids, (0, core * length), (row_count, length))
    seg_other = lax.dynamic_slice(segment_ids, (0, (1 - core) * length), (row_count, length))
    seg_here = jnp.concatenate([seg_own, seg_other], axis=1)
    seg_key, seg_query = seg_here[:, :, None], seg_here[:, None, :]

    inputs_both = inputs_all.reshape(2 * tokens, D)
    projected = (dot(inputs_both, heads_low) + heads_bias).astype(low)
    heads_here = projected.reshape(2, row_count, length, 3 * half)
    context_here = attend(heads_here, seg_key, seg_query).reshape(2, tokens, half)
    context_other = swap_cores(context_here[1])
    first_heads = jnp.where(core == 0, context_here[0], context_other)
    last_heads = jnp.where(core == 0, context_other, context_here[0])
    flat_context = jnp.concatenate([first_heads, last_heads], axis=1)
    attended = dot(flat_context, merge_low) + vectors[4]
    normed_one, inverse_one = normalize(flat_input.astype(wide) + attended)
    first_low = (normed_one * gain_one + vectors[5]).astype(low)
    pre_active = dot(first_low, expand_low) + hidden_full
    active_low = gelu_value(pre_active).astype(low)
    branch_out = dot(active_low, shrink_low) + vectors[6]
    normed_two, inverse_two = normalize(first_low.astype(wide) + branch_out)
    work_output = (normed_two * gain_two + vectors[7]).astype(low).reshape(layer_input.shape)

    upstream = cotangent.reshape(-1, D).astype(wide)
    grad_gain_two = jnp.sum(upstream * normed_two, axis=0)
    grad_shift_two = jnp.sum(upstream, axis=0)
    grad_second = norm_back(upstream * gain_two, normed_two, inverse_two)
    branch_grad = grad_second.astype(low)
    grad_shrink = cross_rows(active_low, branch_grad).astype(low)
    grad_shrink_bias = jnp.sum(branch_grad.astype(wide), axis=0)
    active_grad = (cross_cols(branch_grad, shrink_low) * gelu_slope(pre_active)).astype(low)
    grad_expand = cross_rows(first_low, active_grad).astype(low)
    grad_hidden = jnp.sum(active_grad.astype(wide), axis=0)
    grad_first = grad_second + cross_cols(active_grad, expand_low)
    grad_gain_one = jnp.sum(grad_first * normed_one, axis=0)
    grad_shift_one = jnp.sum(grad_first, axis=0)
    grad_sum_one = norm_back(grad_first * gain_one, normed_one, inverse_one)
    attended_grad = grad_sum_one.astype(low)
    grad_merge = cross_rows(flat_context, attended_grad).astype(low)
    grad_merge_bias = jnp.sum(attended_grad.astype(wide), axis=0)
    context_grad = cross_cols(attended_grad, merge_low).astype(low)

    def own_columns(piece):
        return lax.dynamic_update_slice(jnp.zeros((D,), wide), piece, (core * half,))

    def small_grads(heads_bias_grad):
        if heads_bias_grad is None:
            nothing = jnp.zeros((D,), wide)
            query_bias, value_bias = nothing, nothing
        else:
            query_bias = own_columns(heads_bias_grad[:half])
            value_bias = own_columns(heads_bias_grad[2 * half :])
        found = jnp.stack(
            [
                grad_gain_one,
                grad_gain_two,
                query_bias,
                value_bias,
                grad_merge_bias,
                grad_shift_one,
                grad_shrink_bias,
                grad_shift_two,
            ]
        )
        found = jnp.concatenate([found, grad_hidden.reshape(-1, D)], axis=0)
        return jnp.pad(found, ((0, -found.shape[0] % 8), (0, 0)))

    grad_merge = grad_merge.reshape(block + (rows, D))
    grad_expand = grad_expand.reshape(block + (rows, expand_weight.shape[1]))
    grad_shrink = grad_shrink.reshape(block + (hidden_rows, D))
    if kernels:
        *sums, input_parts = finish_all(
            chips // 4,
            heads_here,
            context_grad.reshape(row_count, length, D),
            seg_key,
            seg_query,
            inputs_both,
            heads_low,
            grad_merge,
            grad_expand,
            grad_shrink,
            small_grads(None),
        )
        input_parts = input_parts.reshape(tokens, D)
    else:
        own = jnp.where(core == 0, context_grad[:, :half], context_grad[:, half:])
        other = swap_cores(jnp.where(core == 0, context_grad[:, half:], context_grad[:, :half]))
        grad_here = jnp.stack([own, other]).reshape(2, row_count, length, half)
        heads_grad = attend_back(heads_here, grad_here, seg_key, seg_query)
        heads_grad = heads_grad.reshape(2 * tokens, 3 * half)
        input_parts = cross_cols(heads_grad, heads_low)
        input_parts = input_parts[:tokens] + swap_cores(input_parts[tokens:].astype(low))
        grad_heads = cross_rows(inputs_both, heads_grad).astype(low)
        small_grad = small_grads(jnp.sum(heads_grad.astype(wide), axis=0))
        grad_heads = grad_heads.reshape(block + (rows, 3 * half))
        sums = scatter_plain(grad_heads, grad_merge, grad_expand, grad_shrink, small_grad)
    work_gradient = (grad_sum_one + input_parts).reshape(layer_input.shape)
    heads_sum, merge_sum, expand_sum, shrink_sum, small_sum, squares = sums
    vector_sum = lax.dynamic_slice(small_sum, (0, index * rows), (8, rows)).T
    hidden_sum = lax.dynamic_slice(
        small_sum[8 : 8 + hidden_rows * devices // D].reshape(-1), (index * hidden_rows,), (hidden_rows,)
    )
    states = (
        (heads_weight, heads_first, heads_second, rate_matrix),
        (merge_weight, merge_first, merge_second, rate_matrix),
        (expand_weight, expand_first, expand_second, rate_matrix),
        (shrink_weight, shrink_first, shrink_second, rate_matrix),
        (norm_gains, gains_first, gains_second, rate_vector),
        (branch_bias, branch_first, branch_second, rate_vector),
        (hidden_bias, hidden_first, hidden_second, rate_vector),
    )
    matrix_sums = (heads_sum, merge_sum, expand_sum, shrink_sum)
    vector_sums = (vector_sum[:, 0:2], vector_sum[:, 2:8], hidden_sum)
    if kernels:
        matrices, gradient_norm = update_all(
            squares, small_sum, [(matrix_sums[i], *states[i][:3]) for i in range(4)]
        )
        factor = jnp.minimum(1.0, clip_limit / gradient_norm)
    else:
        gradient_norm = jnp.sqrt(squares + jnp.sum(small_sum * small_sum))
        factor = jnp.minimum(1.0, clip_limit / gradient_norm)
        by_half = heads_sum.reshape(2, rows, 3, half).transpose(1, 2, 0, 3)
        matrices = []
        for i in range(4):
            slope = by_half.reshape(rows, 3 * D) if i == 0 else matrix_sums[i]
            found = adamw(*states[i][:3], slope, factor, rate_matrix)
            matrices.append([*found, found[0].astype(low)])
    vectors_new = [adamw(*states[i][:3], vector_sums[i - 4], factor, rate_vector) for i in range(4, 7)]
    return (
        work_output,
        work_gradient,
        gradient_norm,
        *[value for found in matrices for value in found[:3]],
        *[value for found in vectors_new for value in found],
        *[found[3] for found in matrices],
    )


def solution(mesh):
    matrix, vector = P(("dp", "seq"), None), P(("dp", "seq"))
    tokens = P("dp", "seq", None)
    states = (matrix,) * 18 + (vector,) * 3
    return jax.shard_map(
        functools.partial(per_device, mesh.shape["dp"]),
        mesh=mesh,
        in_specs=(tokens, P("dp", None), tokens) + states,
        out_specs=(tokens, tokens, P()) + states + (matrix,) * 4,
        check_vma=False,
    )
```

```python
import functools

import jax
import jax.numpy as jnp
from jax import lax
from jax.experimental import pallas as pl
from jax.experimental.pallas import tpu as pltpu
from jax.sharding import PartitionSpec as P

D = 768
HEAD_DIM = 64
STEP = 5
LANES = 128
MESH = pl.DeviceIdType.MESH

norm_epsilon = 1e-12
masked_score = -1e30
root_half = 0.7071067811865476
inv_root_tau = 0.3989422804014327
clip_limit = 1.0
decay_first = 0.9
decay_second = 0.999
adam_epsilon = 1e-08
weight_decay = 0.01
rate_matrix = 0.05
rate_vector = 0.5


def place():
    chip, core = lax.axis_index("dp"), lax.axis_index("seq")
    return chip // 4, (chip // 2) % 2, chip % 2, core


def device(z, y, x, core):
    return ((z * 2 + y) * 2 + x, core)


def signal(semaphore, target):
    pl.semaphore_signal(semaphore, inc=1, device_id=target, device_id_type=MESH)


def greet(layers, others=()):
    z, y, x, core = place()
    barrier = pltpu.get_barrier_semaphore()
    across = (device(z, y, x, 1 - core), device(z, y, 1 - x, core), device(z, 1 - y, x, core))
    for target in across + tuple(others):
        signal(barrier, target)

    @pl.when(z > 0)
    def _():
        signal(barrier, device(z - 1, y, x, core))

    @pl.when(z < layers - 1)
    def _():
        signal(barrier, device(z + 1, y, x, core))

    beside = jnp.where(z > 0, 1, 0) + jnp.where(z < layers - 1, 1, 0)
    pl.semaphore_wait(barrier, 3 + len(others) + beside)


def others_of(layers):
    z, y, x, core = place()
    line = [device((z + step) % layers, y, x, core) for step in range(1, layers)]
    plane = [
        device(
            z,
            1 - y if bits & 4 else y,
            1 - x if bits & 2 else x,
            1 - core if bits & 1 else core,
        )
        for bits in range(1, 8)
    ]
    return line, plane


def greet_line_and_plane(layers):
    barrier = pltpu.get_barrier_semaphore()
    line, plane = others_of(layers)
    for target in line + plane:
        signal(barrier, target)
    pl.semaphore_wait(barrier, len(line) + len(plane))


class Summed:
    def __init__(self, layers, line, plane, line_send, line_recv, plane_send, plane_recv):
        z, y, x, core = place()
        self.rooms = (line, plane)
        self.sems = ((line_send, line_recv), (plane_send, plane_recv))
        self.others = others_of(layers)
        at = y * 4 + x * 2 + core
        self.own = (z, at)
        self.sources = (
            [(z + layers - step) % layers for step in range(1, layers)],
            [
                (1 - y if bits & 4 else y) * 4
                + (1 - x if bits & 2 else x) * 2
                + (1 - core if bits & 1 else core)
                for bits in range(1, 8)
            ],
        )

    def copy(self, stage, which, slot):
        here = self.rooms[stage].at[slot]
        send, recv = self.sems[stage]
        return remote(here, here, send.at[which], recv.at[which], self.others[stage][which])

    def start(self, stage, value):
        self.rooms[stage][self.own[stage]] = value
        for which in range(len(self.others[stage])):
            self.copy(stage, which, self.own[stage]).start()

    def finish(self, stage):
        for which, slot in enumerate(self.sources[stage]):
            self.copy(stage, which, slot).wait_recv()
        room = self.rooms[stage]
        total = room[0]
        for slot in range(1, room.shape[0]):
            total = total + room[slot]
        return total

    def settle(self):
        for stage in range(2):
            for which in range(len(self.others[stage])):
                self.copy(stage, which, self.own[stage]).wait_send()


def remote(source, target, sent, received, to):
    return pltpu.make_async_remote_copy(
        src_ref=source,
        dst_ref=target,
        send_sem=sent,
        recv_sem=received,
        device_id=to,
        device_id_type=MESH,
    )


GATHERED = (
    ("heads", 0, 768, False),
    ("merge", 0, 768, True),
    ("small", 0, 128, True),
    ("heads", 768, 384, True),
    ("shrink", 0, 768, False),
    ("expand", 0, 3072, True),
)


def gather_kernel(
    layers,
    heads_in,
    merge_in,
    expand_in,
    shrink_in,
    small_in,
    tokens_in,
    seg_key,
    seg_query,
    weight_out,
    merge_all,
    expand_all,
    shrink_all,
    small_all,
    inputs_out,
    heads_out,
    context_out,
    vectors_out,
    heads_sent,
    merge_own,
    expand_own,
    shrink_own,
    heads_all,
    small_room,
    weight,
    tokens,
    heads_here,
    bias_row,
    bias,
    context_sent,
    context,
    pair_send,
    pair_recv,
    own_sem,
    out_sem,
    line_send,
    line_recv,
    first_send,
    first_recv,
    second_send,
    second_recv,
    core_send,
    core_recv,
    context_send,
    context_recv,
):
    z, y, x, core = place()
    partner = device(z, y, x, 1 - core)
    low, wide = jnp.bfloat16, jnp.float32
    own = {"merge": merge_own, "expand": expand_own, "shrink": shrink_own}
    full = {
        "merge": merge_all,
        "expand": expand_all,
        "shrink": shrink_all,
        "small": small_room,
        "heads": heads_all,
    }
    _, rows, length, columns = heads_here.shape
    width = columns // 3
    pairs = width // LANES

    tokens_keep = pltpu.make_async_copy(tokens_in, tokens.at[0], own_sem.at[0])
    tokens_keep.start()
    for part in range(3):
        for away in range(2):
            here = core if away == 0 else 1 - core
            start = pl.multiple_of((part * 2 + here) * width, LANES)
            block = heads_in[:, pl.ds(start, width)].astype(low)
            if away == 0:
                heads_all[z, y, x, core, :, part * width : (part + 1) * width] = block
            else:
                heads_sent[:, part * width : (part + 1) * width] = block
    small_room[z, y, x, core] = small_in[...]
    greet(layers)

    heads_pair = remote(
        heads_sent, heads_all.at[z, y, x, core], pair_send.at[0], pair_recv.at[0], partner
    )
    heads_pair.start()
    tokens_pair = remote(tokens_in, tokens.at[1], pair_send.at[1], pair_recv.at[1], partner)
    tokens_pair.start()
    merge_own[...] = merge_in[...].astype(low)
    shrink_own[...] = shrink_in[...].astype(low)
    expand_own[...] = expand_in[...].astype(low)

    def block(piece, zz, yy, xx, plane):
        name, start, wide_by, _ = GATHERED[piece]
        if name == "heads":
            return full[name].at[zz, yy, xx, :, :, pl.ds(start, wide_by)]
        return full[name].at[zz, yy, xx, plane]

    def own_block(piece):
        name = GATHERED[piece][0]
        return own[name] if name in own else block(piece, z, y, x, core)

    def couple(piece, zz, plane, moved):
        name, start, wide_by, y_first = GATHERED[piece]
        yy = y if y_first or not moved else 1 - y
        xx = x if not y_first or not moved else 1 - x
        if name == "heads":
            if y_first:
                return full[name].at[zz, :, xx, :, :, pl.ds(start, wide_by)]
            return full[name].at[zz, yy, :, :, :, pl.ds(start, wide_by)]
        if y_first:
            return full[name].at[zz, :, xx, plane]
        return full[name].at[zz, yy, :, plane]

    def across(piece, second):
        y_turn = GATHERED[piece][3] != second
        return device(z, 1 - y, x, core) if y_turn else device(z, y, 1 - x, core)

    def first_block(piece, zz):
        if GATHERED[piece][3]:
            return (zz, 1 - y, x)
        return (zz, y, 1 - x)

    def line_copy(piece, zz, source, target_z):
        return remote(
            source,
            block(piece, zz, y, x, core),
            line_send.at[piece, zz, jnp.where(target_z > z, 0, 1)],
            line_recv.at[piece, zz],
            device(target_z, y, x, core),
        )

    def first_copy(piece, zz, source):
        return remote(
            source,
            block(piece, zz, y, x, core),
            first_send.at[piece, zz],
            first_recv.at[piece, zz],
            across(piece, False),
        )

    def second_copy(piece, zz):
        both = couple(piece, zz, core, False)
        return remote(
            both, both, second_send.at[piece, zz], second_recv.at[piece, zz], across(piece, True)
        )

    def core_copy(piece, zz, stage, source, target):
        return remote(
            source,
            target,
            core_send.at[piece, zz, stage],
            core_recv.at[piece, zz, stage],
            partner,
        )

    def own_copy(piece):
        return pltpu.make_async_copy(
            own_block(piece), block(piece, z, y, x, core), own_sem.at[1 + piece]
        )

    def shared(piece):
        return GATHERED[piece][0] != "heads"

    pieces = range(len(GATHERED))
    near = [piece for piece in pieces if GATHERED[piece][0] not in own]
    far = [piece for piece in pieces if GATHERED[piece][0] in own]

    def begin_line(some):
        for piece in some:
            mine = own_block(piece)

            @pl.when(z < layers - 1)
            def _(piece=piece, mine=mine):
                line_copy(piece, z, mine, z + 1).start()

            @pl.when(z > 0)
            def _(piece=piece, mine=mine):
                line_copy(piece, z, mine, z - 1).start()

    def begin_first(some):
        for piece in some:
            mine = own_block(piece)
            first_copy(piece, z, mine).start()
            if shared(piece):
                core_copy(piece, z, 0, mine, block(piece, z, y, x, core)).start()
            if piece in far:
                own_copy(piece).start()

    def arrive_line(piece, zz, below):
        here = block(piece, zz, y, x, core)
        line_copy(piece, zz, here, z).wait_recv()
        if below:

            @pl.when(z < layers - 1)
            def _():
                line_copy(piece, zz, here, z + 1).start()

        else:

            @pl.when(z > 0)
            def _():
                line_copy(piece, zz, here, z - 1).start()

        first_copy(piece, zz, here).start()
        if shared(piece):
            core_copy(piece, zz, 0, here, here).start()

    def arrive_first(piece, zz, below):
        here = block(piece, *first_block(piece, zz), core)
        remote(
            here, here, first_send.at[piece, zz], first_recv.at[piece, zz], across(piece, False)
        ).wait_recv()
        second_copy(piece, zz).start()
        if shared(piece):
            core_copy(piece, zz, 1, here, here).start()

    def arrive_second(piece, zz, below):
        here = couple(piece, zz, core, True)
        remote(
            here, here, second_send.at[piece, zz], second_recv.at[piece, zz], across(piece, True)
        ).wait_recv()
        if shared(piece):
            core_copy(piece, zz, 2, here, here).start()

    def each(some, distance, action):
        if distance == 0:
            for piece in some:
                action(piece, z, None)
            return

        @pl.when(z - distance >= 0)
        def _():
            for piece in some:
                action(piece, z - distance, True)

        @pl.when(z + distance < layers)
        def _():
            for piece in some:
                action(piece, z + distance, False)

    def settle_core(piece, zz):
        mine = block(piece, zz, y, x, core)
        theirs = block(piece, zz, y, x, 1 - core)
        crossed = block(piece, *first_block(piece, zz), 1 - core)
        both = couple(piece, zz, 1 - core, True)
        core_copy(piece, zz, 0, mine, theirs).wait()
        core_copy(piece, zz, 1, mine, crossed).wait()
        core_copy(piece, zz, 2, both, both).wait()

    small_piece = [piece for piece in near if shared(piece)]
    heads_pieces = [piece for piece in near if not shared(piece)]
    heads_pair.wait_recv()
    begin_line(near)
    begin_first(near)
    begin_first(far)
    for piece in far:
        own_copy(piece).wait()
    each(near, 1, arrive_line)
    each(near, 0, arrive_first)
    each(near, 2, arrive_line)
    begin_line(far)
    each(near, 1, arrive_first)
    each(near, 0, arrive_second)
    each(far, 0, arrive_first)
    each(near, 3, arrive_line)
    each(near, 2, arrive_first)
    each(near, 1, arrive_second)
    each(far, 1, arrive_line)
    each(near, 3, arrive_first)
    each(near, 2, arrive_second)
    each(near, 3, arrive_second)
    for piece in small_piece:
        for zz in range(layers):
            settle_core(piece, zz)

    for zz in range(layers):
        depth = weight.shape[0] // layers
        weight[zz * depth : (zz + 1) * depth] = heads_all[zz].reshape(depth, columns)
    rows_each = small_room.shape[4] - 8
    found = small_room[...].astype(wide).reshape(-1, rows_each + 8, LANES)[:, :rows_each]
    vectors_out[...] = found.reshape(-1, LANES).T[0:8]
    bias_row[...] = jnp.zeros(bias_row.shape, wide)
    mine = pl.ds(pl.multiple_of(core * width, LANES), width)
    bias_row[:, 0:width] = vectors_out[2:3, mine]
    bias_row[:, 2 * width : 3 * width] = vectors_out[3:4, mine]
    tokens_keep.wait()
    tokens_pair.wait_recv()
    weight_copy = pltpu.make_async_copy(weight, weight_out, out_sem.at[0])
    inputs_copy = pltpu.make_async_copy(tokens, inputs_out, out_sem.at[1])
    heads_copy = pltpu.make_async_copy(heads_here, heads_out, out_sem.at[2])
    small_copy = pltpu.make_async_copy(small_room, small_all, out_sem.at[3])
    weight_copy.start()
    inputs_copy.start()
    small_copy.start()

    def project_step(step, carry):
        half, row = step // rows, step % rows
        start = pl.multiple_of(row * length, LANES)
        found = dot(tokens[half, pl.ds(start, length)], weight[...]) + bias_row[...]
        heads_here[half, row] = found.astype(low)

        @pl.when(step == 1)
        def _():
            each(far, 1, arrive_first)

        @pl.when(step == 5)
        def _():
            each(far, 2, arrive_line)
            each(far, 0, arrive_second)

        return carry

    lax.fori_loop(0, 2 * rows, project_step, 0)
    heads_copy.start()

    def context_copy(row):
        return remote(
            context_sent.at[row],
            context.at[row, :, pl.ds(pl.multiple_of(core * width, LANES), width)],
            context_send.at[row],
            context_recv.at[row],
            partner,
        )

    def attention_step(step, carry):
        row, pair = step // pairs, step % pairs

        @pl.when(pair == 0)
        def _():
            bias[...] = jnp.where(seg_key[row] == seg_query[row], 0.0, masked_score)

        def part(which):
            start = pl.multiple_of(which * width + pair * LANES, LANES)
            return heads_here[:, row, :, pl.ds(start, LANES)].reshape(2 * length, LANES)

        found = pair_forward(part(0), part(1), part(2), bias).reshape(2, length, LANES)
        context[row, :, pl.ds(pl.multiple_of(core * width + pair * LANES, LANES), LANES)] = found[0]
        context_sent[row, :, pl.ds(pl.multiple_of(pair * LANES, LANES), LANES)] = found[1]

        @pl.when(pair == pairs - 1)
        def _():
            context_copy(row).start()

        @pl.when(step == 0)
        def _():
            each(far, 2, arrive_first)

        @pl.when(step == 3)
        def _():
            each(far, 3, arrive_line)
            each(far, 1, arrive_second)

        @pl.when(step == 6)
        def _():
            each(far, 3, arrive_first)
            each(far, 2, arrive_second)

        return carry

    lax.fori_loop(0, rows * pairs, attention_step, 0)
    for row in range(rows):
        other = pl.ds(pl.multiple_of((1 - core) * width, LANES), width)
        remote(
            context_sent.at[row],
            context.at[row, :, other],
            context_send.at[row],
            context_recv.at[row],
            partner,
        ).wait()
    context_keep = pltpu.make_async_copy(context, context_out, out_sem.at[4])
    context_keep.start()
    each(far, 3, arrive_second)

    heads_pair.wait_send()
    tokens_pair.wait_send()

    def settle(zz, carry):
        for piece in pieces:
            here = block(piece, zz, y, x, core)
            first_copy(piece, zz, here).wait_send()
            second_copy(piece, zz).wait_send()
            if piece in far:
                settle_core(piece, zz)

            @pl.when(jnp.logical_and(z < layers - 1, zz <= z))
            def _(piece=piece, here=here):
                line_copy(piece, zz, here, z + 1).wait_send()

            @pl.when(jnp.logical_and(z > 0, zz >= z))
            def _(piece=piece, here=here):
                line_copy(piece, zz, here, z - 1).wait_send()

        return carry

    lax.fori_loop(0, layers, settle, 0)
    for copy in (weight_copy, inputs_copy, heads_copy, small_copy, context_keep):
        copy.wait()


def gather_attend(layers, heads, merge, expand, shrink, small, tokens, seg_key, seg_query):
    chips = (layers, 2, 2, 2)
    low, wide = jnp.bfloat16, jnp.float32
    count = len(GATHERED)
    sems = pltpu.SemaphoreType.DMA
    row_count, both = seg_query.shape[0], seg_query.shape[2]
    length, columns = both // 2, heads.shape[1] // 2
    rows = chips + (heads.shape[0], columns)
    depth = tokens.shape[1]
    here = (2, row_count, length, columns)
    vmem, anywhere = pl.BlockSpec(memory_space=pltpu.VMEM), pl.BlockSpec(memory_space=pl.ANY)
    return pl.pallas_call(
        functools.partial(gather_kernel, layers),
        out_shape=[
            jax.ShapeDtypeStruct((depth, columns), low),
            *[jax.ShapeDtypeStruct(chips + part.shape, low) for part in (merge, expand, shrink, small)],
            jax.ShapeDtypeStruct((2,) + tokens.shape, low),
            jax.ShapeDtypeStruct(here, low),
            jax.ShapeDtypeStruct((row_count, length, depth), low),
            jax.ShapeDtypeStruct((8, depth), wide),
        ],
        in_specs=[vmem] * 5 + [anywhere, vmem, vmem],
        out_specs=[anywhere] * 8 + [vmem],
        scratch_shapes=[
            pltpu.VMEM((heads.shape[0], columns), low),
            pltpu.VMEM(merge.shape, low),
            pltpu.VMEM(expand.shape, low),
            pltpu.VMEM(shrink.shape, low),
            pltpu.VMEM(rows, low),
            pltpu.VMEM(chips + small.shape, low),
            pltpu.VMEM((depth, columns), low),
            pltpu.VMEM((2,) + tokens.shape, low),
            pltpu.VMEM(here, low),
            pltpu.VMEM((1, columns), wide),
            pltpu.VMEM((both, both), wide),
            pltpu.VMEM((row_count, length, columns // 3), low),
            pltpu.VMEM((row_count, length, depth), low),
            sems((2,)),
            sems((2,)),
            sems((1 + count,)),
            sems((5,)),
            sems((count, layers, 2)),
            sems((count, layers)),
            sems((count, layers)),
            sems((count, layers)),
            sems((count, layers)),
            sems((count, layers)),
            sems((count, layers, 3)),
            sems((count, layers, 3)),
            sems((row_count,)),
            sems((row_count,)),
        ],
        compiler_params=pltpu.CompilerParams(
            collective_id=0, has_side_effects=True, vmem_limit_bytes=63 * 2**20
        ),
        name="gather_attend",
    )(heads, merge, expand, shrink, small, tokens, seg_key, seg_query)


SCATTERED = (
    ("shrink", 0, 768, False),
    ("expand", 0, 3072, True),
    ("merge", 0, 768, True),
    ("heads", 0, 768, False),
    ("heads", 768, 384, True),
)


def finish_kernel(
    layers,
    heads_ref,
    upstream_ref,
    seg_key,
    seg_query,
    inputs_ref,
    weight_ref,
    merge_in,
    expand_in,
    shrink_in,
    small_in,
    heads_out,
    merge_out,
    expand_out,
    shrink_out,
    small_out,
    square_out,
    tokens_out,
    heads_here,
    upstream_here,
    heads_grad,
    inputs_here,
    weight_here,
    bias,
    tokens_sent,
    tokens_room,
    totals,
    core_rooms,
    first_rooms,
    second_rooms,
    line_rooms,
    heads_last,
    heads_room,
    small_line,
    small_plane,
    square_line,
    square_plane,
    bring_sem,
    upstream_send,
    upstream_recv,
    tokens_send,
    tokens_recv,
    load_sem,
    core_send,
    core_recv,
    first_send,
    first_recv,
    second_send,
    second_recv,
    line_send,
    line_recv,
    last_send,
    last_recv,
    small_sems,
    square_sems,
):
    z, y, x, core = place()
    partner = device(z, y, x, 1 - core)
    sources = {"merge": merge_in, "expand": expand_in, "shrink": shrink_in}
    results = {"merge": merge_out, "expand": expand_out, "shrink": shrink_out}
    small_sum = Summed(layers, small_line, small_plane, *small_sems)
    square_sum = Summed(layers, square_line, square_plane, *square_sems)
    low, wide = jnp.bfloat16, jnp.float32
    _, rows, length, columns = heads_here.shape
    width = columns // 3
    pairs = width // LANES

    def bring_row(row):
        return pltpu.make_async_copy(heads_ref.at[:, row], heads_here.at[:, row], bring_sem.at[row])

    def columns_of(plane):
        return pl.ds(pl.multiple_of(plane * width, LANES), width)

    def upstream_keep(row):
        return pltpu.make_async_copy(
            upstream_ref.at[row, :, columns_of(core)], upstream_here.at[0, row], bring_sem.at[4 + row]
        )

    def upstream_copy(row):
        return remote(
            upstream_ref.at[row, :, columns_of(1 - core)],
            upstream_here.at[1, row],
            upstream_send.at[row],
            upstream_recv.at[row],
            partner,
        )

    bring_inputs = pltpu.make_async_copy(inputs_ref, inputs_here, bring_sem.at[8])
    bring_weight = pltpu.make_async_copy(weight_ref, weight_here, bring_sem.at[9])
    for row in range(rows):
        bring_row(row).start()
        upstream_keep(row).start()

    greet_line_and_plane(layers)
    for row in range(rows):
        upstream_copy(row).start()

    pieces = range(len(SCATTERED))
    early = [piece for piece in pieces if SCATTERED[piece][0] != "heads"]
    late = [piece for piece in pieces if SCATTERED[piece][0] == "heads"]

    def is_heads(piece):
        return SCATTERED[piece][0] == "heads"

    def y_first(piece):
        return SCATTERED[piece][3]

    def load(piece, zz):
        return pltpu.make_async_copy(
            sources[SCATTERED[piece][0]].at[zz, :, :, core], totals[piece].at[zz], load_sem.at[piece, zz]
        )

    def core_copy(piece, zz):
        return remote(
            sources[SCATTERED[piece][0]].at[zz, :, :, 1 - core],
            core_rooms[piece].at[zz],
            core_send.at[piece, zz],
            core_recv.at[piece, zz],
            partner,
        )

    def first_copy(piece, zz):
        if y_first(piece):
            source, to = totals[piece].at[zz, 1 - y], device(z, 1 - y, x, core)
        else:
            source, to = totals[piece].at[zz, :, 1 - x], device(z, y, 1 - x, core)
        return remote(
            source, first_rooms[piece].at[zz], first_send.at[piece, zz], first_recv.at[piece, zz], to
        )

    def second_copy(piece, zz):
        if y_first(piece):
            source, to = totals[piece].at[zz, y, 1 - x], device(z, y, 1 - x, core)
        else:
            source, to = totals[piece].at[zz, 1 - y, x], device(z, 1 - y, x, core)
        return remote(
            source,
            second_rooms[piece].at[zz],
            second_send.at[piece, zz],
            second_recv.at[piece, zz],
            to,
        )

    def line_copy(piece, zz, downward):
        to = z - 1 if downward else z + 1
        return remote(
            totals[piece].at[zz, y, x],
            line_rooms[piece].at[downward, zz],
            line_send.at[piece, zz],
            line_recv.at[piece, downward, zz],
            device(to, y, x, core),
        )

    def add(target, room):
        target[...] = (target[...].astype(wide) + room[...].astype(wide)).astype(low)

    def layer_of(step):
        upward = jnp.where(z < layers // 2, 1, 0)
        turned = jnp.where(jnp.logical_and(step >= 2, jnp.logical_or(z == 1, z == 2)), 5 - step, step)
        return jnp.where(upward == 1, layers - 1 - turned, turned)

    def on_first(piece, zz):
        if not is_heads(piece):
            load(piece, zz).wait()
            core_copy(piece, zz).wait_recv()

            def merge_one(index, carry):
                add(
                    totals[piece].at[zz, index // 2, index % 2],
                    core_rooms[piece].at[zz, index // 2, index % 2],
                )
                return carry

            lax.fori_loop(0, 4, merge_one, 0)
        first_copy(piece, zz).start()

    def on_second(piece, zz):
        first_copy(piece, zz).wait_recv()

        def merge_one(index, carry):
            if y_first(piece):
                target = totals[piece].at[zz, y, index]
            else:
                target = totals[piece].at[zz, index, x]
            add(target, first_rooms[piece].at[zz, index])
            return carry

        lax.fori_loop(0, 2, merge_one, 0)
        second_copy(piece, zz).start()

    def on_line(piece, zz):
        second_copy(piece, zz).wait_recv()
        mine = totals[piece].at[zz, y, x]
        add(mine, second_rooms[piece].at[zz])

        @pl.when(zz > z)
        def _():
            @pl.when(z > 0)
            def _():
                line_copy(piece, zz, 0).wait_recv()
                add(mine, line_rooms[piece].at[0, zz])

            line_copy(piece, zz, 0).start()

        @pl.when(zz < z)
        def _():
            @pl.when(z < layers - 1)
            def _():
                line_copy(piece, zz, 1).wait_recv()
                add(mine, line_rooms[piece].at[1, zz])

            line_copy(piece, zz, 1).start()

    def start_early(step, carry):
        for piece in early:
            core_copy(piece, layer_of(step)).start()
            load(piece, layer_of(step)).start()
        return carry

    lax.fori_loop(0, layers, start_early, 0)
    bring_inputs.start()
    bring_weight.start()

    scale = HEAD_DIM**-0.5

    def attention_step(step, carry):
        row, pair = step // pairs, step % pairs

        @pl.when(pair == 0)
        def _():
            bring_row(row).wait()
            upstream_keep(row).wait()
            upstream_copy(row).wait_recv()
            bias[...] = jnp.where(seg_key[row] == seg_query[row], 0.0, masked_score)

        def part(which):
            start = pl.multiple_of(which * width + pair * LANES, LANES)
            return heads_here[:, row, :, pl.ds(start, LANES)].reshape(2 * length, LANES)

        at = pl.multiple_of(pair * LANES, LANES)
        upstream = upstream_here[:, row, :, pl.ds(at, LANES)].reshape(2 * length, LANES)
        grads = pair_back(part(0), part(1), part(2), upstream, bias)
        for which in range(3):
            start = pl.multiple_of(which * width + pair * LANES, LANES)
            heads_grad[:, row, :, pl.ds(start, LANES)] = grads[which].reshape(2, length, LANES)

        @pl.when(jnp.logical_and(step >= 4, step % 3 == 1))
        def _():
            for piece in early:
                on_second(piece, layer_of((step - 4) // 3))

        @pl.when(jnp.logical_or(step == 0, jnp.logical_and(step < 9, step % 3 == 1)))
        def _():
            for piece in early:
                on_first(piece, layer_of((step + 2) // 3))

        @pl.when(jnp.logical_or(step == 9, step == 11))
        def _():
            for piece in early:
                on_line(piece, layer_of((step - 9) // 2))

        return carry

    lax.fori_loop(0, rows * pairs, attention_step, 0)

    bring_inputs.wait()
    flat_grad = heads_grad[...].reshape(2 * rows * length, columns)
    ones = jnp.ones((8, 2 * rows * length), low)
    sums = dot(ones, flat_grad)
    small_out[...] = small_in[...]
    small_out[2:3, columns_of(core)] = sums[0:1, 0:width]
    small_out[3:4, columns_of(core)] = sums[0:1, 2 * width : 3 * width]
    small_sum.start(0, small_out[...])
    depth = inputs_here.shape[1] // 2

    def weight_step(turn, carry):
        step = jnp.where(z < layers // 2, 1 - turn, turn)
        start = pl.multiple_of(step * depth, LANES)
        found = dot(inputs_here[:, pl.ds(start, depth)], flat_grad, (((0,), (0,)), ((), ())))
        for piece in late:
            _, first, wide_by, _ = SCATTERED[piece]
            block = found[:, first : first + wide_by]
            block = block.reshape((layers // 2,) + totals[piece].shape[1:]).astype(low)
            totals[piece][pl.ds(step * (layers // 2), layers // 2)] = block

        @pl.when(turn == 0)
        def _():
            for piece in early:
                on_second(piece, layer_of(layers - 1))

        for which in range(layers // 2):
            for piece in late:
                on_first(piece, layer_of(turn * (layers // 2) + which))
        return carry

    lax.fori_loop(0, 2, weight_step, 0)

    bring_weight.wait()

    def tokens_copy(row):
        return remote(
            tokens_sent.at[row], tokens_room.at[row], tokens_send.at[row], tokens_recv.at[row], partner
        )

    def other_step(row, carry):
        tokens_sent[row] = dot(heads_grad[1, row], weight_here[...], FAR).astype(low)
        tokens_copy(row).start()

        @pl.when(row >= 1)
        def _():
            for piece in late:
                on_second(piece, layer_of(row - 1))

        @pl.when(row % 2 == 0)
        def _():
            for piece in early:
                on_line(piece, layer_of(2 + row // 2))

        @pl.when(row == 2)
        def _():
            small_sum.start(1, small_sum.finish(0))

        return carry

    def own_step(row, carry):
        found = dot(heads_grad[0, row], weight_here[...], FAR)
        tokens_copy(row).wait_recv()
        tokens_out[row] = found + tokens_room[row].astype(wide)

        @pl.when(row == 0)
        def _():
            for piece in late:
                on_second(piece, layer_of(layers - 1))

        for piece in late:
            on_line(piece, layer_of(row))
        return carry

    lax.fori_loop(0, rows, other_step, 0)
    lax.fori_loop(0, rows, own_step, 0)
    small_out[...] = small_sum.finish(1)

    def squares(value):
        by_row = jnp.sum((value * value).reshape(value.shape[0] // 8, 8, value.shape[1]), axis=0)
        total = by_row[:, 0:LANES]
        for start in range(LANES, value.shape[1], LANES):
            total = total + by_row[:, start : start + LANES]
        return total

    def last_copy(piece):
        _, start, wide_by, _ = SCATTERED[piece]
        return remote(
            heads_last.at[:, pl.ds(start, wide_by)],
            heads_room.at[:, pl.ds(start, wide_by)],
            last_send.at[piece],
            last_recv.at[piece],
            partner,
        )

    found_squares = jnp.zeros((8, LANES), wide)
    for piece in early + late:
        name, start, wide_by, _ = SCATTERED[piece]
        mine = totals[piece].at[z, y, x]

        @pl.when(z > 0)
        def _(piece=piece, mine=mine):
            line_copy(piece, z, 0).wait_recv()
            add(mine, line_rooms[piece].at[0, z])

        @pl.when(z < layers - 1)
        def _(piece=piece, mine=mine):
            line_copy(piece, z, 1).wait_recv()
            add(mine, line_rooms[piece].at[1, z])

        if is_heads(piece):
            heads_last[:, start : start + wide_by] = mine[1 - core]
            last_copy(piece).start()
            kept = mine[core].astype(wide)
            heads_out[core, :, start : start + wide_by] = kept
        else:
            kept = mine[...].astype(wide)
            results[name][...] = kept
        found_squares = found_squares + squares(kept)
    for piece in late:
        _, start, wide_by, _ = SCATTERED[piece]
        last_copy(piece).wait_recv()
        theirs = heads_room[:, start : start + wide_by].astype(wide)
        heads_out[1 - core, :, start : start + wide_by] = theirs
        found_squares = found_squares + squares(theirs)

    square_sum.start(0, found_squares)
    square_sum.start(1, square_sum.finish(0))
    square_out[...] = square_sum.finish(1)

    small_sum.settle()
    square_sum.settle()
    for row in range(rows):
        upstream_copy(row).wait_send()
        tokens_copy(row).wait_send()

    def settle(zz, carry):
        for piece in pieces:
            if not is_heads(piece):
                core_copy(piece, zz).wait_send()
            first_copy(piece, zz).wait_send()
            second_copy(piece, zz).wait_send()

            @pl.when(zz > z)
            def _(piece=piece):
                line_copy(piece, zz, 0).wait_send()

            @pl.when(zz < z)
            def _(piece=piece):
                line_copy(piece, zz, 1).wait_send()

        return carry

    lax.fori_loop(0, layers, settle, 0)
    for piece in late:
        last_copy(piece).wait_send()


def finish_all(layers, heads, upstream, seg_key, seg_query, inputs, weight, merge, expand, shrink, small):
    low, wide = jnp.bfloat16, jnp.float32
    block_rows = merge.shape[4]
    _, rows, length, columns = heads.shape
    width = columns // 3
    sums_rows = {"merge": block_rows, "expand": block_rows, "shrink": shrink.shape[4]}
    sems = pltpu.SemaphoreType.DMA

    def rooms(*lead, some=SCATTERED):
        return [
            pltpu.VMEM(
                tuple(lead)
                + ((2, block_rows, wide_by) if name == "heads" else (sums_rows[name], wide_by)),
                low,
            )
            for name, _, wide_by, _ in some
        ]

    count = len(SCATTERED)
    early = [piece for piece in SCATTERED if piece[0] != "heads"]
    vmem, anywhere = pl.BlockSpec(memory_space=pltpu.VMEM), pl.BlockSpec(memory_space=pl.ANY)
    return pl.pallas_call(
        functools.partial(finish_kernel, layers),
        out_shape=[
            jax.ShapeDtypeStruct((2, block_rows, columns), wide),
            *[jax.ShapeDtypeStruct(part.shape[4:], wide) for part in (merge, expand, shrink)],
            jax.ShapeDtypeStruct(small.shape, wide),
            jax.ShapeDtypeStruct((8, LANES), wide),
            jax.ShapeDtypeStruct((rows, length, inputs.shape[1]), wide),
        ],
        in_specs=[anywhere, anywhere, vmem, vmem] + [anywhere] * 5 + [vmem],
        out_specs=[vmem] * 7,
        scratch_shapes=[
            pltpu.VMEM(heads.shape, low),
            pltpu.VMEM((2, rows, length, width), low),
            pltpu.VMEM(heads.shape, low),
            pltpu.VMEM(inputs.shape, low),
            pltpu.VMEM(weight.shape, low),
            pltpu.VMEM((2 * length, 2 * length), wide),
            pltpu.VMEM((rows, length, inputs.shape[1]), low),
            pltpu.VMEM((rows, length, inputs.shape[1]), low),
            rooms(layers, 2, 2),
            rooms(layers, 2, 2, some=early),
            rooms(layers, 2),
            rooms(layers),
            rooms(2, layers),
            pltpu.VMEM((block_rows, columns), low),
            pltpu.VMEM((block_rows, columns), low),
            pltpu.VMEM((layers,) + small.shape, wide),
            pltpu.VMEM((8,) + small.shape, wide),
            pltpu.VMEM((layers, 8, LANES), wide),
            pltpu.VMEM((8, 8, LANES), wide),
            sems((10,)),
            sems((rows,)),
            sems((rows,)),
            sems((rows,)),
            sems((rows,)),
            sems((count, layers)),
            sems((count, layers)),
            sems((count, layers)),
            sems((count, layers)),
            sems((count, layers)),
            sems((count, layers)),
            sems((count, layers)),
            sems((count, layers)),
            sems((count, 2, layers)),
            sems((count,)),
            sems((count,)),
            [sems((layers - 1,)), sems((layers - 1,)), sems((7,)), sems((7,))],
            [sems((layers - 1,)), sems((layers - 1,)), sems((7,)), sems((7,))],
        ],
        compiler_params=pltpu.CompilerParams(
            collective_id=1, has_side_effects=True, vmem_limit_bytes=63 * 2**20
        ),
        name="finish_all",
    )(heads, upstream, seg_key, seg_query, inputs, weight, merge, expand, shrink, small)


def update_kernel(squares, small, *refs):
    count = len(refs) // 8
    total = jnp.sum(squares[...], keepdims=True) + jnp.sum(small[...] * small[...], keepdims=True)
    norm = jnp.sqrt(total)
    factor = jnp.minimum(1.0, clip_limit / norm)
    refs[-1][...] = norm
    for which in range(count):
        gradient, weight, moment, square = (refs[which * 4 + i] for i in range(4))
        outs = refs[count * 4 + which * 4 : count * 4 + which * 4 + 4]
        half = weight.shape[1] // 6
        if len(gradient.shape) == 3:
            spans = [
                (slice((part * 2 + core) * half, (part * 2 + core + 1) * half), part, core)
                for part in range(3)
                for core in range(2)
            ]
        else:
            spans = [(slice(0, weight.shape[1]), None, None)]
        for span, part, core in spans:
            if part is None:
                slope = gradient[...]
            else:
                slope = gradient[core, :, part * half : (part + 1) * half]
            updated, first, second = adamw(
                weight[:, span], moment[:, span], square[:, span], slope, factor, rate_matrix
            )
            outs[0][:, span] = updated
            outs[1][:, span] = first
            outs[2][:, span] = second
            outs[3][:, span] = updated.astype(jnp.bfloat16)


def update_all(squares, small, states):
    whole = pl.BlockSpec(memory_space=pltpu.VMEM)
    flat = [part for state in states for part in state]
    shapes = []
    for state in states:
        shapes += [jax.ShapeDtypeStruct(state[1].shape, jnp.float32)] * 3
        shapes += [jax.ShapeDtypeStruct(state[1].shape, jnp.bfloat16)]
    shapes.append(jax.ShapeDtypeStruct((1, 1), jnp.float32))
    found = pl.pallas_call(
        update_kernel,
        out_shape=shapes,
        in_specs=[whole] * (2 + len(flat)),
        out_specs=[whole] * len(shapes),
        name="update_all",
    )(squares, small, *flat)
    return [found[4 * which : 4 * which + 4] for which in range(len(states))], found[-1][0, 0]


FAR = (((1,), (1,)), ((), ()))
NEAR = (((1,), (0,)), ((), ()))


def dot(left, right, dims=NEAR):
    return lax.dot_general(left, right, dims, preferred_element_type=jnp.float32)


def write_bias(bias, seg_key, seg_query):
    @pl.when(pl.program_id(1) == 0)
    def _():
        bias[...] = jnp.where(seg_key[0] == seg_query[0], 0.0, masked_score)


def both_halves(ref):
    halves, rows, length, lanes = ref.shape
    return ref[...].reshape(halves * rows * length, lanes)


def only_head(head, value):
    lane = lax.broadcasted_iota(jnp.int32, value.shape, 1)
    return jnp.where((lane // HEAD_DIM) == head, value, jnp.zeros_like(value))


def softmax_of(keys, query, bias):
    scores = dot(keys, query, FAR) + bias[...]
    unscaled = jnp.exp(scores - jnp.max(scores, axis=0, keepdims=True))
    return unscaled * (1.0 / jnp.sum(unscaled, axis=0, keepdims=True))


def pair_forward(query, keys, values, bias):
    query = query * jnp.asarray(HEAD_DIM**-0.5, jnp.bfloat16)
    flipped = values.T
    found = []
    for head in range(2):
        weights = softmax_of(keys, only_head(head, query), bias).astype(jnp.bfloat16)
        found.append(dot(flipped[head * HEAD_DIM : (head + 1) * HEAD_DIM], weights))
    return jnp.concatenate(found, axis=0).T.astype(jnp.bfloat16)


def attend_kernel(query_ref, key_ref, value_ref, seg_key, seg_query, out_ref, bias):
    write_bias(bias, seg_key, seg_query)
    refs = (query_ref, key_ref, value_ref)
    context = pair_forward(*[both_halves(ref) for ref in refs], bias)
    out_ref[...] = context.reshape(out_ref.shape)


def pair_back(query, keys, values, upstream, bias):
    scale = HEAD_DIM**-0.5
    query = query * jnp.asarray(scale, jnp.bfloat16)
    flipped = keys.T
    found_query, found_key, found_value = [], [], []
    for head in range(2):
        weights = softmax_of(keys, only_head(head, query), bias)
        grad_weights = dot(only_head(head, values), upstream, FAR)
        inner = jnp.sum(weights * grad_weights, axis=0, keepdims=True)
        grad_scores = (weights * (grad_weights - inner)).astype(jnp.bfloat16)
        found_value.append(dot(weights.astype(jnp.bfloat16), upstream))
        found_key.append(dot(grad_scores, query))
        found_query.append(dot(flipped[head * HEAD_DIM : (head + 1) * HEAD_DIM], grad_scores))
    lane = lax.broadcasted_iota(jnp.int32, found_key[0].shape, 1)
    return (
        (jnp.concatenate(found_query, axis=0).T * scale).astype(jnp.bfloat16),
        jnp.where(lane < HEAD_DIM, found_key[0], found_key[1]).astype(jnp.bfloat16),
        jnp.where(lane < HEAD_DIM, found_value[0], found_value[1]).astype(jnp.bfloat16),
    )


def attend_back_kernel(
    query_ref, key_ref, value_ref, upstream_ref, seg_key, seg_query, out_ref, bias
):
    write_bias(bias, seg_key, seg_query)
    refs = (query_ref, key_ref, value_ref, upstream_ref)
    grads = pair_back(*[both_halves(ref) for ref in refs], bias)
    width = out_ref.shape[3] // 3
    for which in range(3):
        start = pl.multiple_of(pl.program_id(1) * LANES + which * width, LANES)
        out_ref[:, :, :, pl.ds(start, LANES)] = grads[which].reshape(query_ref.shape)


def head_block(length, first):
    return pl.BlockSpec((2, 1, length, LANES), lambda row, pair: (0, row, 0, first + pair))


def attention_specs(rows, length):
    return [
        pl.BlockSpec((1, 2 * length, 1), lambda row, pair: (row, 0, 0)),
        pl.BlockSpec((1, 1, 2 * length), lambda row, pair: (row, 0, 0)),
    ]


def attend(heads, seg_key, seg_query):
    _, rows, length, columns = heads.shape
    width = columns // 3
    pairs = width // LANES
    flops = 4 * rows * width * (2 * length) ** 2
    return pl.pallas_call(
        attend_kernel,
        grid=(rows, pairs),
        out_shape=jax.ShapeDtypeStruct((2, rows, length, width), jnp.bfloat16),
        in_specs=[
            head_block(length, 0),
            head_block(length, pairs),
            head_block(length, 2 * pairs),
            *attention_specs(rows, length),
        ],
        out_specs=head_block(length, 0),
        scratch_shapes=[pltpu.VMEM((2 * length, 2 * length), jnp.float32)],
        cost_estimate=pl.CostEstimate(
            flops=flops, bytes_accessed=8 * heads.size // 3, transcendentals=flops // 256
        ),
        name="attend",
    )(heads, heads, heads, seg_key, seg_query)


def attend_back(heads, upstream, seg_key, seg_query):
    _, rows, length, columns = heads.shape
    width = columns // 3
    pairs = width // LANES
    flops = 10 * rows * width * (2 * length) ** 2
    return pl.pallas_call(
        attend_back_kernel,
        grid=(rows, pairs),
        out_shape=jax.ShapeDtypeStruct(heads.shape, jnp.bfloat16),
        in_specs=[
            head_block(length, 0),
            head_block(length, pairs),
            head_block(length, 2 * pairs),
            head_block(length, 0),
            *attention_specs(rows, length),
        ],
        out_specs=pl.BlockSpec((2, 1, length, columns), lambda row, pair: (0, row, 0, 0)),
        scratch_shapes=[pltpu.VMEM((2 * length, 2 * length), jnp.float32)],
        cost_estimate=pl.CostEstimate(
            flops=flops, bytes_accessed=14 * heads.size // 3, transcendentals=flops // 640
        ),
        name="attend_back",
    )(heads, heads, heads, upstream, seg_key, seg_query)


def normalize(hidden):
    center = hidden - jnp.mean(hidden, axis=-1, keepdims=True)
    inverse_scale = lax.rsqrt(jnp.mean(center * center, axis=-1, keepdims=True) + norm_epsilon)
    return (center * inverse_scale, inverse_scale)


def norm_back(upstream, normed, inverse_scale):
    mean_upstream = jnp.mean(upstream, axis=-1, keepdims=True)
    mean_cross = jnp.mean(upstream * normed, axis=-1, keepdims=True)
    return inverse_scale * (upstream - mean_upstream - normed * mean_cross)


def gelu_value(inputs):
    return 0.5 * inputs * (1.0 + lax.erf(inputs * root_half))


def gelu_slope(inputs):
    return (
        0.5 * (1.0 + lax.erf(inputs * root_half))
        + inputs * jnp.exp(-0.5 * inputs * inputs) * inv_root_tau
    )


def cross_rows(operand_left, operand_right):
    return lax.dot_general(
        operand_left, operand_right, (((0,), (0,)), ((), ())), preferred_element_type=jnp.float32
    )


def cross_cols(operand_left, operand_right):
    return dot(operand_left, operand_right, FAR)


def adamw(weight, moment, square, gradient, factor, step_rate):
    clipped = gradient * factor
    moment_new = decay_first * moment + (1.0 - decay_first) * clipped
    square_new = decay_second * square + (1.0 - decay_second) * clipped * clipped
    corrected = (
        moment_new
        / (1.0 - decay_first**STEP)
        / (jnp.sqrt(square_new / (1.0 - decay_second**STEP)) + adam_epsilon)
    )
    return (weight - step_rate * (corrected + weight_decay * weight), moment_new, square_new)


def swap_cores(value):
    return lax.ppermute(value, "seq", [(0, 1), (1, 0)])


def gather_plain(heads, merge, expand, shrink, small, tokens):
    core = lax.axis_index("seq")

    def full(part):
        return lax.all_gather(part, ("dp", "seq"), axis=0, tiled=False)

    mine = lax.dynamic_index_in_dim(full(heads), core, 1, keepdims=False)
    return [mine, *map(full, (merge, expand, shrink, small)), jnp.stack([tokens, swap_cores(tokens)])]


def scatter_plain(heads, merge, expand, shrink, small):
    def sums(part):
        flat = part.astype(jnp.float32).reshape((-1,) + part.shape[-2:])
        return lax.psum_scatter(flat, ("dp", "seq"), scatter_dimension=0, tiled=False)

    own = heads.astype(jnp.float32).reshape((-1, 2) + heads.shape[-2:])
    own = lax.psum_scatter(own, "dp", scatter_dimension=0, tiled=False)
    own = lax.all_to_all(own, "seq", split_axis=0, concat_axis=0, tiled=True)
    reduced = [own, *map(sums, (merge, expand, shrink))]
    squares = lax.psum(sum(jnp.sum(part * part) for part in reduced), ("dp", "seq"))
    return [*reduced, lax.psum(small, ("dp", "seq")), squares]


def per_device(
    chips,
    layer_input,
    segment_ids,
    cotangent,
    heads_weight,
    heads_first,
    heads_second,
    merge_weight,
    merge_first,
    merge_second,
    expand_weight,
    expand_first,
    expand_second,
    shrink_weight,
    shrink_first,
    shrink_second,
    norm_gains,
    gains_first,
    gains_second,
    branch_bias,
    branch_first,
    branch_second,
    hidden_bias,
    hidden_first,
    hidden_second,
):
    low, wide = jnp.bfloat16, jnp.float32
    core = lax.axis_index("seq")
    index = lax.axis_index("dp") * 2 + core
    row_count, length = layer_input.shape[:2]
    rows = heads_weight.shape[0]
    devices = chips * 2
    hidden_rows = shrink_weight.shape[0]
    half = D // 2
    flat_input = layer_input.reshape(-1, D)
    tokens = flat_input.shape[0]
    kernels = rows % 8 == 0 and chips == 16
    block = (chips // 4, 2, 2, 2) if kernels else (devices,)

    small_rows = -(-rows // 8) * 8 + 8
    small_part = jnp.concatenate([norm_gains, branch_bias, jnp.zeros((rows, LANES - 8), wide)], axis=1)
    bottom = jnp.pad(hidden_bias[None], ((0, small_rows - rows - 1), (0, LANES - hidden_rows)))
    small_part = jnp.concatenate([small_part, bottom], axis=0).astype(low)
    seg_own = lax.dynamic_slice(segment_ids, (0, core * length), (row_count, length))
    seg_other = lax.dynamic_slice(segment_ids, (0, (1 - core) * length), (row_count, length))
    seg_here = jnp.concatenate([seg_own, seg_other], axis=1)
    seg_key, seg_query = seg_here[:, :, None], seg_here[:, None, :]

    if kernels:
        heads_low, merge_all, expand_all, shrink_all, small_all, inputs_all, heads_here, *found = gather_attend(
            chips // 4,
            heads_weight,
            merge_weight,
            expand_weight,
            shrink_weight,
            small_part,
            flat_input,
            seg_key,
            seg_query,
        )
        flat_context, vectors = found[0].reshape(tokens, D), found[1]
    else:
        heads_parts = heads_weight.astype(low).reshape(rows, 3, 2, half)
        heads_parts = heads_parts.transpose(2, 0, 1, 3).reshape(2, rows, 3 * half)
        heads_all, merge_all, expand_all, shrink_all, small_all, inputs_all = gather_plain(
            heads_parts,
            merge_weight.astype(low),
            expand_weight.astype(low),
            shrink_weight.astype(low),
            small_part,
            flat_input,
        )
        heads_low = heads_all.reshape(D, 3 * half)
    merge_low = merge_all.reshape(D, D)
    expand_low = expand_all.reshape(D, -1)
    shrink_low = shrink_all.reshape(-1, D)
    small_all = small_all.reshape(devices, small_rows, LANES).astype(wide)
    hidden_full = small_all[:, rows, :hidden_rows].reshape(-1)
    inputs_both = inputs_all.reshape(2 * tokens, D)
    if not kernels:
        vectors = small_all[:, :rows, :8].reshape(D, 8).T
        heads_bias = jnp.concatenate(
            [
                lax.dynamic_slice(vectors[2], (core * half,), (half,)),
                jnp.zeros((half,), wide),
                lax.dynamic_slice(vectors[3], (core * half,), (half,)),
            ]
        )
        projected = (dot(inputs_both, heads_low) + heads_bias).astype(low)
        heads_here = projected.reshape(2, row_count, length, 3 * half)
        context_here = attend(heads_here, seg_key, seg_query).reshape(2, tokens, half)
        context_other = swap_cores(context_here[1])
        first_heads = jnp.where(core == 0, context_here[0], context_other)
        last_heads = jnp.where(core == 0, context_other, context_here[0])
        flat_context = jnp.concatenate([first_heads, last_heads], axis=1)
    gain_one, gain_two = vectors[0], vectors[1]
    attended = dot(flat_context, merge_low) + vectors[4]
    normed_one, inverse_one = normalize(flat_input.astype(wide) + attended)
    first_low = (normed_one * gain_one + vectors[5]).astype(low)
    pre_active = dot(first_low, expand_low) + hidden_full
    active_low = gelu_value(pre_active).astype(low)
    branch_out = dot(active_low, shrink_low) + vectors[6]
    normed_two, inverse_two = normalize(first_low.astype(wide) + branch_out)
    work_output = (normed_two * gain_two + vectors[7]).astype(low).reshape(layer_input.shape)

    upstream = cotangent.reshape(-1, D).astype(wide)
    grad_gain_two = jnp.sum(upstream * normed_two, axis=0)
    grad_shift_two = jnp.sum(upstream, axis=0)
    grad_second = norm_back(upstream * gain_two, normed_two, inverse_two)
    branch_grad = grad_second.astype(low)
    grad_shrink = cross_rows(active_low, branch_grad).astype(low)
    grad_shrink_bias = jnp.sum(branch_grad.astype(wide), axis=0)
    active_grad = (cross_cols(branch_grad, shrink_low) * gelu_slope(pre_active)).astype(low)
    grad_expand = cross_rows(first_low, active_grad).astype(low)
    grad_hidden = jnp.sum(active_grad.astype(wide), axis=0)
    grad_first = grad_second + cross_cols(active_grad, expand_low)
    grad_gain_one = jnp.sum(grad_first * normed_one, axis=0)
    grad_shift_one = jnp.sum(grad_first, axis=0)
    grad_sum_one = norm_back(grad_first * gain_one, normed_one, inverse_one)
    attended_grad = grad_sum_one.astype(low)
    grad_merge = cross_rows(flat_context, attended_grad).astype(low)
    grad_merge_bias = jnp.sum(attended_grad.astype(wide), axis=0)
    context_grad = cross_cols(attended_grad, merge_low).astype(low)

    def own_columns(piece):
        return lax.dynamic_update_slice(jnp.zeros((D,), wide), piece, (core * half,))

    def small_grads(heads_bias_grad):
        if heads_bias_grad is None:
            nothing = jnp.zeros((D,), wide)
            query_bias, value_bias = nothing, nothing
        else:
            query_bias = own_columns(heads_bias_grad[:half])
            value_bias = own_columns(heads_bias_grad[2 * half :])
        found = jnp.stack(
            [
                grad_gain_one,
                grad_gain_two,
                query_bias,
                value_bias,
                grad_merge_bias,
                grad_shift_one,
                grad_shrink_bias,
                grad_shift_two,
            ]
        )
        found = jnp.concatenate([found, grad_hidden.reshape(-1, D)], axis=0)
        return jnp.pad(found, ((0, -found.shape[0] % 8), (0, 0)))

    grad_merge = grad_merge.reshape(block + (rows, D))
    grad_expand = grad_expand.reshape(block + (rows, expand_weight.shape[1]))
    grad_shrink = grad_shrink.reshape(block + (hidden_rows, D))
    if kernels:
        *sums, input_parts = finish_all(
            chips // 4,
            heads_here,
            context_grad.reshape(row_count, length, D),
            seg_key,
            seg_query,
            inputs_both,
            heads_low,
            grad_merge,
            grad_expand,
            grad_shrink,
            small_grads(None),
        )
        input_parts = input_parts.reshape(tokens, D)
    else:
        own = jnp.where(core == 0, context_grad[:, :half], context_grad[:, half:])
        other = swap_cores(jnp.where(core == 0, context_grad[:, half:], context_grad[:, :half]))
        grad_here = jnp.stack([own, other]).reshape(2, row_count, length, half)
        heads_grad = attend_back(heads_here, grad_here, seg_key, seg_query)
        heads_grad = heads_grad.reshape(2 * tokens, 3 * half)
        input_parts = cross_cols(heads_grad, heads_low)
        input_parts = input_parts[:tokens] + swap_cores(input_parts[tokens:].astype(low))
        grad_heads = cross_rows(inputs_both, heads_grad).astype(low)
        small_grad = small_grads(jnp.sum(heads_grad.astype(wide), axis=0))
        grad_heads = grad_heads.reshape(block + (rows, 3 * half))
        sums = scatter_plain(grad_heads, grad_merge, grad_expand, grad_shrink, small_grad)
    work_gradient = (grad_sum_one + input_parts).reshape(layer_input.shape)
    heads_sum, merge_sum, expand_sum, shrink_sum, small_sum, squares = sums
    vector_sum = lax.dynamic_slice(small_sum, (0, index * rows), (8, rows)).T
    hidden_sum = lax.dynamic_slice(
        small_sum[8 : 8 + hidden_rows * devices // D].reshape(-1), (index * hidden_rows,), (hidden_rows,)
    )
    states = (
        (heads_weight, heads_first, heads_second, rate_matrix),
        (merge_weight, merge_first, merge_second, rate_matrix),
        (expand_weight, expand_first, expand_second, rate_matrix),
        (shrink_weight, shrink_first, shrink_second, rate_matrix),
        (norm_gains, gains_first, gains_second, rate_vector),
        (branch_bias, branch_first, branch_second, rate_vector),
        (hidden_bias, hidden_first, hidden_second, rate_vector),
    )
    matrix_sums = (heads_sum, merge_sum, expand_sum, shrink_sum)
    vector_sums = (vector_sum[:, 0:2], vector_sum[:, 2:8], hidden_sum)
    if kernels:
        matrices, gradient_norm = update_all(
            squares, small_sum, [(matrix_sums[i], *states[i][:3]) for i in range(4)]
        )
        factor = jnp.minimum(1.0, clip_limit / gradient_norm)
    else:
        gradient_norm = jnp.sqrt(squares + jnp.sum(small_sum * small_sum))
        factor = jnp.minimum(1.0, clip_limit / gradient_norm)
        by_half = heads_sum.reshape(2, rows, 3, half).transpose(1, 2, 0, 3)
        matrices = []
        for i in range(4):
            slope = by_half.reshape(rows, 3 * D) if i == 0 else matrix_sums[i]
            found = adamw(*states[i][:3], slope, factor, rate_matrix)
            matrices.append([*found, found[0].astype(low)])
    vectors_new = [adamw(*states[i][:3], vector_sums[i - 4], factor, rate_vector) for i in range(4, 7)]
    return (
        work_output,
        work_gradient,
        gradient_norm,
        *[value for found in matrices for value in found[:3]],
        *[value for found in vectors_new for value in found],
        *[found[3] for found in matrices],
    )


def solution(mesh):
    matrix, vector = P(("dp", "seq"), None), P(("dp", "seq"))
    tokens = P("dp", "seq", None)
    states = (matrix,) * 18 + (vector,) * 3
    return jax.shard_map(
        functools.partial(per_device, mesh.shape["dp"]),
        mesh=mesh,
        in_specs=(tokens, P("dp", None), tokens) + states,
        out_specs=(tokens, tokens, P()) + states + (matrix,) * 4,
        check_vma=False,
    )
```

```python
import functools

import jax
import jax.numpy as jnp
from jax import lax
from jax.experimental import pallas as pl
from jax.experimental.pallas import tpu as pltpu
from jax.sharding import PartitionSpec as P

D = 768
HEAD_DIM = 64
STEP = 5
LANES = 128
MESH = pl.DeviceIdType.MESH

norm_epsilon = 1e-12
masked_score = -1e30
root_half = 0.7071067811865476
inv_root_tau = 0.3989422804014327
clip_limit = 1.0
decay_first = 0.9
decay_second = 0.999
adam_epsilon = 1e-08
weight_decay = 0.01
rate_matrix = 0.05
rate_vector = 0.5


def place():
    chip, core = lax.axis_index("dp"), lax.axis_index("seq")
    return chip // 4, (chip // 2) % 2, chip % 2, core


def device(z, y, x, core):
    return ((z * 2 + y) * 2 + x, core)


def signal(semaphore, target):
    pl.semaphore_signal(semaphore, inc=1, device_id=target, device_id_type=MESH)


def greet(layers, others=()):
    z, y, x, core = place()
    barrier = pltpu.get_barrier_semaphore()
    across = (device(z, y, x, 1 - core), device(z, y, 1 - x, core), device(z, 1 - y, x, core))
    for target in across + tuple(others):
        signal(barrier, target)

    @pl.when(z > 0)
    def _():
        signal(barrier, device(z - 1, y, x, core))

    @pl.when(z < layers - 1)
    def _():
        signal(barrier, device(z + 1, y, x, core))

    beside = jnp.where(z > 0, 1, 0) + jnp.where(z < layers - 1, 1, 0)
    pl.semaphore_wait(barrier, 3 + len(others) + beside)


def others_of(layers):
    z, y, x, core = place()
    line = [device((z + step) % layers, y, x, core) for step in range(1, layers)]
    plane = [
        device(
            z,
            1 - y if bits & 4 else y,
            1 - x if bits & 2 else x,
            1 - core if bits & 1 else core,
        )
        for bits in range(1, 8)
    ]
    return line, plane


def greet_line_and_plane(layers):
    barrier = pltpu.get_barrier_semaphore()
    line, plane = others_of(layers)
    for target in line + plane:
        signal(barrier, target)
    pl.semaphore_wait(barrier, len(line) + len(plane))


class Summed:
    def __init__(self, layers, line, plane, line_send, line_recv, plane_send, plane_recv):
        z, y, x, core = place()
        self.rooms = (line, plane)
        self.sems = ((line_send, line_recv), (plane_send, plane_recv))
        self.others = others_of(layers)
        at = y * 4 + x * 2 + core
        self.own = (z, at)
        self.sources = (
            [(z + layers - step) % layers for step in range(1, layers)],
            [
                (1 - y if bits & 4 else y) * 4
                + (1 - x if bits & 2 else x) * 2
                + (1 - core if bits & 1 else core)
                for bits in range(1, 8)
            ],
        )

    def copy(self, stage, which, slot):
        here = self.rooms[stage].at[slot]
        send, recv = self.sems[stage]
        return remote(here, here, send.at[which], recv.at[which], self.others[stage][which])

    def start(self, stage, value):
        self.rooms[stage][self.own[stage]] = value
        for which in range(len(self.others[stage])):
            self.copy(stage, which, self.own[stage]).start()

    def finish(self, stage):
        for which, slot in enumerate(self.sources[stage]):
            self.copy(stage, which, slot).wait_recv()
        room = self.rooms[stage]
        total = room[0]
        for slot in range(1, room.shape[0]):
            total = total + room[slot]
        return total

    def settle(self):
        for stage in range(2):
            for which in range(len(self.others[stage])):
                self.copy(stage, which, self.own[stage]).wait_send()


def remote(source, target, sent, received, to):
    return pltpu.make_async_remote_copy(
        src_ref=source,
        dst_ref=target,
        send_sem=sent,
        recv_sem=received,
        device_id=to,
        device_id_type=MESH,
    )


GATHERED = (
    ("heads", 0, 768, False),
    ("merge", 0, 768, True),
    ("small", 0, 128, True),
    ("heads", 768, 384, True),
    ("shrink", 0, 768, False),
    ("expand", 0, 3072, True),
)


def gather_kernel(
    layers,
    heads_in,
    merge_in,
    expand_in,
    shrink_in,
    small_in,
    tokens_in,
    seg_key,
    seg_query,
    weight_out,
    merge_all,
    expand_all,
    shrink_all,
    small_all,
    inputs_out,
    heads_out,
    context_out,
    vectors_out,
    heads_sent,
    merge_own,
    expand_own,
    shrink_own,
    heads_all,
    small_room,
    weight,
    tokens,
    heads_here,
    bias_row,
    bias,
    context_sent,
    context,
    pair_send,
    pair_recv,
    own_sem,
    out_sem,
    line_send,
    line_recv,
    first_send,
    first_recv,
    second_send,
    second_recv,
    core_send,
    core_recv,
    context_send,
    context_recv,
):
    z, y, x, core = place()
    partner = device(z, y, x, 1 - core)
    low, wide = jnp.bfloat16, jnp.float32
    own = {"merge": merge_own, "expand": expand_own, "shrink": shrink_own}
    full = {
        "merge": merge_all,
        "expand": expand_all,
        "shrink": shrink_all,
        "small": small_room,
        "heads": heads_all,
    }
    _, rows, length, columns = heads_here.shape
    width = columns // 3
    pairs = width // LANES

    tokens_keep = pltpu.make_async_copy(tokens_in, tokens.at[0], own_sem.at[0])
    tokens_keep.start()
    for part in range(3):
        for away in range(2):
            here = core if away == 0 else 1 - core
            start = pl.multiple_of((part * 2 + here) * width, LANES)
            block = heads_in[:, pl.ds(start, width)].astype(low)
            if away == 0:
                heads_all[z, y, x, core, :, part * width : (part + 1) * width] = block
            else:
                heads_sent[:, part * width : (part + 1) * width] = block
    small_room[z, y, x, core] = small_in[...]
    greet(layers)

    heads_pair = remote(
        heads_sent, heads_all.at[z, y, x, core], pair_send.at[0], pair_recv.at[0], partner
    )
    heads_pair.start()
    tokens_pair = remote(tokens_in, tokens.at[1], pair_send.at[1], pair_recv.at[1], partner)
    tokens_pair.start()
    merge_own[...] = merge_in[...].astype(low)
    shrink_own[...] = shrink_in[...].astype(low)
    expand_own[...] = expand_in[...].astype(low)

    def block(piece, zz, yy, xx, plane):
        name, start, wide_by, _ = GATHERED[piece]
        if name == "heads":
            return full[name].at[zz, yy, xx, :, :, pl.ds(start, wide_by)]
        return full[name].at[zz, yy, xx, plane]

    def own_block(piece):
        name = GATHERED[piece][0]
        return own[name] if name in own else block(piece, z, y, x, core)

    def couple(piece, zz, plane, moved):
        name, start, wide_by, y_first = GATHERED[piece]
        yy = y if y_first or not moved else 1 - y
        xx = x if not y_first or not moved else 1 - x
        if name == "heads":
            if y_first:
                return full[name].at[zz, :, xx, :, :, pl.ds(start, wide_by)]
            return full[name].at[zz, yy, :, :, :, pl.ds(start, wide_by)]
        if y_first:
            return full[name].at[zz, :, xx, plane]
        return full[name].at[zz, yy, :, plane]

    def across(piece, second):
        y_turn = GATHERED[piece][3] != second
        return device(z, 1 - y, x, core) if y_turn else device(z, y, 1 - x, core)

    def first_block(piece, zz):
        if GATHERED[piece][3]:
            return (zz, 1 - y, x)
        return (zz, y, 1 - x)

    def line_copy(piece, zz, source, target_z):
        return remote(
            source,
            block(piece, zz, y, x, core),
            line_send.at[piece, zz, jnp.where(target_z > z, 0, 1)],
            line_recv.at[piece, zz],
            device(target_z, y, x, core),
        )

    def first_copy(piece, zz, source):
        return remote(
            source,
            block(piece, zz, y, x, core),
            first_send.at[piece, zz],
            first_recv.at[piece, zz],
            across(piece, False),
        )

    def second_copy(piece, zz):
        both = couple(piece, zz, core, False)
        return remote(
            both, both, second_send.at[piece, zz], second_recv.at[piece, zz], across(piece, True)
        )

    def core_copy(piece, zz, stage, source, target):
        return remote(
            source,
            target,
            core_send.at[piece, zz, stage],
            core_recv.at[piece, zz, stage],
            partner,
        )

    def own_copy(piece):
        return pltpu.make_async_copy(
            own_block(piece), block(piece, z, y, x, core), own_sem.at[1 + piece]
        )

    def shared(piece):
        return GATHERED[piece][0] != "heads"

    pieces = range(len(GATHERED))
    near = [piece for piece in pieces if GATHERED[piece][0] not in own]
    far = [piece for piece in pieces if GATHERED[piece][0] in own]

    def begin_line(some):
        for piece in some:
            mine = own_block(piece)

            @pl.when(z < layers - 1)
            def _(piece=piece, mine=mine):
                line_copy(piece, z, mine, z + 1).start()

            @pl.when(z > 0)
            def _(piece=piece, mine=mine):
                line_copy(piece, z, mine, z - 1).start()

    def begin_first(some):
        for piece in some:
            mine = own_block(piece)
            first_copy(piece, z, mine).start()
            if shared(piece):
                core_copy(piece, z, 0, mine, block(piece, z, y, x, core)).start()
            if piece in far:
                own_copy(piece).start()

    def arrive_line(piece, zz, below):
        here = block(piece, zz, y, x, core)
        line_copy(piece, zz, here, z).wait_recv()
        if below:

            @pl.when(z < layers - 1)
            def _():
                line_copy(piece, zz, here, z + 1).start()

        else:

            @pl.when(z > 0)
            def _():
                line_copy(piece, zz, here, z - 1).start()

        first_copy(piece, zz, here).start()
        if shared(piece):
            core_copy(piece, zz, 0, here, here).start()

    def arrive_first(piece, zz, below):
        here = block(piece, *first_block(piece, zz), core)
        remote(
            here, here, first_send.at[piece, zz], first_recv.at[piece, zz], across(piece, False)
        ).wait_recv()
        second_copy(piece, zz).start()
        if shared(piece):
            core_copy(piece, zz, 1, here, here).start()

    def arrive_second(piece, zz, below):
        here = couple(piece, zz, core, True)
        remote(
            here, here, second_send.at[piece, zz], second_recv.at[piece, zz], across(piece, True)
        ).wait_recv()
        if shared(piece):
            core_copy(piece, zz, 2, here, here).start()

    def each(some, distance, action):
        if distance == 0:
            for piece in some:
                action(piece, z, None)
            return

        @pl.when(z - distance >= 0)
        def _():
            for piece in some:
                action(piece, z - distance, True)

        @pl.when(z + distance < layers)
        def _():
            for piece in some:
                action(piece, z + distance, False)

    def settle_core(piece, zz):
        mine = block(piece, zz, y, x, core)
        theirs = block(piece, zz, y, x, 1 - core)
        crossed = block(piece, *first_block(piece, zz), 1 - core)
        both = couple(piece, zz, 1 - core, True)
        core_copy(piece, zz, 0, mine, theirs).wait()
        core_copy(piece, zz, 1, mine, crossed).wait()
        core_copy(piece, zz, 2, both, both).wait()

    small_piece = [piece for piece in near if shared(piece)]
    heads_pieces = [piece for piece in near if not shared(piece)]
    heads_pair.wait_recv()
    begin_line(near)
    begin_first(near)
    begin_line(far)
    begin_first(far)
    for piece in far:
        own_copy(piece).wait()
    each(near, 1, arrive_line)
    each(near, 0, arrive_first)
    each(near, 2, arrive_line)
    each(near, 1, arrive_first)
    each(near, 0, arrive_second)
    each(far, 0, arrive_first)
    each(far, 1, arrive_line)
    each(near, 3, arrive_line)
    each(near, 2, arrive_first)
    each(near, 1, arrive_second)
    each(near, 3, arrive_first)
    each(near, 2, arrive_second)
    each(near, 3, arrive_second)
    for piece in small_piece:
        for zz in range(layers):
            settle_core(piece, zz)

    for zz in range(layers):
        depth = weight.shape[0] // layers
        weight[zz * depth : (zz + 1) * depth] = heads_all[zz].reshape(depth, columns)
    rows_each = small_room.shape[4] - 8
    found = small_room[...].astype(wide).reshape(-1, rows_each + 8, LANES)[:, :rows_each]
    vectors_out[...] = found.reshape(-1, LANES).T[0:8]
    bias_row[...] = jnp.zeros(bias_row.shape, wide)
    mine = pl.ds(pl.multiple_of(core * width, LANES), width)
    bias_row[:, 0:width] = vectors_out[2:3, mine]
    bias_row[:, 2 * width : 3 * width] = vectors_out[3:4, mine]
    tokens_keep.wait()
    tokens_pair.wait_recv()
    weight_copy = pltpu.make_async_copy(weight, weight_out, out_sem.at[0])
    inputs_copy = pltpu.make_async_copy(tokens, inputs_out, out_sem.at[1])
    heads_copy = pltpu.make_async_copy(heads_here, heads_out, out_sem.at[2])
    small_copy = pltpu.make_async_copy(small_room, small_all, out_sem.at[3])
    weight_copy.start()
    inputs_copy.start()
    small_copy.start()

    def project_step(step, carry):
        half, row = step // rows, step % rows
        start = pl.multiple_of(row * length, LANES)
        found = dot(tokens[half, pl.ds(start, length)], weight[...]) + bias_row[...]
        heads_here[half, row] = found.astype(low)

        @pl.when(step == 1)
        def _():
            each(far, 2, arrive_line)
            each(far, 1, arrive_first)

        @pl.when(step == 5)
        def _():
            each(far, 0, arrive_second)

        return carry

    lax.fori_loop(0, 2 * rows, project_step, 0)
    heads_copy.start()

    def context_copy(row):
        return remote(
            context_sent.at[row],
            context.at[row, :, pl.ds(pl.multiple_of(core * width, LANES), width)],
            context_send.at[row],
            context_recv.at[row],
            partner,
        )

    def attention_step(step, carry):
        row, pair = step // pairs, step % pairs

        @pl.when(pair == 0)
        def _():
            bias[...] = jnp.where(seg_key[row] == seg_query[row], 0.0, masked_score)

        def part(which):
            start = pl.multiple_of(which * width + pair * LANES, LANES)
            return heads_here[:, row, :, pl.ds(start, LANES)].reshape(2 * length, LANES)

        found = pair_forward(part(0), part(1), part(2), bias).reshape(2, length, LANES)
        context[row, :, pl.ds(pl.multiple_of(core * width + pair * LANES, LANES), LANES)] = found[0]
        context_sent[row, :, pl.ds(pl.multiple_of(pair * LANES, LANES), LANES)] = found[1]

        @pl.when(pair == pairs - 1)
        def _():
            context_copy(row).start()

        @pl.when(step == 0)
        def _():
            each(far, 3, arrive_line)
            each(far, 2, arrive_first)

        @pl.when(step == 3)
        def _():
            each(far, 1, arrive_second)

        @pl.when(step == 6)
        def _():
            each(far, 3, arrive_first)
            each(far, 2, arrive_second)

        return carry

    lax.fori_loop(0, rows * pairs, attention_step, 0)
    for row in range(rows):
        other = pl.ds(pl.multiple_of((1 - core) * width, LANES), width)
        remote(
            context_sent.at[row],
            context.at[row, :, other],
            context_send.at[row],
            context_recv.at[row],
            partner,
        ).wait()
    context_keep = pltpu.make_async_copy(context, context_out, out_sem.at[4])
    context_keep.start()
    each(far, 3, arrive_second)

    heads_pair.wait_send()
    tokens_pair.wait_send()

    def settle(zz, carry):
        for piece in pieces:
            here = block(piece, zz, y, x, core)
            first_copy(piece, zz, here).wait_send()
            second_copy(piece, zz).wait_send()
            if piece in far:
                settle_core(piece, zz)

            @pl.when(jnp.logical_and(z < layers - 1, zz <= z))
            def _(piece=piece, here=here):
                line_copy(piece, zz, here, z + 1).wait_send()

            @pl.when(jnp.logical_and(z > 0, zz >= z))
            def _(piece=piece, here=here):
                line_copy(piece, zz, here, z - 1).wait_send()

        return carry

    lax.fori_loop(0, layers, settle, 0)
    for copy in (weight_copy, inputs_copy, heads_copy, small_copy, context_keep):
        copy.wait()


def gather_attend(layers, heads, merge, expand, shrink, small, tokens, seg_key, seg_query):
    chips = (layers, 2, 2, 2)
    low, wide = jnp.bfloat16, jnp.float32
    count = len(GATHERED)
    sems = pltpu.SemaphoreType.DMA
    row_count, both = seg_query.shape[0], seg_query.shape[2]
    length, columns = both // 2, heads.shape[1] // 2
    rows = chips + (heads.shape[0], columns)
    depth = tokens.shape[1]
    here = (2, row_count, length, columns)
    vmem, anywhere = pl.BlockSpec(memory_space=pltpu.VMEM), pl.BlockSpec(memory_space=pl.ANY)
    return pl.pallas_call(
        functools.partial(gather_kernel, layers),
        out_shape=[
            jax.ShapeDtypeStruct((depth, columns), low),
            *[jax.ShapeDtypeStruct(chips + part.shape, low) for part in (merge, expand, shrink, small)],
            jax.ShapeDtypeStruct((2,) + tokens.shape, low),
            jax.ShapeDtypeStruct(here, low),
            jax.ShapeDtypeStruct((row_count, length, depth), low),
            jax.ShapeDtypeStruct((8, depth), wide),
        ],
        in_specs=[vmem] * 5 + [anywhere, vmem, vmem],
        out_specs=[anywhere] * 8 + [vmem],
        scratch_shapes=[
            pltpu.VMEM((heads.shape[0], columns), low),
            pltpu.VMEM(merge.shape, low),
            pltpu.VMEM(expand.shape, low),
            pltpu.VMEM(shrink.shape, low),
            pltpu.VMEM(rows, low),
            pltpu.VMEM(chips + small.shape, low),
            pltpu.VMEM((depth, columns), low),
            pltpu.VMEM((2,) + tokens.shape, low),
            pltpu.VMEM(here, low),
            pltpu.VMEM((1, columns), wide),
            pltpu.VMEM((both, both), wide),
            pltpu.VMEM((row_count, length, columns // 3), low),
            pltpu.VMEM((row_count, length, depth), low),
            sems((2,)),
            sems((2,)),
            sems((1 + count,)),
            sems((5,)),
            sems((count, layers, 2)),
            sems((count, layers)),
            sems((count, layers)),
            sems((count, layers)),
            sems((count, layers)),
            sems((count, layers)),
            sems((count, layers, 3)),
            sems((count, layers, 3)),
            sems((row_count,)),
            sems((row_count,)),
        ],
        compiler_params=pltpu.CompilerParams(
            collective_id=0, has_side_effects=True, vmem_limit_bytes=63 * 2**20
        ),
        name="gather_attend",
    )(heads, merge, expand, shrink, small, tokens, seg_key, seg_query)


SCATTERED = (
    ("shrink", 0, 768, False),
    ("expand", 0, 3072, True),
    ("merge", 0, 768, True),
    ("heads", 0, 768, False),
    ("heads", 768, 384, True),
)


def finish_kernel(
    layers,
    heads_ref,
    upstream_ref,
    seg_key,
    seg_query,
    inputs_ref,
    weight_ref,
    merge_in,
    expand_in,
    shrink_in,
    small_in,
    heads_out,
    merge_out,
    expand_out,
    shrink_out,
    small_out,
    square_out,
    tokens_out,
    heads_here,
    upstream_here,
    heads_grad,
    inputs_here,
    weight_here,
    bias,
    tokens_sent,
    tokens_room,
    totals,
    core_rooms,
    first_rooms,
    second_rooms,
    line_rooms,
    heads_last,
    heads_room,
    small_line,
    small_plane,
    square_line,
    square_plane,
    bring_sem,
    upstream_send,
    upstream_recv,
    tokens_send,
    tokens_recv,
    load_sem,
    core_send,
    core_recv,
    first_send,
    first_recv,
    second_send,
    second_recv,
    line_send,
    line_recv,
    last_send,
    last_recv,
    small_sems,
    square_sems,
):
    z, y, x, core = place()
    partner = device(z, y, x, 1 - core)
    sources = {"merge": merge_in, "expand": expand_in, "shrink": shrink_in}
    results = {"merge": merge_out, "expand": expand_out, "shrink": shrink_out}
    small_sum = Summed(layers, small_line, small_plane, *small_sems)
    square_sum = Summed(layers, square_line, square_plane, *square_sems)
    low, wide = jnp.bfloat16, jnp.float32
    _, rows, length, columns = heads_here.shape
    width = columns // 3
    pairs = width // LANES

    def bring_row(row):
        return pltpu.make_async_copy(heads_ref.at[:, row], heads_here.at[:, row], bring_sem.at[row])

    def columns_of(plane):
        return pl.ds(pl.multiple_of(plane * width, LANES), width)

    def upstream_keep(row):
        return pltpu.make_async_copy(
            upstream_ref.at[row, :, columns_of(core)], upstream_here.at[0, row], bring_sem.at[4 + row]
        )

    def upstream_copy(row):
        return remote(
            upstream_ref.at[row, :, columns_of(1 - core)],
            upstream_here.at[1, row],
            upstream_send.at[row],
            upstream_recv.at[row],
            partner,
        )

    bring_inputs = pltpu.make_async_copy(inputs_ref, inputs_here, bring_sem.at[8])
    bring_weight = pltpu.make_async_copy(weight_ref, weight_here, bring_sem.at[9])
    for row in range(rows):
        bring_row(row).start()
        upstream_keep(row).start()

    greet_line_and_plane(layers)
    for row in range(rows):
        upstream_copy(row).start()

    pieces = range(len(SCATTERED))
    early = [piece for piece in pieces if SCATTERED[piece][0] != "heads"]
    late = [piece for piece in pieces if SCATTERED[piece][0] == "heads"]

    def is_heads(piece):
        return SCATTERED[piece][0] == "heads"

    def y_first(piece):
        return SCATTERED[piece][3]

    def load(piece, zz):
        return pltpu.make_async_copy(
            sources[SCATTERED[piece][0]].at[zz, :, :, core], totals[piece].at[zz], load_sem.at[piece, zz]
        )

    def core_copy(piece, zz):
        return remote(
            sources[SCATTERED[piece][0]].at[zz, :, :, 1 - core],
            core_rooms[piece].at[zz],
            core_send.at[piece, zz],
            core_recv.at[piece, zz],
            partner,
        )

    def first_copy(piece, zz):
        if y_first(piece):
            source, to = totals[piece].at[zz, 1 - y], device(z, 1 - y, x, core)
        else:
            source, to = totals[piece].at[zz, :, 1 - x], device(z, y, 1 - x, core)
        return remote(
            source, first_rooms[piece].at[zz], first_send.at[piece, zz], first_recv.at[piece, zz], to
        )

    def second_copy(piece, zz):
        if y_first(piece):
            source, to = totals[piece].at[zz, y, 1 - x], device(z, y, 1 - x, core)
        else:
            source, to = totals[piece].at[zz, 1 - y, x], device(z, 1 - y, x, core)
        return remote(
            source,
            second_rooms[piece].at[zz],
            second_send.at[piece, zz],
            second_recv.at[piece, zz],
            to,
        )

    def line_copy(piece, zz, downward):
        to = z - 1 if downward else z + 1
        return remote(
            totals[piece].at[zz, y, x],
            line_rooms[piece].at[downward, zz],
            line_send.at[piece, zz],
            line_recv.at[piece, downward, zz],
            device(to, y, x, core),
        )

    def add(target, room):
        target[...] = (target[...].astype(wide) + room[...].astype(wide)).astype(low)

    def layer_of(step):
        upward = jnp.where(z < layers // 2, 1, 0)
        turned = jnp.where(jnp.logical_and(step >= 2, jnp.logical_or(z == 1, z == 2)), 5 - step, step)
        return jnp.where(upward == 1, layers - 1 - turned, turned)

    def on_first(piece, zz):
        if not is_heads(piece):
            load(piece, zz).wait()
            core_copy(piece, zz).wait_recv()

            def merge_one(index, carry):
                add(
                    totals[piece].at[zz, index // 2, index % 2],
                    core_rooms[piece].at[zz, index // 2, index % 2],
                )
                return carry

            lax.fori_loop(0, 4, merge_one, 0)
        first_copy(piece, zz).start()

    def on_second(piece, zz):
        first_copy(piece, zz).wait_recv()

        def merge_one(index, carry):
            if y_first(piece):
                target = totals[piece].at[zz, y, index]
            else:
                target = totals[piece].at[zz, index, x]
            add(target, first_rooms[piece].at[zz, index])
            return carry

        lax.fori_loop(0, 2, merge_one, 0)
        second_copy(piece, zz).start()

    def on_line(piece, zz):
        second_copy(piece, zz).wait_recv()
        mine = totals[piece].at[zz, y, x]
        add(mine, second_rooms[piece].at[zz])

        @pl.when(zz > z)
        def _():
            @pl.when(z > 0)
            def _():
                line_copy(piece, zz, 0).wait_recv()
                add(mine, line_rooms[piece].at[0, zz])

            line_copy(piece, zz, 0).start()

        @pl.when(zz < z)
        def _():
            @pl.when(z < layers - 1)
            def _():
                line_copy(piece, zz, 1).wait_recv()
                add(mine, line_rooms[piece].at[1, zz])

            line_copy(piece, zz, 1).start()

    def start_early(step, carry):
        for piece in early:
            core_copy(piece, layer_of(step)).start()
            load(piece, layer_of(step)).start()
        return carry

    lax.fori_loop(0, layers, start_early, 0)
    bring_inputs.start()
    bring_weight.start()

    scale = HEAD_DIM**-0.5

    def attention_step(step, carry):
        row, pair = step // pairs, step % pairs

        @pl.when(pair == 0)
        def _():
            bring_row(row).wait()
            upstream_keep(row).wait()
            upstream_copy(row).wait_recv()
            bias[...] = jnp.where(seg_key[row] == seg_query[row], 0.0, masked_score)

        def part(which):
            start = pl.multiple_of(which * width + pair * LANES, LANES)
            return heads_here[:, row, :, pl.ds(start, LANES)].reshape(2 * length, LANES)

        at = pl.multiple_of(pair * LANES, LANES)
        upstream = upstream_here[:, row, :, pl.ds(at, LANES)].reshape(2 * length, LANES)
        grads = pair_back(part(0), part(1), part(2), upstream, bias)
        for which in range(3):
            start = pl.multiple_of(which * width + pair * LANES, LANES)
            heads_grad[:, row, :, pl.ds(start, LANES)] = grads[which].reshape(2, length, LANES)

        @pl.when(jnp.logical_and(step >= 4, step % 3 == 1))
        def _():
            for piece in early:
                on_second(piece, layer_of((step - 4) // 3))

        @pl.when(jnp.logical_or(step == 0, jnp.logical_and(step < 9, step % 3 == 1)))
        def _():
            for piece in early:
                on_first(piece, layer_of((step + 2) // 3))

        @pl.when(jnp.logical_or(step == 9, step == 11))
        def _():
            for piece in early:
                on_line(piece, layer_of((step - 9) // 2))

        return carry

    lax.fori_loop(0, rows * pairs, attention_step, 0)

    bring_inputs.wait()
    flat_grad = heads_grad[...].reshape(2 * rows * length, columns)
    ones = jnp.ones((8, 2 * rows * length), low)
    sums = dot(ones, flat_grad)
    small_out[...] = small_in[...]
    small_out[2:3, columns_of(core)] = sums[0:1, 0:width]
    small_out[3:4, columns_of(core)] = sums[0:1, 2 * width : 3 * width]
    small_sum.start(0, small_out[...])
    depth = inputs_here.shape[1] // 2

    def weight_step(turn, carry):
        step = jnp.where(z < layers // 2, 1 - turn, turn)
        start = pl.multiple_of(step * depth, LANES)
        found = dot(inputs_here[:, pl.ds(start, depth)], flat_grad, (((0,), (0,)), ((), ())))
        for piece in late:
            _, first, wide_by, _ = SCATTERED[piece]
            block = found[:, first : first + wide_by]
            block = block.reshape((layers // 2,) + totals[piece].shape[1:]).astype(low)
            totals[piece][pl.ds(step * (layers // 2), layers // 2)] = block

        @pl.when(turn == 0)
        def _():
            for piece in early:
                on_second(piece, layer_of(layers - 1))

        for which in range(layers // 2):
            for piece in late:
                on_first(piece, layer_of(turn * (layers // 2) + which))
        return carry

    lax.fori_loop(0, 2, weight_step, 0)

    bring_weight.wait()

    def tokens_copy(row):
        return remote(
            tokens_sent.at[row], tokens_room.at[row], tokens_send.at[row], tokens_recv.at[row], partner
        )

    def other_step(row, carry):
        tokens_sent[row] = dot(heads_grad[1, row], weight_here[...], FAR).astype(low)
        tokens_copy(row).start()

        @pl.when(row >= 1)
        def _():
            for piece in late:
                on_second(piece, layer_of(row - 1))

        @pl.when(row % 2 == 0)
        def _():
            for piece in early:
                on_line(piece, layer_of(2 + row // 2))

        @pl.when(row == 2)
        def _():
            small_sum.start(1, small_sum.finish(0))

        return carry

    def own_step(row, carry):
        found = dot(heads_grad[0, row], weight_here[...], FAR)
        tokens_copy(row).wait_recv()
        tokens_out[row] = found + tokens_room[row].astype(wide)

        @pl.when(row == 0)
        def _():
            for piece in late:
                on_second(piece, layer_of(layers - 1))

        for piece in late:
            on_line(piece, layer_of(row))
        return carry

    lax.fori_loop(0, rows, other_step, 0)
    lax.fori_loop(0, rows, own_step, 0)
    small_out[...] = small_sum.finish(1)

    def squares(value):
        by_row = jnp.sum((value * value).reshape(value.shape[0] // 8, 8, value.shape[1]), axis=0)
        total = by_row[:, 0:LANES]
        for start in range(LANES, value.shape[1], LANES):
            total = total + by_row[:, start : start + LANES]
        return total

    def last_copy(piece):
        _, start, wide_by, _ = SCATTERED[piece]
        return remote(
            heads_last.at[:, pl.ds(start, wide_by)],
            heads_room.at[:, pl.ds(start, wide_by)],
            last_send.at[piece],
            last_recv.at[piece],
            partner,
        )

    found_squares = jnp.zeros((8, LANES), wide)
    for piece in early + late:
        name, start, wide_by, _ = SCATTERED[piece]
        mine = totals[piece].at[z, y, x]

        @pl.when(z > 0)
        def _(piece=piece, mine=mine):
            line_copy(piece, z, 0).wait_recv()
            add(mine, line_rooms[piece].at[0, z])

        @pl.when(z < layers - 1)
        def _(piece=piece, mine=mine):
            line_copy(piece, z, 1).wait_recv()
            add(mine, line_rooms[piece].at[1, z])

        if is_heads(piece):
            heads_last[:, start : start + wide_by] = mine[1 - core]
            last_copy(piece).start()
            kept = mine[core].astype(wide)
            heads_out[core, :, start : start + wide_by] = kept
        else:
            kept = mine[...].astype(wide)
            results[name][...] = kept
        found_squares = found_squares + squares(kept)
    for piece in late:
        _, start, wide_by, _ = SCATTERED[piece]
        last_copy(piece).wait_recv()
        theirs = heads_room[:, start : start + wide_by].astype(wide)
        heads_out[1 - core, :, start : start + wide_by] = theirs
        found_squares = found_squares + squares(theirs)

    square_sum.start(0, found_squares)
    square_sum.start(1, square_sum.finish(0))
    square_out[...] = square_sum.finish(1)

    small_sum.settle()
    square_sum.settle()
    for row in range(rows):
        upstream_copy(row).wait_send()
        tokens_copy(row).wait_send()

    def settle(zz, carry):
        for piece in pieces:
            if not is_heads(piece):
                core_copy(piece, zz).wait_send()
            first_copy(piece, zz).wait_send()
            second_copy(piece, zz).wait_send()

            @pl.when(zz > z)
            def _(piece=piece):
                line_copy(piece, zz, 0).wait_send()

            @pl.when(zz < z)
            def _(piece=piece):
                line_copy(piece, zz, 1).wait_send()

        return carry

    lax.fori_loop(0, layers, settle, 0)
    for piece in late:
        last_copy(piece).wait_send()


def finish_all(layers, heads, upstream, seg_key, seg_query, inputs, weight, merge, expand, shrink, small):
    low, wide = jnp.bfloat16, jnp.float32
    block_rows = merge.shape[4]
    _, rows, length, columns = heads.shape
    width = columns // 3
    sums_rows = {"merge": block_rows, "expand": block_rows, "shrink": shrink.shape[4]}
    sems = pltpu.SemaphoreType.DMA

    def rooms(*lead, some=SCATTERED):
        return [
            pltpu.VMEM(
                tuple(lead)
                + ((2, block_rows, wide_by) if name == "heads" else (sums_rows[name], wide_by)),
                low,
            )
            for name, _, wide_by, _ in some
        ]

    count = len(SCATTERED)
    early = [piece for piece in SCATTERED if piece[0] != "heads"]
    vmem, anywhere = pl.BlockSpec(memory_space=pltpu.VMEM), pl.BlockSpec(memory_space=pl.ANY)
    return pl.pallas_call(
        functools.partial(finish_kernel, layers),
        out_shape=[
            jax.ShapeDtypeStruct((2, block_rows, columns), wide),
            *[jax.ShapeDtypeStruct(part.shape[4:], wide) for part in (merge, expand, shrink)],
            jax.ShapeDtypeStruct(small.shape, wide),
            jax.ShapeDtypeStruct((8, LANES), wide),
            jax.ShapeDtypeStruct((rows, length, inputs.shape[1]), wide),
        ],
        in_specs=[anywhere, anywhere, vmem, vmem] + [anywhere] * 5 + [vmem],
        out_specs=[vmem] * 7,
        scratch_shapes=[
            pltpu.VMEM(heads.shape, low),
            pltpu.VMEM((2, rows, length, width), low),
            pltpu.VMEM(heads.shape, low),
            pltpu.VMEM(inputs.shape, low),
            pltpu.VMEM(weight.shape, low),
            pltpu.VMEM((2 * length, 2 * length), wide),
            pltpu.VMEM((rows, length, inputs.shape[1]), low),
            pltpu.VMEM((rows, length, inputs.shape[1]), low),
            rooms(layers, 2, 2),
            rooms(layers, 2, 2, some=early),
            rooms(layers, 2),
            rooms(layers),
            rooms(2, layers),
            pltpu.VMEM((block_rows, columns), low),
            pltpu.VMEM((block_rows, columns), low),
            pltpu.VMEM((layers,) + small.shape, wide),
            pltpu.VMEM((8,) + small.shape, wide),
            pltpu.VMEM((layers, 8, LANES), wide),
            pltpu.VMEM((8, 8, LANES), wide),
            sems((10,)),
            sems((rows,)),
            sems((rows,)),
            sems((rows,)),
            sems((rows,)),
            sems((count, layers)),
            sems((count, layers)),
            sems((count, layers)),
            sems((count, layers)),
            sems((count, layers)),
            sems((count, layers)),
            sems((count, layers)),
            sems((count, layers)),
            sems((count, 2, layers)),
            sems((count,)),
            sems((count,)),
            [sems((layers - 1,)), sems((layers - 1,)), sems((7,)), sems((7,))],
            [sems((layers - 1,)), sems((layers - 1,)), sems((7,)), sems((7,))],
        ],
        compiler_params=pltpu.CompilerParams(
            collective_id=1, has_side_effects=True, vmem_limit_bytes=63 * 2**20
        ),
        name="finish_all",
    )(heads, upstream, seg_key, seg_query, inputs, weight, merge, expand, shrink, small)


def update_kernel(squares, small, *refs):
    count = len(refs) // 8
    total = jnp.sum(squares[...], keepdims=True) + jnp.sum(small[...] * small[...], keepdims=True)
    norm = jnp.sqrt(total)
    factor = jnp.minimum(1.0, clip_limit / norm)
    refs[-1][...] = norm
    for which in range(count):
        gradient, weight, moment, square = (refs[which * 4 + i] for i in range(4))
        outs = refs[count * 4 + which * 4 : count * 4 + which * 4 + 4]
        half = weight.shape[1] // 6
        if len(gradient.shape) == 3:
            spans = [
                (slice((part * 2 + core) * half, (part * 2 + core + 1) * half), part, core)
                for part in range(3)
                for core in range(2)
            ]
        else:
            spans = [(slice(0, weight.shape[1]), None, None)]
        for span, part, core in spans:
            if part is None:
                slope = gradient[...]
            else:
                slope = gradient[core, :, part * half : (part + 1) * half]
            updated, first, second = adamw(
                weight[:, span], moment[:, span], square[:, span], slope, factor, rate_matrix
            )
            outs[0][:, span] = updated
            outs[1][:, span] = first
            outs[2][:, span] = second
            outs[3][:, span] = updated.astype(jnp.bfloat16)


def update_all(squares, small, states):
    whole = pl.BlockSpec(memory_space=pltpu.VMEM)
    flat = [part for state in states for part in state]
    shapes = []
    for state in states:
        shapes += [jax.ShapeDtypeStruct(state[1].shape, jnp.float32)] * 3
        shapes += [jax.ShapeDtypeStruct(state[1].shape, jnp.bfloat16)]
    shapes.append(jax.ShapeDtypeStruct((1, 1), jnp.float32))
    found = pl.pallas_call(
        update_kernel,
        out_shape=shapes,
        in_specs=[whole] * (2 + len(flat)),
        out_specs=[whole] * len(shapes),
        name="update_all",
    )(squares, small, *flat)
    return [found[4 * which : 4 * which + 4] for which in range(len(states))], found[-1][0, 0]


FAR = (((1,), (1,)), ((), ()))
NEAR = (((1,), (0,)), ((), ()))


def dot(left, right, dims=NEAR):
    return lax.dot_general(left, right, dims, preferred_element_type=jnp.float32)


def write_bias(bias, seg_key, seg_query):
    @pl.when(pl.program_id(1) == 0)
    def _():
        bias[...] = jnp.where(seg_key[0] == seg_query[0], 0.0, masked_score)


def both_halves(ref):
    halves, rows, length, lanes = ref.shape
    return ref[...].reshape(halves * rows * length, lanes)


def only_head(head, value):
    lane = lax.broadcasted_iota(jnp.int32, value.shape, 1)
    return jnp.where((lane // HEAD_DIM) == head, value, jnp.zeros_like(value))


def softmax_of(keys, query, bias):
    scores = dot(keys, query, FAR) + bias[...]
    unscaled = jnp.exp(scores - jnp.max(scores, axis=0, keepdims=True))
    return unscaled * (1.0 / jnp.sum(unscaled, axis=0, keepdims=True))


def pair_forward(query, keys, values, bias):
    query = query * jnp.asarray(HEAD_DIM**-0.5, jnp.bfloat16)
    flipped = values.T
    found = []
    for head in range(2):
        weights = softmax_of(keys, only_head(head, query), bias).astype(jnp.bfloat16)
        found.append(dot(flipped[head * HEAD_DIM : (head + 1) * HEAD_DIM], weights))
    return jnp.concatenate(found, axis=0).T.astype(jnp.bfloat16)


def attend_kernel(query_ref, key_ref, value_ref, seg_key, seg_query, out_ref, bias):
    write_bias(bias, seg_key, seg_query)
    refs = (query_ref, key_ref, value_ref)
    context = pair_forward(*[both_halves(ref) for ref in refs], bias)
    out_ref[...] = context.reshape(out_ref.shape)


def pair_back(query, keys, values, upstream, bias):
    scale = HEAD_DIM**-0.5
    query = query * jnp.asarray(scale, jnp.bfloat16)
    flipped = keys.T
    found_query, found_key, found_value = [], [], []
    for head in range(2):
        weights = softmax_of(keys, only_head(head, query), bias)
        grad_weights = dot(only_head(head, values), upstream, FAR)
        inner = jnp.sum(weights * grad_weights, axis=0, keepdims=True)
        grad_scores = (weights * (grad_weights - inner)).astype(jnp.bfloat16)
        found_value.append(dot(weights.astype(jnp.bfloat16), upstream))
        found_key.append(dot(grad_scores, query))
        found_query.append(dot(flipped[head * HEAD_DIM : (head + 1) * HEAD_DIM], grad_scores))
    lane = lax.broadcasted_iota(jnp.int32, found_key[0].shape, 1)
    return (
        (jnp.concatenate(found_query, axis=0).T * scale).astype(jnp.bfloat16),
        jnp.where(lane < HEAD_DIM, found_key[0], found_key[1]).astype(jnp.bfloat16),
        jnp.where(lane < HEAD_DIM, found_value[0], found_value[1]).astype(jnp.bfloat16),
    )


def attend_back_kernel(
    query_ref, key_ref, value_ref, upstream_ref, seg_key, seg_query, out_ref, bias
):
    write_bias(bias, seg_key, seg_query)
    refs = (query_ref, key_ref, value_ref, upstream_ref)
    grads = pair_back(*[both_halves(ref) for ref in refs], bias)
    width = out_ref.shape[3] // 3
    for which in range(3):
        start = pl.multiple_of(pl.program_id(1) * LANES + which * width, LANES)
        out_ref[:, :, :, pl.ds(start, LANES)] = grads[which].reshape(query_ref.shape)


def head_block(length, first):
    return pl.BlockSpec((2, 1, length, LANES), lambda row, pair: (0, row, 0, first + pair))


def attention_specs(rows, length):
    return [
        pl.BlockSpec((1, 2 * length, 1), lambda row, pair: (row, 0, 0)),
        pl.BlockSpec((1, 1, 2 * length), lambda row, pair: (row, 0, 0)),
    ]


def attend(heads, seg_key, seg_query):
    _, rows, length, columns = heads.shape
    width = columns // 3
    pairs = width // LANES
    flops = 4 * rows * width * (2 * length) ** 2
    return pl.pallas_call(
        attend_kernel,
        grid=(rows, pairs),
        out_shape=jax.ShapeDtypeStruct((2, rows, length, width), jnp.bfloat16),
        in_specs=[
            head_block(length, 0),
            head_block(length, pairs),
            head_block(length, 2 * pairs),
            *attention_specs(rows, length),
        ],
        out_specs=head_block(length, 0),
        scratch_shapes=[pltpu.VMEM((2 * length, 2 * length), jnp.float32)],
        cost_estimate=pl.CostEstimate(
            flops=flops, bytes_accessed=8 * heads.size // 3, transcendentals=flops // 256
        ),
        name="attend",
    )(heads, heads, heads, seg_key, seg_query)


def attend_back(heads, upstream, seg_key, seg_query):
    _, rows, length, columns = heads.shape
    width = columns // 3
    pairs = width // LANES
    flops = 10 * rows * width * (2 * length) ** 2
    return pl.pallas_call(
        attend_back_kernel,
        grid=(rows, pairs),
        out_shape=jax.ShapeDtypeStruct(heads.shape, jnp.bfloat16),
        in_specs=[
            head_block(length, 0),
            head_block(length, pairs),
            head_block(length, 2 * pairs),
            head_block(length, 0),
            *attention_specs(rows, length),
        ],
        out_specs=pl.BlockSpec((2, 1, length, columns), lambda row, pair: (0, row, 0, 0)),
        scratch_shapes=[pltpu.VMEM((2 * length, 2 * length), jnp.float32)],
        cost_estimate=pl.CostEstimate(
            flops=flops, bytes_accessed=14 * heads.size // 3, transcendentals=flops // 640
        ),
        name="attend_back",
    )(heads, heads, heads, upstream, seg_key, seg_query)


def normalize(hidden):
    center = hidden - jnp.mean(hidden, axis=-1, keepdims=True)
    inverse_scale = lax.rsqrt(jnp.mean(center * center, axis=-1, keepdims=True) + norm_epsilon)
    return (center * inverse_scale, inverse_scale)


def norm_back(upstream, normed, inverse_scale):
    mean_upstream = jnp.mean(upstream, axis=-1, keepdims=True)
    mean_cross = jnp.mean(upstream * normed, axis=-1, keepdims=True)
    return inverse_scale * (upstream - mean_upstream - normed * mean_cross)


def gelu_value(inputs):
    return 0.5 * inputs * (1.0 + lax.erf(inputs * root_half))


def gelu_slope(inputs):
    return (
        0.5 * (1.0 + lax.erf(inputs * root_half))
        + inputs * jnp.exp(-0.5 * inputs * inputs) * inv_root_tau
    )


def cross_rows(operand_left, operand_right):
    return lax.dot_general(
        operand_left, operand_right, (((0,), (0,)), ((), ())), preferred_element_type=jnp.float32
    )


def cross_cols(operand_left, operand_right):
    return dot(operand_left, operand_right, FAR)


def adamw(weight, moment, square, gradient, factor, step_rate):
    clipped = gradient * factor
    moment_new = decay_first * moment + (1.0 - decay_first) * clipped
    square_new = decay_second * square + (1.0 - decay_second) * clipped * clipped
    corrected = (
        moment_new
        / (1.0 - decay_first**STEP)
        / (jnp.sqrt(square_new / (1.0 - decay_second**STEP)) + adam_epsilon)
    )
    return (weight - step_rate * (corrected + weight_decay * weight), moment_new, square_new)


def swap_cores(value):
    return lax.ppermute(value, "seq", [(0, 1), (1, 0)])


def gather_plain(heads, merge, expand, shrink, small, tokens):
    core = lax.axis_index("seq")

    def full(part):
        return lax.all_gather(part, ("dp", "seq"), axis=0, tiled=False)

    mine = lax.dynamic_index_in_dim(full(heads), core, 1, keepdims=False)
    return [mine, *map(full, (merge, expand, shrink, small)), jnp.stack([tokens, swap_cores(tokens)])]


def scatter_plain(heads, merge, expand, shrink, small):
    def sums(part):
        flat = part.astype(jnp.float32).reshape((-1,) + part.shape[-2:])
        return lax.psum_scatter(flat, ("dp", "seq"), scatter_dimension=0, tiled=False)

    own = heads.astype(jnp.float32).reshape((-1, 2) + heads.shape[-2:])
    own = lax.psum_scatter(own, "dp", scatter_dimension=0, tiled=False)
    own = lax.all_to_all(own, "seq", split_axis=0, concat_axis=0, tiled=True)
    reduced = [own, *map(sums, (merge, expand, shrink))]
    squares = lax.psum(sum(jnp.sum(part * part) for part in reduced), ("dp", "seq"))
    return [*reduced, lax.psum(small, ("dp", "seq")), squares]


def per_device(
    chips,
    layer_input,
    segment_ids,
    cotangent,
    heads_weight,
    heads_first,
    heads_second,
    merge_weight,
    merge_first,
    merge_second,
    expand_weight,
    expand_first,
    expand_second,
    shrink_weight,
    shrink_first,
    shrink_second,
    norm_gains,
    gains_first,
    gains_second,
    branch_bias,
    branch_first,
    branch_second,
    hidden_bias,
    hidden_first,
    hidden_second,
):
    low, wide = jnp.bfloat16, jnp.float32
    core = lax.axis_index("seq")
    index = lax.axis_index("dp") * 2 + core
    row_count, length = layer_input.shape[:2]
    rows = heads_weight.shape[0]
    devices = chips * 2
    hidden_rows = shrink_weight.shape[0]
    half = D // 2
    flat_input = layer_input.reshape(-1, D)
    tokens = flat_input.shape[0]
    kernels = rows % 8 == 0 and chips == 16
    block = (chips // 4, 2, 2, 2) if kernels else (devices,)

    small_rows = -(-rows // 8) * 8 + 8
    small_part = jnp.concatenate([norm_gains, branch_bias, jnp.zeros((rows, LANES - 8), wide)], axis=1)
    bottom = jnp.pad(hidden_bias[None], ((0, small_rows - rows - 1), (0, LANES - hidden_rows)))
    small_part = jnp.concatenate([small_part, bottom], axis=0).astype(low)
    seg_own = lax.dynamic_slice(segment_ids, (0, core * length), (row_count, length))
    seg_other = lax.dynamic_slice(segment_ids, (0, (1 - core) * length), (row_count, length))
    seg_here = jnp.concatenate([seg_own, seg_other], axis=1)
    seg_key, seg_query = seg_here[:, :, None], seg_here[:, None, :]

    if kernels:
        heads_low, merge_all, expand_all, shrink_all, small_all, inputs_all, heads_here, *found = gather_attend(
            chips // 4,
            heads_weight,
            merge_weight,
            expand_weight,
            shrink_weight,
            small_part,
            flat_input,
            seg_key,
            seg_query,
        )
        flat_context, vectors = found[0].reshape(tokens, D), found[1]
    else:
        heads_parts = heads_weight.astype(low).reshape(rows, 3, 2, half)
        heads_parts = heads_parts.transpose(2, 0, 1, 3).reshape(2, rows, 3 * half)
        heads_all, merge_all, expand_all, shrink_all, small_all, inputs_all = gather_plain(
            heads_parts,
            merge_weight.astype(low),
            expand_weight.astype(low),
            shrink_weight.astype(low),
            small_part,
            flat_input,
        )
        heads_low = heads_all.reshape(D, 3 * half)
    merge_low = merge_all.reshape(D, D)
    expand_low = expand_all.reshape(D, -1)
    shrink_low = shrink_all.reshape(-1, D)
    small_all = small_all.reshape(devices, small_rows, LANES).astype(wide)
    hidden_full = small_all[:, rows, :hidden_rows].reshape(-1)
    inputs_both = inputs_all.reshape(2 * tokens, D)
    if not kernels:
        vectors = small_all[:, :rows, :8].reshape(D, 8).T
        heads_bias = jnp.concatenate(
            [
                lax.dynamic_slice(vectors[2], (core * half,), (half,)),
                jnp.zeros((half,), wide),
                lax.dynamic_slice(vectors[3], (core * half,), (half,)),
            ]
        )
        projected = (dot(inputs_both, heads_low) + heads_bias).astype(low)
        heads_here = projected.reshape(2, row_count, length, 3 * half)
        context_here = attend(heads_here, seg_key, seg_query).reshape(2, tokens, half)
        context_other = swap_cores(context_here[1])
        first_heads = jnp.where(core == 0, context_here[0], context_other)
        last_heads = jnp.where(core == 0, context_other, context_here[0])
        flat_context = jnp.concatenate([first_heads, last_heads], axis=1)
    gain_one, gain_two = vectors[0], vectors[1]
    attended = dot(flat_context, merge_low) + vectors[4]
    normed_one, inverse_one = normalize(flat_input.astype(wide) + attended)
    first_low = (normed_one * gain_one + vectors[5]).astype(low)
    pre_active = dot(first_low, expand_low) + hidden_full
    active_low = gelu_value(pre_active).astype(low)
    branch_out = dot(active_low, shrink_low) + vectors[6]
    normed_two, inverse_two = normalize(first_low.astype(wide) + branch_out)
    work_output = (normed_two * gain_two + vectors[7]).astype(low).reshape(layer_input.shape)

    upstream = cotangent.reshape(-1, D).astype(wide)
    grad_gain_two = jnp.sum(upstream * normed_two, axis=0)
    grad_shift_two = jnp.sum(upstream, axis=0)
    grad_second = norm_back(upstream * gain_two, normed_two, inverse_two)
    branch_grad = grad_second.astype(low)
    grad_shrink = cross_rows(active_low, branch_grad).astype(low)
    grad_shrink_bias = jnp.sum(branch_grad.astype(wide), axis=0)
    active_grad = (cross_cols(branch_grad, shrink_low) * gelu_slope(pre_active)).astype(low)
    grad_expand = cross_rows(first_low, active_grad).astype(low)
    grad_hidden = jnp.sum(active_grad.astype(wide), axis=0)
    grad_first = grad_second + cross_cols(active_grad, expand_low)
    grad_gain_one = jnp.sum(grad_first * normed_one, axis=0)
    grad_shift_one = jnp.sum(grad_first, axis=0)
    grad_sum_one = norm_back(grad_first * gain_one, normed_one, inverse_one)
    attended_grad = grad_sum_one.astype(low)
    grad_merge = cross_rows(flat_context, attended_grad).astype(low)
    grad_merge_bias = jnp.sum(attended_grad.astype(wide), axis=0)
    context_grad = cross_cols(attended_grad, merge_low).astype(low)

    def own_columns(piece):
        return lax.dynamic_update_slice(jnp.zeros((D,), wide), piece, (core * half,))

    def small_grads(heads_bias_grad):
        if heads_bias_grad is None:
            nothing = jnp.zeros((D,), wide)
            query_bias, value_bias = nothing, nothing
        else:
            query_bias = own_columns(heads_bias_grad[:half])
            value_bias = own_columns(heads_bias_grad[2 * half :])
        found = jnp.stack(
            [
                grad_gain_one,
                grad_gain_two,
                query_bias,
                value_bias,
                grad_merge_bias,
                grad_shift_one,
                grad_shrink_bias,
                grad_shift_two,
            ]
        )
        found = jnp.concatenate([found, grad_hidden.reshape(-1, D)], axis=0)
        return jnp.pad(found, ((0, -found.shape[0] % 8), (0, 0)))

    grad_merge = grad_merge.reshape(block + (rows, D))
    grad_expand = grad_expand.reshape(block + (rows, expand_weight.shape[1]))
    grad_shrink = grad_shrink.reshape(block + (hidden_rows, D))
    if kernels:
        *sums, input_parts = finish_all(
            chips // 4,
            heads_here,
            context_grad.reshape(row_count, length, D),
            seg_key,
            seg_query,
            inputs_both,
            heads_low,
            grad_merge,
            grad_expand,
            grad_shrink,
            small_grads(None),
        )
        input_parts = input_parts.reshape(tokens, D)
    else:
        own = jnp.where(core == 0, context_grad[:, :half], context_grad[:, half:])
        other = swap_cores(jnp.where(core == 0, context_grad[:, half:], context_grad[:, :half]))
        grad_here = jnp.stack([own, other]).reshape(2, row_count, length, half)
        heads_grad = attend_back(heads_here, grad_here, seg_key, seg_query)
        heads_grad = heads_grad.reshape(2 * tokens, 3 * half)
        input_parts = cross_cols(heads_grad, heads_low)
        input_parts = input_parts[:tokens] + swap_cores(input_parts[tokens:].astype(low))
        grad_heads = cross_rows(inputs_both, heads_grad).astype(low)
        small_grad = small_grads(jnp.sum(heads_grad.astype(wide), axis=0))
        grad_heads = grad_heads.reshape(block + (rows, 3 * half))
        sums = scatter_plain(grad_heads, grad_merge, grad_expand, grad_shrink, small_grad)
    work_gradient = (grad_sum_one + input_parts).reshape(layer_input.shape)
    heads_sum, merge_sum, expand_sum, shrink_sum, small_sum, squares = sums
    vector_sum = lax.dynamic_slice(small_sum, (0, index * rows), (8, rows)).T
    hidden_sum = lax.dynamic_slice(
        small_sum[8 : 8 + hidden_rows * devices // D].reshape(-1), (index * hidden_rows,), (hidden_rows,)
    )
    states = (
        (heads_weight, heads_first, heads_second, rate_matrix),
        (merge_weight, merge_first, merge_second, rate_matrix),
        (expand_weight, expand_first, expand_second, rate_matrix),
        (shrink_weight, shrink_first, shrink_second, rate_matrix),
        (norm_gains, gains_first, gains_second, rate_vector),
        (branch_bias, branch_first, branch_second, rate_vector),
        (hidden_bias, hidden_first, hidden_second, rate_vector),
    )
    matrix_sums = (heads_sum, merge_sum, expand_sum, shrink_sum)
    vector_sums = (vector_sum[:, 0:2], vector_sum[:, 2:8], hidden_sum)
    if kernels:
        matrices, gradient_norm = update_all(
            squares, small_sum, [(matrix_sums[i], *states[i][:3]) for i in range(4)]
        )
        factor = jnp.minimum(1.0, clip_limit / gradient_norm)
    else:
        gradient_norm = jnp.sqrt(squares + jnp.sum(small_sum * small_sum))
        factor = jnp.minimum(1.0, clip_limit / gradient_norm)
        by_half = heads_sum.reshape(2, rows, 3, half).transpose(1, 2, 0, 3)
        matrices = []
        for i in range(4):
            slope = by_half.reshape(rows, 3 * D) if i == 0 else matrix_sums[i]
            found = adamw(*states[i][:3], slope, factor, rate_matrix)
            matrices.append([*found, found[0].astype(low)])
    vectors_new = [adamw(*states[i][:3], vector_sums[i - 4], factor, rate_vector) for i in range(4, 7)]
    return (
        work_output,
        work_gradient,
        gradient_norm,
        *[value for found in matrices for value in found[:3]],
        *[value for found in vectors_new for value in found],
        *[found[3] for found in matrices],
    )


def solution(mesh):
    matrix, vector = P(("dp", "seq"), None), P(("dp", "seq"))
    tokens = P("dp", "seq", None)
    states = (matrix,) * 18 + (vector,) * 3
    return jax.shard_map(
        functools.partial(per_device, mesh.shape["dp"]),
        mesh=mesh,
        in_specs=(tokens, P("dp", None), tokens) + states,
        out_specs=(tokens, tokens, P()) + states + (matrix,) * 4,
        check_vma=False,
    )
```
